32 devices in a mesh: group: 2 (over core), local: 16 (over z, y, x).
Axes of the slice: x: 2, y: 2, z: 4, core: 2. Of those that a mesh axis runs over, the one named last changes fastest.
Arguments:
- features: bfloat16 [64, 32, 1728], P(('group', 'local')), may hold values from -6 to 6
- neighbours: int32 [64, 27], P(('group', 'local')), may hold values from -1 to 1, as said below
- coarse_dest: int32 [64], P(('group', 'local')), may hold values from -1 to 3, as said below
- weight_first: bfloat16 [32, 864], replicated, may hold values from -0.21875 to 0.21875
- bias_first: float32 [32], replicated, may hold values from -3 to 3
- reduce_weight: bfloat16 [64, 256], replicated, may hold values from -0.375 to 0.375
- reduce_bias: float32 [64], replicated, may hold values from -3 to 3
- weight_coarse: bfloat16 [64, 1728], replicated, may hold values from -0.15625 to 0.15625
- bias_coarse: float32 [64], replicated, may hold values from -3 to 3
- weight_up: bfloat16 [32, 64], replicated, may hold values from -0.75 to 0.75
- bias_up: float32 [32], replicated, may hold values from -3 to 3
- weight_last: bfloat16 [32, 1728], replicated, may hold values from -0.15625 to 0.15625
- bias_last: float32 [32], replicated, may hold values from -3 to 3
Outputs:
- decoded: bfloat16 [64, 32, 1728], P(('group', 'local'))
- balanced_coarse: bfloat16 [128, 64, 216], P(('group', 'local'))
The draws below stay inside these ranges and needn't reach their ends.
Inputs may be any that keep to these rules, and one draw needn't show every extreme that they name: `neighbours`: both slots of every device are live. For a live slot, entry (dx + 1) * 9 + (dy + 1) * 3 + dz + 1 names the live slot of the device with the same group index and local index l + dx that holds the block at offset (dx, dy, dz), or -1 where that block is absent or lies outside the group; entry 13 is the slot itself. The blocks of one device form one layer of blocks along the first dimension, the next local index holding the next layer. `coarse_dest`: -1 exactly for empty slots; else r * 2 + k, naming slot k of the coarse cubes that this device sends to the device of the same local index in group r. No two slots of a device share a value; in every draw some device sends 2 cubes to one group.
All inputs are finite; a program needn't handle non-finite values.
Results may differ from the reference program's by a relative error of at most 0.0049.
Values may be sent and summed in bfloat16 or wider, within the bound.
A program may use at most 64 MiB of HBM per device.

```python
import math
import jax
import jax.numpy as jnp
from jax import lax

C = 32
CC = 64
SIDE = 12
SEND_CAP = 2
CAP = 2
BLOCKS = 64
BAL_SLOTS = 128
N_GROUP = 2
N_LOCAL = 16


def layout(key):
    base_key = jax.random.fold_in(key, 4099)
    key_base, key_jitter, key_place, key_offset = jax.random.split(base_key, 4)
    grid_side = int(math.ceil(math.sqrt(CAP)))
    base_count = jax.random.randint(key_base, (N_GROUP, 1), max(CAP - 1, 2), CAP + 1)
    jitter = jax.random.randint(key_jitter, (N_GROUP, N_LOCAL), -1, 2)
    live_count = jnp.clip(base_count + jitter, 2, CAP)
    live_count = live_count.at[0, 0].set(CAP).at[N_GROUP - 1, N_LOCAL - 1].set(2)
    device_keys = jax.random.split(key_place, N_GROUP * N_LOCAL)
    places = jax.vmap(lambda device_key: jax.random.permutation(device_key, grid_side * grid_side))(device_keys)
    places = places[:, :CAP].reshape(N_GROUP, N_LOCAL, CAP).astype(jnp.int32)
    slot_ids = jnp.arange(CAP, dtype=jnp.int32)
    live_slots = slot_ids[None, None, :] < live_count[:, :, None]
    places = jnp.where(live_slots, places, -1)
    local_ids = jnp.arange(N_LOCAL, dtype=jnp.int32).reshape(1, N_LOCAL, 1)
    entries = []
    for step_x in (-1, 0, 1):
        beside = jnp.roll(places, -step_x, axis=1)
        device_ok = (local_ids + step_x >= 0) & (local_ids + step_x < N_LOCAL)
        for step_y in (-1, 0, 1):
            for step_z in (-1, 0, 1):
                along_y = places // grid_side + step_y
                along_z = places % grid_side + step_z
                inside = (along_y >= 0) & (along_y < grid_side) & (along_z >= 0) & (along_z < grid_side) & live_slots & device_ok
                target = along_y * grid_side + along_z
                matches = beside[:, :, None, :] == target[:, :, :, None]
                located = jnp.any(matches, axis=3) & inside
                chosen = jnp.sum(matches.astype(jnp.int32) * slot_ids, axis=3)
                entries.append(jnp.where(located, chosen, -1))
    neighbours = jnp.stack(entries, axis=3).reshape(BLOCKS, 27)
    offsets = jax.random.randint(key_offset, (N_GROUP, N_LOCAL, 1), 0, N_GROUP)
    group_ids = jnp.arange(N_GROUP, dtype=jnp.int32).reshape(N_GROUP, 1, 1)
    targets = (group_ids + offsets + slot_ids // 2) % N_GROUP * SEND_CAP + slot_ids % 2
    targets = jnp.where(live_slots, targets, -1).reshape(BLOCKS)
    return (neighbours.astype(jnp.int32), targets.astype(jnp.int32))


def draw_neighbours(key, part):
    return layout(key)[0]


def draw_coarse_dest(key, part):
    return layout(key)[1]


def block_levels(key, shape, shards, least, top_value):
    gain, own = 1.0, jax.random.fold_in(key, 6)
    for dim, parts in shards:
        draws = jnp.exp(jax.random.uniform(jax.random.fold_in(own, dim), (parts,), jnp.float32, least / len(shards), top_value / len(shards)))
        gain = gain * jnp.repeat(draws, shape[dim] // parts).reshape([-1 if axis == dim else 1 for axis in range(len(shape))])
    return gain


def centred(rng, dims, spread, most, cuts=(), kind=jnp.bfloat16):
    factor_of = block_levels(rng, dims, cuts, -0.22, 0.18) if cuts else 1.0
    array = jax.random.normal(rng, dims, jnp.float32) * spread * factor_of
    return jnp.minimum(jnp.maximum(array, -most), most).astype(kind)


def setup_inputs(seed: int = 0) -> dict:
    key_of = jax.random.split(jax.random.key(seed), 14)
    return {
        "features": centred(key_of[0], (BLOCKS, C, SIDE**3), 1.0, 6.0, ((0, 32),)),
        "neighbours": draw_neighbours(jax.random.fold_in(key_of[13], 71), 0),
        "coarse_dest": draw_coarse_dest(jax.random.fold_in(key_of[13], 71), 0),
        "weight_first": centred(key_of[3], (C, 27 * C), (27 * C) ** -0.5, 0.21875),
        "bias_first": centred(key_of[4], (C,), 0.5, 3.0, (), jnp.float32),
        "reduce_weight": centred(key_of[5], (CC, 8 * C), (8 * C) ** -0.5, 0.375),
        "reduce_bias": centred(key_of[6], (CC,), 0.5, 3.0, (), jnp.float32),
        "weight_coarse": centred(key_of[7], (CC, 27 * CC), (27 * CC) ** -0.5, 0.15625),
        "bias_coarse": centred(key_of[8], (CC,), 0.5, 3.0, (), jnp.float32),
        "weight_up": centred(key_of[9], (C, CC), CC ** -0.5, 0.75),
        "bias_up": centred(key_of[10], (C,), 0.5, 3.0, (), jnp.float32),
        "weight_last": centred(key_of[11], (C, 54 * C), (54 * C) ** -0.5, 0.15625),
        "bias_last": centred(key_of[12], (C,), 0.5, 3.0, (), jnp.float32),
    }


def assemble(extended, slot_table):
    count = extended.shape[0]
    cube_side = extended.shape[3]
    slot_index = jnp.maximum(slot_table, 0)
    present = slot_table >= 0
    across = {-1: (0, 1), 0: (1, cube_side + 1), 1: (cube_side + 1, cube_side + 2)}
    within = {-1: (cube_side - 1, cube_side), 0: (0, cube_side), 1: (0, 1)}
    slabs = []
    for step_x in (-1, 0, 1):
        strips = []
        for step_y in (-1, 0, 1):
            pieces = []
            for step_z in (-1, 0, 1):
                direction = (step_x + 1) * 9 + (step_y + 1) * 3 + step_z + 1
                window = extended[:, :, slice(*across[step_x]), slice(*within[step_y]), slice(*within[step_z])]
                window = jnp.take(window, slot_index[:, direction], axis=0)
                keep_here = present[:, direction].reshape(count, 1, 1, 1, 1)
                pieces.append(jnp.where(keep_here, window, jnp.zeros((), window.dtype)))
            strips.append(jnp.concatenate(pieces, axis=4))
        slabs.append(jnp.concatenate(strips, axis=3))
    return jnp.concatenate(slabs, axis=2)


def conv_block(cube, weight):
    channels = cube.shape[0]
    cube_side = cube.shape[1] - 2
    outputs = weight.shape[0]
    kernel = weight.reshape(outputs, 3, 3, 3, channels).transpose(0, 4, 1, 2, 3)
    result = lax.conv_general_dilated(cube[None], kernel, (1, 1, 1), "VALID", dimension_numbers=("NCDHW", "OIDHW", "NCDHW"), preferred_element_type=jnp.float32)
    return result.reshape(outputs, cube_side ** 3)


def fine_layer(extended, slot_table, occupied_mask, weight, bias_vec):
    count, channels, padded, plane = extended.shape
    cube_side = padded - 2
    cubes = assemble(extended.reshape(count, channels, padded, cube_side, cube_side), slot_table)
    preact = lax.map(lambda cube: conv_block(cube, weight), cubes)
    return (occupied_mask[:, None, None] * jax.nn.silu(preact + bias_vec[None, :, None])).astype(jnp.bfloat16)


def stride_reduce(leading_output, reduce_weight, reduce_bias, occupied_mask):
    count, channels, cells_all = leading_output.shape
    coarse_side = SIDE // 2
    grouped = leading_output.reshape(count, channels, coarse_side, 2, coarse_side, 2, coarse_side, 2)
    grouped = grouped.transpose(0, 3, 5, 7, 1, 2, 4, 6).reshape(count, 8 * channels, coarse_side ** 3)
    preact = lax.map(lambda stacked: jnp.dot(reduce_weight, stacked, preferred_element_type=jnp.float32), grouped)
    return (occupied_mask[:, None, None] * jax.nn.silu(preact + reduce_bias[None, :, None])).astype(jnp.bfloat16)


def coarse_tiles(extended, slot_table):
    count, channels, padded, plane = extended.shape
    coarse_side = padded - 2
    cubes = assemble(extended.reshape(count, channels, padded, coarse_side, coarse_side), slot_table)
    cube_cells = padded ** 3
    tile_width = (cube_cells + 127) // 128 * 128
    flattened = cubes.reshape(count, channels, cube_cells)
    return jnp.pad(flattened, ((0, 0), (0, 0), (0, tile_width - cube_cells)))


def coarse_conv(tile_rows, keep_mask, weight_coarse, bias_coarse):
    channels = tile_rows.shape[1]
    padded = SIDE // 2 + 2

    def convolve(tile_row):
        cube = tile_row[:, :padded ** 3].reshape(channels, padded, padded, padded)
        return conv_block(cube, weight_coarse)

    preact = lax.map(convolve, tile_rows)
    return (keep_mask[:, None, None] * jax.nn.silu(preact + bias_coarse[None, :, None])).astype(jnp.bfloat16)


def upsample(coarse_out, weight_up, bias_up, occupied_mask):
    count = coarse_out.shape[0]
    coarse_side = SIDE // 2
    projected = lax.map(lambda stacked: jnp.dot(weight_up, stacked, preferred_element_type=jnp.float32), coarse_out)
    projected = projected + bias_up[None, :, None]
    channels = projected.shape[1]
    cubes = projected.reshape(count, channels, coarse_side, 1, coarse_side, 1, coarse_side, 1)
    cubes = jnp.broadcast_to(cubes, (count, channels, coarse_side, 2, coarse_side, 2, coarse_side, 2))
    return (occupied_mask[:, None, None] * cubes.reshape(count, channels, SIDE ** 3)).astype(jnp.bfloat16)


def faces_ref(values, cube_side):
    devices, count, channels, cells_all = values.shape
    device_grid = values.reshape(N_GROUP, N_LOCAL, count, channels, cube_side, cube_side * cube_side)
    zero_plane = jnp.zeros_like(device_grid[:, :1, :, :, :1, :])
    lower_plane = jnp.concatenate([zero_plane, device_grid[:, :-1, :, :, -1:, :]], axis=1)
    upper_plane = jnp.concatenate([device_grid[:, 1:, :, :, :1, :], zero_plane], axis=1)
    extended = jnp.concatenate([lower_plane, device_grid, upper_plane], axis=4)
    return extended.reshape(devices, count, channels, cube_side + 2, cube_side * cube_side)


def reference(features, neighbours, coarse_dest, weight_first, bias_first, reduce_weight, reduce_bias, weight_coarse, bias_coarse, weight_up, bias_up, weight_last, bias_last):
    devices = N_GROUP * N_LOCAL
    slot_table = neighbours.reshape(devices, CAP, 27).astype(jnp.int32)
    occupied_mask = (slot_table[:, :, 13] >= 0).astype(jnp.float32)
    targets = coarse_dest.reshape(devices, CAP).astype(jnp.int32)
    valid_mask = occupied_mask * (targets >= 0).astype(jnp.float32)
    fine_in = features.reshape(devices, CAP, C, SIDE ** 3)
    leading_output = lax.map(lambda input_grids: fine_layer(input_grids[0], input_grids[1], input_grids[2], weight_first, bias_first), (faces_ref(fine_in, SIDE), slot_table, occupied_mask))
    coarse_input = lax.map(lambda input_grids: stride_reduce(input_grids[0], reduce_weight, reduce_bias, input_grids[1]), (leading_output, occupied_mask))
    tile_rows = lax.map(lambda input_grids: coarse_tiles(input_grids[0], input_grids[1]), (faces_ref(coarse_input, SIDE // 2), slot_table))
    coarse_out = lax.map(lambda input_grids: coarse_conv(input_grids[0], input_grids[1], weight_coarse, bias_coarse), (tile_rows, valid_mask))
    group_ids = jnp.arange(N_GROUP, dtype=jnp.int32).reshape(N_GROUP, 1, 1)
    local_ids = jnp.arange(N_LOCAL, dtype=jnp.int32).reshape(1, N_LOCAL, 1)
    grid_targets = targets.reshape(N_GROUP, N_LOCAL, CAP)
    position = ((grid_targets // SEND_CAP * N_LOCAL + local_ids) * N_GROUP + group_ids) * SEND_CAP + grid_targets % SEND_CAP
    position = jnp.where(valid_mask.reshape(N_GROUP, N_LOCAL, CAP) > 0, position, BAL_SLOTS).reshape(-1).astype(jnp.int32)
    coarse_cells = (SIDE // 2) ** 3
    balanced_coarse = jnp.zeros((BAL_SLOTS, CC, coarse_cells), coarse_out.dtype)
    balanced_coarse = balanced_coarse.at[position].set(coarse_out.reshape(-1, CC, coarse_cells), mode="drop")
    upward = lax.map(lambda input_grids: upsample(input_grids[0], weight_up, bias_up, input_grids[1]), (coarse_out, occupied_mask))
    joined = jnp.concatenate([leading_output, upward], axis=2)
    decoded = lax.map(lambda input_grids: fine_layer(input_grids[0], input_grids[1], input_grids[2], weight_last, bias_last), (faces_ref(joined, SIDE), slot_table, occupied_mask))
    return decoded.reshape(BLOCKS, C, SIDE ** 3), balanced_coarse
```

```python
import functools

import jax
import jax.numpy as jnp
from jax import lax
from jax.experimental import pallas as pl
from jax.experimental.pallas import tpu as pltpu
from jax.sharding import PartitionSpec as P

SEND_CAP = 2
MESH = pl.DeviceIdType.MESH
F32 = jnp.float32
BF16 = jnp.bfloat16
I32 = jnp.int32


def iota(shape, dim):
    return lax.broadcasted_iota(I32, shape, dim)


def onehot(mask):
    return jnp.where(mask, 1.0, 0.0).astype(BF16)


def column(row):
    n = row.shape[1]
    wide = jnp.broadcast_to(row, (n, n))
    return jnp.sum(jnp.where(iota((n, n), 0) == iota((n, n), 1), wide, 0.0), axis=1, keepdims=True)


def silu(u):
    return u / (1.0 + jnp.exp(-u))


def shifted(v, s):
    if s == 0:
        return v
    return jnp.concatenate([v[:, s:], v[:, :s]], axis=1)


def dot(a, b):
    return jnp.dot(a, b, preferred_element_type=F32)


def kernel(
    sizes,
    nb,
    dest,
    x_ref,
    w1_ref,
    b1_ref,
    wr_ref,
    br_ref,
    wc_ref,
    bc_ref,
    wu_ref,
    bu_ref,
    w2_ref,
    b2_ref,
    out_ref,
    bal_ref,
    sx,
    rx,
    sc,
    rc,
    sf,
    rf,
    su,
    ru,
    sb,
    rb,
    t1,
    t2,
    tred,
    tc,
    tup,
    tout,
    tbal,
    w1,
    wc,
    w2f,
    w2u,
    lhs,
    pad,
    y1,
    y2,
    fst,
    cin,
    up,
    red,
    sel,
    fm,
    cm,
    send_sem,
    recv_sem,
    bal_send,
    bal_recv,
):
    side, count, ch, cc, n_local, n_group = sizes
    half = side // 2
    face = side * side
    planes = side + 2
    me = lax.axis_index("local")
    grp = lax.axis_index("group")
    right, left = lax.rem(me + 1, n_local), lax.rem(me + n_local - 1, n_local)
    ends = (left, right)
    has_left, has_right = me > 0, me < n_local - 1
    sends, receives = (has_left, has_right), (has_right, has_left)

    def exchange(e, src, dst):
        copies = []
        for d in (0, 1):
            copies.append(
                pltpu.make_async_remote_copy(
                    src_ref=src.at[d],
                    dst_ref=dst.at[d],
                    send_sem=send_sem.at[e, d],
                    recv_sem=recv_sem.at[e, d],
                    device_id={"local": ends[d]},
                    device_id_type=MESH,
                )
            )
        return copies

    def start(copies):
        for d in (0, 1):
            pl.when(sends[d])(copies[d].start)

    def receive(copies):
        for d in (0, 1):
            pl.when(receives[d])(copies[d].wait_recv)

    def finish(copies):
        for d in (0, 1):
            pl.when(sends[d])(copies[d].wait_send)

    for d in (0, 1):

        @pl.when(jnp.logical_not(receives[d]))
        def _():
            for buf in (rx, rc, rf, ru):
                buf[d] = jnp.zeros(buf.shape[1:], BF16)

    barrier = pltpu.get_barrier_semaphore()
    for d in (0, 1):

        @pl.when(sends[d])
        def _():
            pl.semaphore_signal(barrier, inc=1, device_id={"local": ends[d]}, device_id_type=MESH)

    for d in range(1, n_group):
        pl.semaphore_signal(
            barrier, inc=1, device_id={"group": lax.rem(grp + d, n_group)}, device_id_type=MESH
        )
    for t in range(count):
        sx[0, t] = x_ref[t, :, 0:face]
        sx[1, t] = x_ref[t, :, (side - 1) * face : side * face]
    n = iota((1, 256), 1)
    ny, nz = n >> 4, n & 15
    py = jnp.where(ny == 0, side - 1, jnp.where(ny == side + 1, 0, ny - 1))
    pz = jnp.where(nz == 0, side - 1, jnp.where(nz == side + 1, 0, nz - 1))
    inside = (ny < planes) & (nz < planes)
    t1[...] = onehot(iota((face, 256), 0) == jnp.where(inside, py * side + pz, -1))
    t2[...] = onehot(iota((256, 256), 0) == jnp.where(inside, py * 16 + pz, -1))
    n2 = iota((1, 512), 1)
    uy, uz = (n2 >> 4) & 15, n2 & 15
    qy = jnp.where(uy == 0, side - 1, jnp.where(uy == side + 1, 0, uy - 1))
    qz = jnp.where(uz == 0, side - 1, jnp.where(uz == side + 1, 0, uz - 1))
    target = (n2 >> 8) * 64 + (qy >> 1) * 8 + (qz >> 1)
    target = jnp.where((uy < planes) & (uz < planes), target, -1)
    tup[...] = onehot(iota((128, 512), 0) == target)
    ry, rz = (n2 >> 3) & 7, n2 & 7
    target = ((n2 >> 6) & 1) * 256 + (2 * ry + ((n2 >> 8) & 1)) * 16 + 2 * rz + ((n2 >> 7) & 1)
    target = jnp.where((ry < half) & (rz < half), target, -1)
    tred[...] = onehot(iota((512, 512), 0) == target)
    n1 = iota((1, 128), 1)
    cy, cz = (n1 >> 3) & 7, n1 & 7
    sy = jnp.where(cy == 0, half - 1, jnp.where(cy == half + 1, 0, cy - 1))
    sz = jnp.where(cz == 0, half - 1, jnp.where(cz == half + 1, 0, cz - 1))
    target = (n1 >> 6) * 64 + sy * 8 + sz
    tc[...] = onehot(iota((128, 128), 0) == target)
    k = iota((256, 1), 0)
    ky, kz = k >> 4, k & 15
    target = jnp.where((ky < side) & (kz < side), ky * side + kz, -1)
    tout[...] = onehot(iota((256, face), 1) == target)
    k = iota((64 * half, 1), 0)
    kx, ky, kz = k >> 6, (k >> 3) & 7, k & 7
    target = jnp.where((ky < half) & (kz < half), (kx * half + ky) * half + kz, -1)
    tbal[...] = onehot(iota((64 * half, half**3), 1) == target)

    for p in range(3):
        w1[p * ch : (p + 1) * ch] = w1_ref[:, p * 9 * ch : (p + 1) * 9 * ch]
        wc[p * cc : (p + 1) * cc] = wc_ref[:, p * 9 * cc : (p + 1) * 9 * cc]
        for part, dst in ((0, w2f), (1, w2u)):
            dst[p * ch : (p + 1) * ch] = jnp.concatenate(
                [
                    w2_ref[:, ((9 * p + k) * 2 + part) * ch : ((9 * p + k) * 2 + part + 1) * ch]
                    for k in range(9)
                ],
                axis=1,
            )
    b1, br, bc = column(b1_ref[...]), column(br_ref[...]), column(bc_ref[...])
    bu, b2 = column(bu_ref[...]), column(b2_ref[...])

    live = [jnp.where(nb[b, 13] >= 0, 1.0, 0.0) for b in range(count)]
    valid = [jnp.where(dest[b] >= 0, live[b], 0.0) for b in range(count)]

    def slot_row(b, step, dy, dz):
        row = jnp.zeros_like(dy)
        for iy in (-1, 0, 1):
            for iz in (-1, 0, 1):
                entry = nb[b, (step + 1) * 9 + (iy + 1) * 3 + iz + 1]
                row = jnp.where((dy == iy) & (dz == iz), entry, row)
        return row

    def as_masks(row):
        return [jnp.where(row == t, 1.0, 0.0) for t in range(count)]

    def offset(v, top):
        return jnp.where(v == 0, -1, jnp.where(v == top, 1, 0))

    fy, fz = offset(ny, side + 1), offset(nz, side + 1)
    gy, gz = offset(cy, half + 1), offset(cz, half + 1)
    fine = [[as_masks(slot_row(b, s, fy, fz)) for s in (-1, 0, 1)] for b in range(count)]
    mid = [as_masks(slot_row(b, 0, gy, gz)) for b in range(count)]
    rim = [
        as_masks(jnp.where(n1 < 64, slot_row(b, 1, gy, gz), slot_row(b, -1, gy, gz)))
        for b in range(count)
    ]

    for b in range(count):
        for t in range(count):
            for s in range(3):
                fm[b, s, t] = jnp.broadcast_to(fine[b][s][t], (ch, 256)).astype(BF16)
            cm[b, 0, t] = jnp.broadcast_to(mid[b][t], (cc, 128)).astype(BF16)
            cm[b, 1, t] = jnp.broadcast_to(rim[b][t], (cc, 128)).astype(BF16)

    def blend(parts, masks):
        total = parts[0] * masks[0]
        for t in range(1, count):
            total = total + parts[t] * masks[t]
        return total

    def taps(v, stride):
        return jnp.concatenate([shifted(v, q * stride + r) for q in range(3) for r in range(3)], axis=0)

    def convolve(dst, plane, weight, parts, step):
        both = [taps(blend(parts, fm.at[b, step]), 16) for b in range(count)]
        y = dot(weight[...], jnp.concatenate(both, axis=1))
        for b in range(count):
            dst[b, plane] = y[:, b * 256 : (b + 1) * 256]

    for t in range(count):
        for x in range(side):
            lhs[(x * count + t) * ch : (x * count + t + 1) * ch, 0:face] = x_ref[
                t, :, x * face : (x + 1) * face
            ]
    beside = jnp.where(has_left, 1, 0) + jnp.where(has_right, 1, 0)
    pl.semaphore_wait(barrier, beside + n_group - 1)
    ex = exchange(0, sx, rx)
    start(ex)
    sel[...] = dot(lhs[:, 0:face], t1[...]).astype(BF16)
    for x in range(side):
        parts = [sel[(x * count + t) * ch : (x * count + t + 1) * ch] for t in range(count)]
        convolve(y1, x + 1, w1, parts, 1)
    receive(ex)
    for d, plane, step in ((1, 0, 0), (0, side + 1, 2)):
        a = dot(jnp.concatenate([rx[d, t] for t in range(count)], axis=0), t1[...]).astype(BF16)
        parts = [a[t * ch : (t + 1) * ch] for t in range(count)]
        convolve(y1, plane, w1, parts, step)
    for b in range(count):
        for x in range(side):
            u = y1[b, x, 0:ch] + y1[b, x + 1, ch : 2 * ch] + y1[b, x + 2, 2 * ch : 3 * ch] + b1
            fst[b, x] = (live[b] * silu(u)).astype(BF16)

    for b in range(count):
        sf[0, b] = fst[b, 0]
        sf[1, b] = fst[b, side - 1]
    pairs = half // 2
    for b in range(count):
        for j in range(pairs):
            for p in (0, 1):
                r0 = ((b * pairs + j) * 2 + p) * ch
                lhs[r0 : r0 + ch, 0:256] = fst[b, 4 * j + p]
                lhs[r0 : r0 + ch, 256:512] = fst[b, 4 * j + 2 + p]
    red[...] = dot(lhs[0 : count * pairs * 2 * ch, :], tred[...]).astype(BF16)
    for b in range(count):
        for j in range(pairs):
            r0 = (b * pairs + j) * 2 * ch
            rows = jnp.concatenate(
                [
                    red[r0 + p * ch : r0 + (p + 1) * ch, k * 128 : (k + 1) * 128]
                    for p in (0, 1)
                    for k in range(4)
                ],
                axis=0,
            )
            v = (live[b] * silu(dot(wr_ref[...], rows) + br)).astype(BF16)
            cin[b, j] = v
            if j == 0:
                sc[0, b] = v
            if j == pairs - 1:
                sc[1, b] = v
    ec, ef = exchange(1, sc, rc), exchange(2, sf, rf)
    start(ec)
    start(ef)

    for t in range(count):
        for x in range(side):
            lhs[(x * count + t) * ch : (x * count + t + 1) * ch, 0:256] = fst[t, x]
    sel[...] = dot(lhs[:, 0:256], t2[...]).astype(BF16)
    for x in range(side):
        parts = [sel[(x * count + t) * ch : (x * count + t + 1) * ch] for t in range(count)]
        convolve(y1, x + 1, w2f, parts, 1)

    for j in range(pairs):
        a = dot(jnp.concatenate([cin[t, j] for t in range(count)], axis=0), tc[...]).astype(BF16)
        parts = [a[t * cc : (t + 1) * cc] for t in range(count)]
        for b in range(count):
            pad[b, j] = blend(parts, cm.at[b, 0])
    receive(ec)
    edge = [jnp.where(n1 < 64, rc[0, t].astype(F32), rc[1, t].astype(F32)).astype(BF16) for t in range(count)]
    a = dot(jnp.concatenate(edge, axis=0), tc[...]).astype(BF16)
    parts = [a[t * cc : (t + 1) * cc] for t in range(count)]
    for b in range(count):
        pad[b, pairs] = blend(parts, cm.at[b, 1])
    coarse = []
    for b in range(count):
        y = dot(wc[...], jnp.concatenate([taps(pad[b, j], 8) for j in range(pairs + 1)], axis=1))
        width = y.shape[1]
        u = pltpu.roll(y[0:cc], 64, 1) + y[cc : 2 * cc] + pltpu.roll(y[2 * cc :], width - 64, 1) + bc
        co = (valid[b] * silu(u[:, 0 : 64 * half])).astype(BF16)
        coarse.append(co)
        v = (live[b] * (dot(wu_ref[...], co) + bu)).astype(BF16)
        for j in range(pairs):
            up[b, j] = v[:, j * 128 : (j + 1) * 128]
        su[0, b] = v[:, 0:128]
        su[1, b] = v[:, (pairs - 1) * 128 : pairs * 128]
    eu = exchange(3, su, ru)
    start(eu)

    dense = [dot(co, tbal[...]) for co in coarse]

    def outgoing(r, k):
        total = jnp.zeros_like(dense[0])
        for b in range(count):
            total = total + dense[b] * jnp.where(dest[b] == r * SEND_CAP + k, valid[b], 0.0)
        return total.astype(BF16)

    sent = []
    for d in range(1, n_group):
        other = lax.rem(grp + d, n_group)
        for k in range(SEND_CAP):
            sb[d - 1, k] = outgoing(other, k)
        c = pltpu.make_async_remote_copy(
            src_ref=sb.at[d - 1],
            dst_ref=rb.at[d - 1],
            send_sem=bal_send.at[d - 1],
            recv_sem=bal_recv.at[d - 1],
            device_id={"group": other},
            device_id_type=MESH,
        )
        c.start()
        sent.append(c)
    for k in range(SEND_CAP):
        bal_ref[grp * SEND_CAP + k] = outgoing(grp, k)

    receive(ef)
    for d, plane, step in ((1, 0, 0), (0, side + 1, 2)):
        a = dot(jnp.concatenate([rf[d, t] for t in range(count)], axis=0), t2[...]).astype(BF16)
        parts = [a[t * ch : (t + 1) * ch] for t in range(count)]
        convolve(y1, plane, w2f, parts, step)

    for j in range(pairs):
        a = dot(jnp.concatenate([up[t, j] for t in range(count)], axis=0), tup[...]).astype(BF16)
        for h in (0, 1):
            parts = [a[t * ch : (t + 1) * ch, h * 256 : (h + 1) * 256] for t in range(count)]
            convolve(y2, 1 + 2 * j + h, w2u, parts, 1)
    receive(eu)
    for d, plane, step, h in ((1, 0, 0, 1), (0, half + 1, 2, 0)):
        a = dot(jnp.concatenate([ru[d, t] for t in range(count)], axis=0), tup[:, h * 256 : (h + 1) * 256]).astype(BF16)
        parts = [a[t * ch : (t + 1) * ch] for t in range(count)]
        convolve(y2, plane, w2u, parts, step)

    for b in range(count):
        done = []
        for x in range(side):
            u = b2
            for p in range(3):
                u = u + y1[b, x + p, p * ch : (p + 1) * ch]
                u = u + y2[b, (x + p + 1) // 2, p * ch : (p + 1) * ch]
            lhs[x * ch : (x + 1) * ch, 0:256] = (live[b] * silu(u)).astype(BF16)
        flat = dot(lhs[0 : side * ch, 0:256], tout[...])
        for x in range(side):
            out_ref[b, :, x * face : (x + 1) * face] = flat[x * ch : (x + 1) * ch].astype(BF16)

    for copies in (ex, ec, ef, eu):
        finish(copies)
    for d, c in enumerate(sent):
        c.wait()
        source = lax.rem(grp + n_group - (d + 1), n_group)
        for k in range(SEND_CAP):
            bal_ref[source * SEND_CAP + k] = rb[d, k]


def local(n_local, n_group, features, neighbours, coarse_dest, *weights):
    count, ch, cells = features.shape
    side = round(cells ** (1 / 3))
    cc = weights[2].shape[0]
    half, face = side // 2, side * side
    pairs = half // 2
    if side + 2 > 16 or half + 2 > 8 or half % 2 or side**3 != cells:
        raise ValueError("side")
    vmem = lambda *shape: pltpu.VMEM(shape, BF16)
    weights = [w.reshape(1, -1) if w.ndim == 1 else w for w in weights]
    whole = pl.BlockSpec(memory_space=pltpu.VMEM)
    smem = pl.BlockSpec(memory_space=pltpu.SMEM)
    return pl.pallas_call(
        functools.partial(kernel, (side, count, ch, cc, n_local, n_group)),
        out_shape=(
            pltpu.VMEM(features.shape, BF16),
            pltpu.VMEM((n_group * SEND_CAP, cc, half**3), BF16),
        ),
        in_specs=[smem, smem] + [whole] * (1 + len(weights)),
        out_specs=(whole, whole),
        scratch_shapes=[
            vmem(2, count, ch, face),
            vmem(2, count, ch, face),
            vmem(2, count, cc, 128),
            vmem(2, count, cc, 128),
            vmem(2, count, ch, 256),
            vmem(2, count, ch, 256),
            vmem(2, count, ch, 128),
            vmem(2, count, ch, 128),
            vmem(n_group - 1, SEND_CAP, cc, half**3),
            vmem(n_group - 1, SEND_CAP, cc, half**3),
            vmem(face, 256),
            vmem(256, 256),
            vmem(512, 512),
            vmem(128, 128),
            vmem(128, 512),
            vmem(256, face),
            vmem(64 * half, half**3),
            vmem(3 * ch, 9 * ch),
            vmem(3 * cc, 9 * cc),
            vmem(3 * ch, 9 * ch),
            vmem(3 * ch, 9 * ch),
            vmem(side * count * ch, 512),
            vmem(count, pairs + 1, cc, 128),
            pltpu.VMEM((count, side + 2, 3 * ch, 256), F32),
            pltpu.VMEM((count, half + 2, 3 * ch, 256), F32),
            vmem(count, side, ch, 256),
            vmem(count, pairs, cc, 128),
            vmem(count, pairs, ch, 128),
            vmem(count * pairs * 2 * ch, 512),
            vmem(side * count * ch, 256),
            vmem(count, 3, count, ch, 256),
            vmem(count, 2, count, cc, 128),
            pltpu.SemaphoreType.DMA((4, 2)),
            pltpu.SemaphoreType.DMA((4, 2)),
            pltpu.SemaphoreType.DMA((n_group - 1,)),
            pltpu.SemaphoreType.DMA((n_group - 1,)),
        ],
        compiler_params=pltpu.CompilerParams(collective_id=0, has_side_effects=True),
    )(neighbours, coarse_dest, features, *weights)


def solution(mesh):
    slots = P(("group", "local"), None, None)
    return jax.shard_map(
        functools.partial(local, mesh.shape["local"], mesh.shape["group"]),
        mesh=mesh,
        in_specs=(slots, P(("group", "local"), None), P(("group", "local"))) + (P(),) * 10,
        out_specs=(slots, slots),
        check_vma=False,
    )
```

```python
import functools

import jax
import jax.numpy as jnp
from jax import lax
from jax.experimental import pallas as pl
from jax.experimental.pallas import tpu as pltpu
from jax.sharding import PartitionSpec as P

SEND_CAP = 2
DEPTH = 5
MESH = pl.DeviceIdType.MESH
F32 = jnp.float32
BF16 = jnp.bfloat16
I32 = jnp.int32


def iota(shape, dim):
    return lax.broadcasted_iota(I32, shape, dim)


def onehot(mask):
    return jnp.where(mask, 1.0, 0.0).astype(BF16)


def column(row):
    n = row.shape[1]
    wide = jnp.broadcast_to(row, (n, n))
    return jnp.sum(jnp.where(iota((n, n), 0) == iota((n, n), 1), wide, 0.0), axis=1, keepdims=True)


def silu(u):
    return u / (1.0 + jnp.exp(-u))


def shifted(v, s):
    if s == 0:
        return v
    return jnp.concatenate([v[:, s:], v[:, :s]], axis=1)


def dot(a, b):
    return jnp.dot(a, b, preferred_element_type=F32)


def taps(v, stride):
    return jnp.concatenate([shifted(v, q * stride + r) for q in range(3) for r in range(3)], axis=0)


def offset(v, top):
    return jnp.where(v == 0, -1, jnp.where(v == top, 1, 0))


def kernel(
    sizes,
    nb_hbm,
    dest_hbm,
    x_hbm,
    w1_hbm,
    b1_hbm,
    wr_hbm,
    br_hbm,
    wc_hbm,
    bc_hbm,
    wu_hbm,
    bu_hbm,
    w2_hbm,
    b2_hbm,
    out_ref,
    bal_ref,
    nb,
    dest,
    nb_ref,
    x_ref,
    w1_ref,
    b1_ref,
    wr_ref,
    br_ref,
    wc_ref,
    bc_ref,
    wu_ref,
    bu_ref,
    w2_ref,
    b2_ref,
    sx,
    rx,
    sm,
    rm,
    sb,
    rb,
    t1,
    t2,
    tred,
    tc,
    tup,
    tout,
    tbal,
    w1,
    wc,
    w2f,
    w2u,
    lhs1,
    lhse,
    lhsr,
    lhso,
    y1,
    ye,
    yf,
    y2,
    fst,
    fe,
    cin,
    sel,
    sele,
    selr,
    fm,
    fe_m,
    cm,
    ce_m,
    load_sem,
    send_sem,
    recv_sem,
    bal_send,
    bal_recv,
):
    side, count, ch, cc, n_local, n_group = sizes
    half = side // 2
    face = side * side
    planes = side + 2
    pairs = half // 2
    me = lax.axis_index("local")
    grp = lax.axis_index("group")
    right, left = lax.rem(me + 1, n_local), lax.rem(me + n_local - 1, n_local)
    ends = (left, right)
    has_left, has_right = me > 0, me < n_local - 1
    sends, receives = (has_left, has_right), (has_right, has_left)

    barrier = pltpu.get_barrier_semaphore()
    for d in (0, 1):

        @pl.when(sends[d])
        def _():
            pl.semaphore_signal(barrier, inc=1, device_id={"local": ends[d]}, device_id_type=MESH)

    for d in range(1, n_group):
        pl.semaphore_signal(
            barrier, inc=1, device_id={"group": lax.rem(grp + d, n_group)}, device_id_type=MESH
        )

    loads = {}
    pieces = (
        ("nbv", nb_hbm, nb_ref),
        ("x", x_hbm, x_ref),
        ("nb", nb_hbm, nb),
        ("dest", dest_hbm, dest),
        ("w1", w1_hbm, w1_ref),
        ("b1", b1_hbm, b1_ref),
        ("w2", w2_hbm, w2_ref),
        ("wr", wr_hbm, wr_ref),
        ("br", br_hbm, br_ref),
        ("wc", wc_hbm, wc_ref),
        ("bc", bc_hbm, bc_ref),
        ("wu", wu_hbm, wu_ref),
        ("bu", bu_hbm, bu_ref),
        ("b2", b2_hbm, b2_ref),
    )
    for i, (name, src, dst) in enumerate(pieces):
        loads[name] = pltpu.make_async_copy(src, dst, load_sem.at[i])
        loads[name].start()

    for d in (0, 1):

        @pl.when(jnp.logical_not(receives[d]))
        def _():
            rx[d] = jnp.zeros(rx.shape[1:], BF16)
            rm[d] = jnp.zeros(rm.shape[1:], BF16)

    n = iota((1, 256), 1)
    ny, nz = n >> 4, n & 15
    n1 = iota((1, 128), 1)
    cy, cz = (n1 >> 3) & 7, n1 & 7
    fy, fz = offset(ny, side + 1), offset(nz, side + 1)
    gy, gz = offset(cy, half + 1), offset(cz, half + 1)

    py = jnp.where(ny == 0, side - 1, jnp.where(ny == side + 1, 0, ny - 1))
    pz = jnp.where(nz == 0, side - 1, jnp.where(nz == side + 1, 0, nz - 1))
    inside = (ny < planes) & (nz < planes)
    t1[...] = onehot(iota((face, 256), 0) == jnp.where(inside, py * side + pz, -1))

    direction = jnp.concatenate([(fy + 1) * 3 + fz + 1, (gy + 1) * 3 + gz + 1], axis=1)
    table = onehot(lax.rem(iota((27, 384), 0), 9) == direction)
    rows = sm.shape[0]
    first_live = 3 * count * count
    first_valid = first_live + count
    loads["nbv"].wait()
    row = iota((rows, 27), 0)
    entries = jnp.zeros((rows, 27), I32)
    for b in range(count):
        entries = jnp.where(lax.rem(row, count) == b, nb_ref[b : b + 1, :], entries)
    slot = lax.rem(lax.div(row, count), count)
    step_of = lax.div(row, count * count)
    chosen = onehot((entries == slot) & (lax.div(iota((rows, 27), 1), 9) == step_of) & (row < first_live))
    table_rows = dot(chosen, table)
    loads["nb"].wait()
    loads["dest"].wait()
    live = [jnp.where(nb[b, 13] >= 0, 1.0, 0.0) for b in range(count)]
    valid = [jnp.where(dest[b] >= 0, live[b], 0.0) for b in range(count)]
    wide_row = iota((rows, 384), 0)
    for b in range(count):
        table_rows = jnp.where(wide_row == first_live + b, live[b], table_rows)
        table_rows = jnp.where(wide_row == first_valid + b, valid[b], table_rows)
    sm[...] = table_rows.astype(BF16)

    loads["x"].wait()
    span = DEPTH * face
    for t in range(count):
        sx[0, t, :, 0:span] = x_ref[t, :, 0:span]
        sx[1, t, :, 0:span] = x_ref[t, :, side * face - span : side * face]
        tail = sx.shape[3] - span
        for d in (0, 1):
            sx[d, t, :, span:] = jnp.zeros((ch, tail), BF16)

    beside = jnp.where(has_left, 1, 0) + jnp.where(has_right, 1, 0)
    pl.semaphore_wait(barrier, beside + n_group - 1)

    def remote(e, d, src, dst):
        return pltpu.make_async_remote_copy(
            src_ref=src,
            dst_ref=dst,
            send_sem=send_sem.at[e, d],
            recv_sem=recv_sem.at[e, d],
            device_id={"local": ends[d]},
            device_id_type=MESH,
        )

    mask_copies = [remote(0, d, sm, rm.at[d]) for d in (0, 1)]
    face_copies = [remote(1, d, sx.at[d], rx.at[d]) for d in (0, 1)]
    for copies in (mask_copies, face_copies):
        for d in (0, 1):
            pl.when(sends[d])(copies[d].start)

    def receive(copies):
        for d in (0, 1):
            pl.when(receives[d])(copies[d].wait_recv)

    def blend(parts, masks):
        total = parts[0] * masks[0]
        for t in range(1, count):
            total = total + parts[t] * masks[t]
        return total

    def mask_row(values, step, t, b):
        r = ((step + 1) * count + t) * count + b
        return values[r : r + 1, :]

    def convolve(store, weight, parts, masks, lo, hi):
        both = [taps(blend(parts, masks(b)), 16) for b in range(count)]
        y = dot(weight[lo * ch : hi * ch], jnp.concatenate(both, axis=1))
        for b in range(count):
            store(b, y[:, b * 256 : (b + 1) * 256])

    def into(dst, plane, lo=0, hi=3):
        def store(b, v):
            dst[b, plane, lo * ch : hi * ch] = v

        return store

    def split(a, base, size, n_parts=count):
        return [a[base + t * size : base + (t + 1) * size] for t in range(n_parts)]

    own = sm[...].astype(F32)
    for b in range(count):
        for t in range(count):
            for s in range(3):
                m = mask_row(own, s - 1, t, b)[:, 0:256]
                fm[b, s, t] = jnp.broadcast_to(m, (ch, 256)).astype(BF16)
    for t in range(count):
        for x in range(side):
            lhs1[(x * count + t) * ch : (x * count + t + 1) * ch, 0:face] = x_ref[
                t, :, x * face : (x + 1) * face
            ]
    loads["w1"].wait()
    for p in range(3):
        w1[p * ch : (p + 1) * ch] = w1_ref[:, p * 9 * ch : (p + 1) * 9 * ch]
    sel[...] = dot(lhs1[:, 0:face], t1[...]).astype(BF16)
    for x in range(side):
        convolve(into(y1, x + 1), w1, split(sel, x * count * ch, ch), lambda b: fm.at[b, 1], 0, 3)
    loads["b1"].wait()
    b1 = column(b1_ref[...])

    def first_plane(b, x):
        u = y1[b, x, 0:ch] + y1[b, x + 1, ch : 2 * ch] + y1[b, x + 2, 2 * ch : 3 * ch] + b1
        fst[b, x] = (live[b] * silu(u)).astype(BF16)

    for b in range(count):
        for x in range(1, side - 1):
            first_plane(b, x)

    t2[...] = onehot(iota((256, 256), 0) == jnp.where(inside, py * 16 + pz, -1))
    loads["w2"].wait()
    for p in range(3):
        for part, dst in ((0, w2f), (1, w2u)):
            dst[p * ch : (p + 1) * ch] = jnp.concatenate(
                [
                    w2_ref[:, ((9 * p + k) * 2 + part) * ch : ((9 * p + k) * 2 + part + 1) * ch]
                    for k in range(9)
                ],
                axis=1,
            )
    for x in range(1, side - 1):
        for t in range(count):
            lhs1[(x * count + t) * ch : (x * count + t + 1) * ch, 256:512] = fst[t, x]
    lo, hi = count * ch, (side - 1) * count * ch
    self_ = dot(lhs1[lo:hi, 256:512], t2[...]).astype(BF16)
    for x in range(1, side - 1):
        convolve(into(yf, x + 1), w2f, split(self_, (x - 1) * count * ch, ch), lambda b: fm.at[b, 1], 0, 3)

    n2 = iota((1, 512), 1)
    ry, rz = (n2 >> 3) & 7, n2 & 7
    target = ((n2 >> 6) & 1) * 256 + (2 * ry + ((n2 >> 8) & 1)) * 16 + 2 * rz + ((n2 >> 7) & 1)
    target = jnp.where((ry < half) & (rz < half), target, -1)
    tred[...] = onehot(iota((512, 512), 0) == target)
    loads["wr"].wait()
    loads["br"].wait()
    br = column(br_ref[...])

    def reduce_units(units):
        for i, (get, _, _) in enumerate(units):
            for p in (0, 1):
                r0 = (i * 2 + p) * ch
                lhsr[r0 : r0 + ch, 0:256] = get(p)
                lhsr[r0 : r0 + ch, 256:512] = get(2 + p)
        size = len(units) * 2 * ch
        selr[0:size] = dot(lhsr[0:size], tred[...]).astype(BF16)
        stacked = [
            jnp.concatenate(
                [
                    selr[(i * 2 + p) * ch : (i * 2 + p + 1) * ch, k * 128 : (k + 1) * 128]
                    for p in (0, 1)
                    for k in range(4)
                ],
                axis=0,
            )
            for i in range(len(units))
        ]
        v = dot(wr_ref[...], jnp.concatenate(stacked, axis=1)) + br
        for i, (_, keep, r0) in enumerate(units):
            cin[r0 : r0 + cc] = (keep * silu(v[:, i * 128 : (i + 1) * 128])).astype(BF16)

    def own_unit(t, j):
        return (lambda q: fst[t, 4 * j + q]), live[t], (j * count + t) * cc

    reduce_units([own_unit(t, j) for j in range(1, pairs - 1) for t in range(count)])

    target = (n1 >> 6) * 64 + jnp.where(cy == 0, half - 1, jnp.where(cy == half + 1, 0, cy - 1)) * 8
    target = target + jnp.where(cz == 0, half - 1, jnp.where(cz == half + 1, 0, cz - 1))
    tc[...] = onehot(iota((128, 128), 0) == target)
    uy, uz = (n2 >> 4) & 15, n2 & 15
    qy = jnp.where(uy == 0, side - 1, jnp.where(uy == side + 1, 0, uy - 1))
    qz = jnp.where(uz == 0, side - 1, jnp.where(uz == side + 1, 0, uz - 1))
    target = (n2 >> 8) * 64 + (qy >> 1) * 8 + (qz >> 1)
    target = jnp.where((uy < planes) & (uz < planes), target, -1)
    tup[...] = onehot(iota((128, 512), 0) == target)
    k = iota((256, 1), 0)
    ky, kz = k >> 4, k & 15
    target = jnp.where((ky < side) & (kz < side), ky * side + kz, -1)
    tout[...] = onehot(iota((256, face), 1) == target)
    k = iota((64 * half, 1), 0)
    kx, ky, kz = k >> 6, (k >> 3) & 7, k & 7
    target = jnp.where((ky < half) & (kz < half), (kx * half + ky) * half + kz, -1)
    tbal[...] = onehot(iota((64 * half, half**3), 1) == target)
    for name in ("wc", "bc", "wu", "bu", "b2"):
        loads[name].wait()
    for p in range(3):
        wc[p * cc : (p + 1) * cc] = wc_ref[:, p * 9 * cc : (p + 1) * 9 * cc]
    bc, bu, b2 = column(bc_ref[...]), column(bu_ref[...]), column(b2_ref[...])
    low = n1 < 64
    for b in range(count):
        for t in range(count):
            m = mask_row(own, 0, t, b)[:, 256:384]
            cm[b, 0, t] = jnp.broadcast_to(m, (cc, 128)).astype(BF16)
            m = jnp.where(low, mask_row(own, 1, t, b)[:, 256:384], mask_row(own, -1, t, b)[:, 256:384])
            cm[b, 1, t] = jnp.broadcast_to(m, (cc, 128)).astype(BF16)

    receive(mask_copies)
    far = [rm[d].astype(F32) for d in (0, 1)]
    cross = (-1, 1)
    for d in (0, 1):
        for b in range(count):
            for t in range(count):
                for i, s in enumerate((0, cross[d])):
                    m = mask_row(far[d], s, t, b)
                    fe_m[d, i, b, t] = jnp.broadcast_to(m[:, 0:256], (ch, 256)).astype(BF16)
                    ce_m[d, i, b, t] = jnp.broadcast_to(m[:, 256:384], (cc, 128)).astype(BF16)
    far_live = [[far[d][first_live + b : first_live + b + 1, :] for b in range(count)] for d in (0, 1)]
    far_valid = [[far[d][first_valid + b : first_valid + b + 1, :] for b in range(count)] for d in (0, 1)]

    receive(face_copies)
    for d in (0, 1):
        for k in range(DEPTH):
            for t in range(count):
                r0 = ((d * DEPTH + k) * count + t) * ch
                lhse[r0 : r0 + ch, 0:face] = rx[d, t, :, k * face : (k + 1) * face]
    sele[...] = dot(lhse[:, 0:face], t1[...]).astype(BF16)

    def far_parts(d, k):
        return split(sele, (d * DEPTH + k) * count * ch, ch)

    convolve(into(y1, 0, 0, 1), w1, far_parts(1, DEPTH - 1), lambda b: fm.at[b, 0], 0, 1)
    convolve(into(y1, side + 1, 2, 3), w1, far_parts(0, 0), lambda b: fm.at[b, 2], 2, 3)
    for b in range(count):
        first_plane(b, 0)
        first_plane(b, side - 1)
    near = (split(sel, (side - 1) * count * ch, ch), split(sel, 0, ch))
    outs = DEPTH - 1
    for d in (0, 1):
        for k in range(DEPTH + 1):
            lo, hi = max(0, k - outs + 1), min(3, k + 1)
            crossing = k == (0 if d == 0 else DEPTH)
            parts = near[d] if crossing else far_parts(d, k - 1 if d == 0 else k)
            i = 1 if crossing else 0
            convolve(into(ye.at[d], k, lo, hi), w1, parts, lambda b: fe_m.at[d, i, b], lo, hi)
        for b in range(count):
            for m in range(outs):
                u = ye[d, b, m, 0:ch] + ye[d, b, m + 1, ch : 2 * ch] + ye[d, b, m + 2, 2 * ch : 3 * ch] + b1
                fe[d, b, m] = (far_live[d][b][:, 0:256] * silu(u)).astype(BF16)

    def far_unit(d, t):
        return (lambda q: fe[d, t, q]), far_live[d][t][:, 256:384], ((pairs + d) * count + t) * cc

    units = [own_unit(t, j) for j in sorted({0, pairs - 1}) for t in range(count)]
    reduce_units(units + [far_unit(d, t) for d in (0, 1) for t in range(count)])

    spread = dot(cin[...], tc[...]).astype(BF16)
    unit = [split(spread, j * count * cc, cc) for j in range(pairs + 2)]
    from_right, from_left = unit[pairs], unit[pairs + 1]

    def pick(a, b):
        return jnp.where(low, a.astype(F32), b.astype(F32)).astype(BF16)

    rim = [pick(from_right[t], from_left[t]) for t in range(count)]
    coarse = []
    ups = []
    for b in range(count):
        padded = [blend(unit[j], cm.at[b, 0]) for j in range(pairs)] + [blend(rim, cm.at[b, 1])]
        y = dot(wc[...], jnp.concatenate([taps(v, 8) for v in padded], axis=1))
        width = y.shape[1]
        u = pltpu.roll(y[0:cc], 64, 1) + y[cc : 2 * cc] + pltpu.roll(y[2 * cc :], width - 64, 1) + bc
        co = (valid[b] * silu(u[:, 0 : 64 * half])).astype(BF16)
        coarse.append(co)
        v = (live[b] * (dot(wu_ref[...], co) + bu)).astype(BF16)
        ups.append([v[:, j * 128 : (j + 1) * 128] for j in range(pairs)])

    zs = ([], [], [])
    for b in range(count):
        a = blend(from_left, ce_m.at[1, 0, b])
        bb = blend(unit[0], ce_m.at[1, 1, b])
        c = blend(unit[pairs - 1], ce_m.at[0, 1, b])
        dd = blend(from_right, ce_m.at[0, 0, b])
        zs[0].append(pick(a, c))
        zs[1].append(shifted(pick(dd, a), 64))
        zs[2].append(pick(bb, dd))
    deep = jnp.concatenate([taps(jnp.concatenate(z, axis=1), 8) for z in zs], axis=0)
    u = dot(wc_ref[...], deep) + bc
    keep = jnp.concatenate(
        [jnp.where(low, far_valid[1][b][:, 256:384], far_valid[0][b][:, 256:384]) for b in range(count)], axis=1
    )
    co = (keep * silu(u)).astype(BF16)
    keep = jnp.concatenate(
        [jnp.where(low, far_live[1][b][:, 256:384], far_live[0][b][:, 256:384]) for b in range(count)], axis=1
    )
    v = (keep * (dot(wu_ref[...], co) + bu)).astype(BF16)
    for b in range(count):
        ups[b].append(v[:, b * 128 : (b + 1) * 128])

    dense = [dot(co, tbal[...]) for co in coarse]

    def outgoing(r, k):
        total = jnp.zeros_like(dense[0])
        for b in range(count):
            total = total + dense[b] * jnp.where(dest[b] == r * SEND_CAP + k, valid[b], 0.0)
        return total.astype(BF16)

    sent = []
    for d in range(1, n_group):
        other = lax.rem(grp + d, n_group)
        for k in range(SEND_CAP):
            sb[d - 1, k] = outgoing(other, k)
        c = pltpu.make_async_remote_copy(
            src_ref=sb.at[d - 1],
            dst_ref=rb.at[d - 1],
            send_sem=bal_send.at[d - 1],
            recv_sem=bal_recv.at[d - 1],
            device_id={"group": other},
            device_id_type=MESH,
        )
        c.start()
        sent.append(c)
    for k in range(SEND_CAP):
        bal_ref[grp * SEND_CAP + k] = outgoing(grp, k)

    sources = [[fe[1, t, outs - 1] for t in range(count)], [fst[t, 0] for t in range(count)]]
    sources += [[fst[t, side - 1] for t in range(count)], [fe[0, t, 0] for t in range(count)]]
    selo = dot(jnp.concatenate([v for s in sources for v in s], axis=0), t2[...]).astype(BF16)
    convolve(into(yf, 0, 0, 1), w2f, split(selo, 0, ch), lambda b: fm.at[b, 0], 0, 1)
    convolve(into(yf, 1), w2f, split(selo, count * ch, ch), lambda b: fm.at[b, 1], 0, 3)
    convolve(into(yf, side), w2f, split(selo, 2 * count * ch, ch), lambda b: fm.at[b, 1], 0, 3)
    convolve(into(yf, side + 1, 2, 3), w2f, split(selo, 3 * count * ch, ch), lambda b: fm.at[b, 2], 2, 3)

    wide = jnp.concatenate([ups[t][j] for j in range(pairs + 1) for t in range(count)], axis=0)
    selu = dot(wide, tup[...]).astype(BF16)
    for j in range(pairs + 1):
        for h in (0, 1):
            parts = [v[:, h * 256 : (h + 1) * 256] for v in split(selu, j * count * ch, ch)]
            if j < pairs:
                convolve(into(y2, 1 + 2 * j + h), w2u, parts, lambda b: fm.at[b, 1], 0, 3)
            elif h == 0:
                convolve(into(y2, 0, 0, 1), w2u, parts, lambda b: fm.at[b, 0], 0, 1)
            else:
                convolve(into(y2, half + 1, 2, 3), w2u, parts, lambda b: fm.at[b, 2], 2, 3)

    for b in range(count):
        for x in range(side):
            u = b2
            for p in range(3):
                u = u + yf[b, x + p, p * ch : (p + 1) * ch]
                u = u + y2[b, (x + p + 1) // 2, p * ch : (p + 1) * ch]
            lhso[b, x * ch : (x + 1) * ch] = (live[b] * silu(u)).astype(BF16)
        flat = dot(lhso[b], tout[...])
        for x in range(side):
            out_ref[b, :, x * face : (x + 1) * face] = flat[x * ch : (x + 1) * ch].astype(BF16)

    for copies in (mask_copies, face_copies):
        for d in (0, 1):
            pl.when(sends[d])(copies[d].wait_send)
    for d, c in enumerate(sent):
        c.wait()
        source = lax.rem(grp + n_group - (d + 1), n_group)
        for k in range(SEND_CAP):
            bal_ref[source * SEND_CAP + k] = rb[d, k]


def local(n_local, n_group, features, neighbours, coarse_dest, *weights):
    count, ch, cells = features.shape
    side = round(cells ** (1 / 3))
    cc = weights[2].shape[0]
    half, face = side // 2, side * side
    pairs = half // 2
    rows = (3 * count * count + 2 * count + 15) // 16 * 16
    span = (DEPTH * face + 127) // 128 * 128
    if side + 2 > 16 or half + 2 > 8 or half % 2 or side**3 != cells or pairs < 2:
        raise ValueError("side")
    vmem = lambda *shape: pltpu.VMEM(shape, BF16)
    weights = [w.reshape(1, -1) if w.ndim == 1 else w for w in weights]
    anywhere = pl.BlockSpec(memory_space=pl.ANY)
    whole = pl.BlockSpec(memory_space=pltpu.VMEM)
    units = (pairs + 2) * count
    return pl.pallas_call(
        functools.partial(kernel, (side, count, ch, cc, n_local, n_group)),
        out_shape=(
            pltpu.VMEM(features.shape, BF16),
            pltpu.VMEM((n_group * SEND_CAP, cc, half**3), BF16),
        ),
        in_specs=[anywhere] * (3 + len(weights)),
        out_specs=(whole, whole),
        scratch_shapes=[
            pltpu.SMEM(neighbours.shape, I32),
            pltpu.SMEM(coarse_dest.shape, I32),
            pltpu.VMEM(neighbours.shape, I32),
            vmem(*features.shape),
        ]
        + [pltpu.VMEM(w.shape, w.dtype) for w in weights]
        + [
            vmem(2, count, ch, span),
            vmem(2, count, ch, span),
            vmem(rows, 384),
            vmem(2, rows, 384),
            vmem(n_group - 1, SEND_CAP, cc, half**3),
            vmem(n_group - 1, SEND_CAP, cc, half**3),
            vmem(face, 256),
            vmem(256, 256),
            vmem(512, 512),
            vmem(128, 128),
            vmem(128, 512),
            vmem(256, face),
            vmem(64 * half, half**3),
            vmem(3 * ch, 9 * ch),
            vmem(3 * cc, 9 * cc),
            vmem(3 * ch, 9 * ch),
            vmem(3 * ch, 9 * ch),
            vmem(side * count * ch, 512),
            vmem(2 * DEPTH * count * ch, 256),
            vmem(units * 2 * ch, 512),
            vmem(count, side * ch, 256),
            pltpu.VMEM((count, side + 2, 3 * ch, 256), F32),
            pltpu.VMEM((2, count, DEPTH + 1, 3 * ch, 256), F32),
            pltpu.VMEM((count, side + 2, 3 * ch, 256), F32),
            pltpu.VMEM((count, half + 2, 3 * ch, 256), F32),
            vmem(count, side, ch, 256),
            vmem(2, count, DEPTH - 1, ch, 256),
            vmem(units * cc, 128),
            vmem(side * count * ch, 256),
            vmem(2 * DEPTH * count * ch, 256),
            vmem(units * 2 * ch, 512),
            vmem(count, 3, count, ch, 256),
            vmem(2, 2, count, count, ch, 256),
            vmem(count, 2, count, cc, 128),
            vmem(2, 2, count, count, cc, 128),
            pltpu.SemaphoreType.DMA((3 + len(weights) + 1,)),
            pltpu.SemaphoreType.DMA((2, 2)),
            pltpu.SemaphoreType.DMA((2, 2)),
            pltpu.SemaphoreType.DMA((n_group - 1,)),
            pltpu.SemaphoreType.DMA((n_group - 1,)),
        ],
        compiler_params=pltpu.CompilerParams(
            collective_id=0, has_side_effects=True, vmem_limit_bytes=60 << 20
        ),
    )(neighbours, coarse_dest, features, *weights)


def solution(mesh):
    slots = P(("group", "local"), None, None)
    return jax.shard_map(
        functools.partial(local, mesh.shape["local"], mesh.shape["group"]),
        mesh=mesh,
        in_specs=(slots, P(("group", "local"), None), P(("group", "local"))) + (P(),) * 10,
        out_specs=(slots, slots),
        check_vma=False,
    )
```

```python
import functools

import jax
import jax.numpy as jnp
import numpy as np
from jax import lax
from jax.experimental import pallas as pl
from jax.experimental.pallas import tpu as pltpu
from jax.sharding import PartitionSpec as P

SEND_CAP = 2
DEPTH = 2
HELD = 4
MESH = pl.DeviceIdType.MESH
F32 = jnp.float32
BF16 = jnp.bfloat16
I32 = jnp.int32


def iota(shape, dim):
    return lax.broadcasted_iota(I32, shape, dim)


def onehot(mask):
    return jnp.where(mask, 1.0, 0.0).astype(BF16)


def column(row):
    n = row.shape[1]
    wide = jnp.broadcast_to(row, (n, n))
    return jnp.sum(jnp.where(iota((n, n), 0) == iota((n, n), 1), wide, 0.0), axis=1, keepdims=True)


def silu(u):
    return u / (1.0 + jnp.exp(-u))


def shifted(v, s):
    if s == 0:
        return v
    return jnp.concatenate([v[:, s:], v[:, :s]], axis=1)


def dot(a, b):
    return jnp.dot(a, b, preferred_element_type=F32)


def taps(v, stride):
    return jnp.concatenate([shifted(v, q * stride + r) for q in range(3) for r in range(3)], axis=0)


def offset(v, top):
    return jnp.where(v == 0, -1, jnp.where(v == top, 1, 0))


def kernel(
    sizes,
    nb_hbm,
    dest_hbm,
    x_hbm,
    w1_hbm,
    b1_hbm,
    wr_hbm,
    br_hbm,
    wc_hbm,
    bc_hbm,
    wu_hbm,
    bu_hbm,
    w2_hbm,
    b2_hbm,
    t1_hbm,
    t2_hbm,
    tred_hbm,
    tup_hbm,
    tout_hbm,
    tbal_hbm,
    rows_ref,
    tout,
    tbal,
    bal_ref,
    nb,
    dest,
    nb_ref,
    x_ref,
    w1_ref,
    b1_ref,
    wr_ref,
    br_ref,
    wc_ref,
    bc_ref,
    wu_ref,
    bu_ref,
    w2_ref,
    b2_ref,
    sx,
    rx,
    sm,
    rm,
    sf,
    rf,
    sc,
    rc,
    sb,
    rb,
    t1,
    t2,
    tred,
    tup,
    w1,
    wc,
    w2f,
    w2u,
    lhs1,
    lhse,
    lhsr,
    y1,
    yf,
    y2,
    uf,
    yc,
    fst,
    fe,
    sel,
    sele,
    fm,
    fe_m,
    cm,
    ce_m,
    load_sem,
    send_sem,
    recv_sem,
    bal_send,
    bal_recv,
):
    side, count, ch, cc, n_local, n_group = sizes
    half = side // 2
    face = side * side
    planes = side + 2
    pairs = half // 2
    me = lax.axis_index("local")
    grp = lax.axis_index("group")
    right, left = lax.rem(me + 1, n_local), lax.rem(me + n_local - 1, n_local)
    ends = (left, right)
    has_left, has_right = me > 0, me < n_local - 1
    sends, receives = (has_left, has_right), (has_right, has_left)

    barrier = pltpu.get_barrier_semaphore()
    for d in (0, 1):

        @pl.when(sends[d])
        def _():
            pl.semaphore_signal(barrier, inc=1, device_id={"local": ends[d]}, device_id_type=MESH)

    for d in range(1, n_group):
        pl.semaphore_signal(
            barrier, inc=1, device_id={"group": lax.rem(grp + d, n_group)}, device_id_type=MESH
        )

    loads = {}
    pieces = (
        ("nbv", nb_hbm, nb_ref),
        ("x", x_hbm, x_ref),
        ("nb", nb_hbm, nb),
        ("dest", dest_hbm, dest),
        ("t1", t1_hbm, t1),
        ("w1", w1_hbm, w1_ref),
        ("b1", b1_hbm, b1_ref),
        ("tred", tred_hbm, tred),
        ("wr", wr_hbm, wr_ref),
        ("br", br_hbm, br_ref),
        ("t2", t2_hbm, t2),
        ("w2", w2_hbm, w2_ref),
        ("wc", wc_hbm, wc_ref),
        ("bc", bc_hbm, bc_ref),
        ("wu", wu_hbm, wu_ref),
        ("bu", bu_hbm, bu_ref),
        ("b2", b2_hbm, b2_ref),
        ("tup", tup_hbm, tup),
        ("tout", tout_hbm, tout),
        ("tbal", tbal_hbm, tbal),
    )
    for i, (name, src, dst) in enumerate(pieces):
        loads[name] = pltpu.make_async_copy(src, dst, load_sem.at[i])
        loads[name].start()

    for d in (0, 1):

        @pl.when(jnp.logical_not(receives[d]))
        def _():
            rx[d] = jnp.zeros(rx.shape[1:], BF16)
            rm[d] = jnp.zeros(rm.shape[1:], BF16)
            rf[d] = jnp.zeros(rf.shape[1:], BF16)
            rc[d] = jnp.zeros(rc.shape[1:], BF16)

    n = iota((1, 256), 1)
    ny, nz = n >> 4, n & 15
    n1 = iota((1, 128), 1)
    cy, cz = (n1 >> 3) & 7, n1 & 7
    low = n1 < 64
    fy, fz = offset(ny, side + 1), offset(nz, side + 1)
    gy, gz = offset(cy, half + 1), offset(cz, half + 1)

    direction = jnp.concatenate([(fy + 1) * 3 + fz + 1, (gy + 1) * 3 + gz + 1], axis=1)
    table = onehot(lax.rem(iota((27, 384), 0), 9) == direction)
    rows = sm.shape[0]
    first_live = 3 * count * count
    first_valid = first_live + count
    loads["nbv"].wait()
    row = iota((rows, 27), 0)
    entries = jnp.zeros((rows, 27), I32)
    for b in range(count):
        entries = jnp.where(lax.rem(row, count) == b, nb_ref[b : b + 1, :], entries)
    slot = lax.rem(lax.div(row, count), count)
    step_of = lax.div(row, count * count)
    chosen = onehot((entries == slot) & (lax.div(iota((rows, 27), 1), 9) == step_of) & (row < first_live))
    table_rows = dot(chosen, table)
    loads["nb"].wait()
    loads["dest"].wait()
    live = [jnp.where(nb[b, 13] >= 0, 1.0, 0.0) for b in range(count)]
    valid = [jnp.where(dest[b] >= 0, live[b], 0.0) for b in range(count)]
    wide_row = iota((rows, 384), 0)
    for b in range(count):
        table_rows = jnp.where(wide_row == first_live + b, live[b], table_rows)
        table_rows = jnp.where(wide_row == first_valid + b, valid[b], table_rows)
    sm[...] = table_rows.astype(BF16)

    loads["x"].wait()
    span = DEPTH * face
    for t in range(count):
        sx[0, t, :, 0:span] = x_ref[t, :, 0:span]
        sx[1, t, :, 0:span] = x_ref[t, :, side * face - span : side * face]
        tail = sx.shape[3] - span
        for d in (0, 1):
            sx[d, t, :, span:] = jnp.zeros((ch, tail), BF16)

    def remote(e, d, src, dst):
        return pltpu.make_async_remote_copy(
            src_ref=src,
            dst_ref=dst,
            send_sem=send_sem.at[e, d],
            recv_sem=recv_sem.at[e, d],
            device_id={"local": ends[d]},
            device_id_type=MESH,
        )

    def receive(copies):
        for d in (0, 1):
            pl.when(receives[d])(copies[d].wait_recv)

    def blend(parts, masks):
        total = parts[0] * masks[0]
        for t in range(1, count):
            total = total + parts[t] * masks[t]
        return total

    def mask_row(values, step, t, b):
        r = ((step + 1) * count + t) * count + b
        return values[r : r + 1, :]

    def convolve(store, weight, parts, masks, lo, hi):
        both = [taps(blend(parts, masks(b)), 16) for b in range(count)]
        y = dot(weight[lo * ch : hi * ch], jnp.concatenate(both, axis=1))
        for b in range(count):
            store(b, y[:, b * 256 : (b + 1) * 256])

    def into(dst, plane, lo=0, hi=3):
        def store(b, v):
            dst[b, plane, lo * ch : hi * ch] = v

        return store

    def split(a, base, size, n_parts=count):
        return [a[base + t * size : base + (t + 1) * size] for t in range(n_parts)]

    beside = jnp.where(has_left, 1, 0) + jnp.where(has_right, 1, 0)
    mask_copies = [remote(0, d, sm, rm.at[d]) for d in (0, 1)]
    face_copies = [remote(1, d, sx.at[d], rx.at[d]) for d in (0, 1)]

    own = sm[...].astype(F32)
    for b in range(count):
        for t in range(count):
            for s in range(3):
                m = mask_row(own, s - 1, t, b)[:, 0:256]
                fm[b, s, t] = jnp.broadcast_to(m, (ch, 256)).astype(BF16)
    pl.semaphore_wait(barrier, beside + n_group - 1)
    for copies in (mask_copies, face_copies):
        for d in (0, 1):
            pl.when(sends[d])(copies[d].start)
    for t in range(count):
        for x in range(side):
            lhs1[(x * count + t) * ch : (x * count + t + 1) * ch, 0:face] = x_ref[
                t, :, x * face : (x + 1) * face
            ]
    loads["w1"].wait()
    for p in range(3):
        w1[p * ch : (p + 1) * ch] = w1_ref[:, p * 9 * ch : (p + 1) * 9 * ch]
    loads["t1"].wait()
    sel[...] = dot(lhs1[:, 0:face], t1[...]).astype(BF16)
    first_planes = [x for x in range(side) if x < 5 or x > side - 6]
    for x in first_planes:
        convolve(into(y1, x + 1), w1, split(sel, x * count * ch, ch), lambda b: fm.at[b, 1], 0, 3)
    loads["b1"].wait()
    b1 = column(b1_ref[...])

    def first_plane(b, x):
        u = y1[b, x, 0:ch] + y1[b, x + 1, ch : 2 * ch] + y1[b, x + 2, 2 * ch : 3 * ch] + b1
        fst[b, x] = (live[b] * silu(u)).astype(BF16)

    for b in range(count):
        for x in (1, 2, 3, side - 4, side - 3, side - 2):
            first_plane(b, x)

    loads["tred"].wait()
    loads["wr"].wait()
    loads["br"].wait()
    br = column(br_ref[...])

    def reduce_units(base, units):
        for i, (low_of, high_of, _) in enumerate(units):
            for p in (0, 1):
                r0 = ((base + i) * 2 + p) * ch
                lhsr[r0 : r0 + ch, 0:256] = low_of(p)
                lhsr[r0 : r0 + ch, 256:512] = high_of(p)
        start, size = base * 2 * ch, len(units) * 2 * ch
        a = dot(lhsr[start : start + size], tred[...]).astype(BF16)
        stacked = [
            jnp.concatenate(
                [
                    a[(i * 2 + p) * ch : (i * 2 + p + 1) * ch, k * 128 : (k + 1) * 128]
                    for p in (0, 1)
                    for k in range(4)
                ],
                axis=0,
            )
            for i in range(len(units))
        ]
        v = dot(wr_ref[...], jnp.concatenate(stacked, axis=1)) + br
        return [(keep * silu(v[:, i * 128 : (i + 1) * 128])).astype(BF16) for i, (_, _, keep) in enumerate(units)]

    def own_unit(t, lower, upper):
        return (lambda p: fst[t, 2 * lower + p]), (lambda p: fst[t, 2 * upper + p]), live[t]

    inner = reduce_units(0, [own_unit(t, half - 2, 1) for t in range(count)])
    for t in range(count):
        sc[t] = inner[t]
        sf[0, t] = fst[t, 1]
        sf[1, t] = fst[t, side - 2]
    first_copies = [remote(2, d, sf.at[d], rf.at[d]) for d in (0, 1)]
    coarse_copies = [remote(3, d, sc, rc.at[d]) for d in (0, 1)]
    for copies in (coarse_copies, first_copies):
        for d in (0, 1):
            pl.when(sends[d])(copies[d].start)

    for x in range(side):
        if x not in first_planes:
            convolve(into(y1, x + 1), w1, split(sel, x * count * ch, ch), lambda b: fm.at[b, 1], 0, 3)
    for b in range(count):
        for x in range(4, side - 4):
            first_plane(b, x)
    middles = [own_unit(t, 2 * j, 2 * j + 1) for j in range(1, pairs - 1) for t in range(count)]
    inner += reduce_units(count, middles)

    loads["b2"].wait()
    b2 = column(b2_ref[...])

    def biased(plane):
        def store(b, v):
            yf[b, plane, 0:ch] = v[0:ch]
            yf[b, plane, ch : 2 * ch] = v[ch : 2 * ch] + b2
            yf[b, plane, 2 * ch :] = v[2 * ch :]

        return store

    loads["t2"].wait()
    loads["w2"].wait()
    for p in range(3):
        for part, dst in ((0, w2f), (1, w2u)):
            dst[p * ch : (p + 1) * ch] = jnp.concatenate(
                [
                    w2_ref[:, ((9 * p + k) * 2 + part) * ch : ((9 * p + k) * 2 + part + 1) * ch]
                    for k in range(9)
                ],
                axis=1,
            )
    for x in range(1, side - 1):
        for t in range(count):
            lhs1[(x * count + t) * ch : (x * count + t + 1) * ch, 256:512] = fst[t, x]
    lo, hi = count * ch, (side - 1) * count * ch
    self_ = dot(lhs1[lo:hi, 256:512], t2[...]).astype(BF16)
    for x in range(1, side - 1):
        convolve(biased(x + 1), w2f, split(self_, (x - 1) * count * ch, ch), lambda b: fm.at[b, 1], 0, 3)

    for name in ("wc", "bc", "wu", "bu", "tup", "tout", "tbal"):
        loads[name].wait()
    for p in range(3):
        wc[p * cc : (p + 1) * cc] = wc_ref[:, p * 9 * cc : (p + 1) * 9 * cc]
    bc, bu = column(bc_ref[...]), column(bu_ref[...])
    for b in range(count):
        for t in range(count):
            m = mask_row(own, 0, t, b)[:, 256:384]
            cm[b, 0, t] = jnp.broadcast_to(m, (cc, 128)).astype(BF16)
            m = jnp.where(low, mask_row(own, 1, t, b)[:, 256:384], mask_row(own, -1, t, b)[:, 256:384])
            cm[b, 1, t] = jnp.broadcast_to(m, (cc, 128)).astype(BF16)

    receive(mask_copies)
    far = [rm[d].astype(F32) for d in (0, 1)]
    cross = (-1, 1)
    for b in range(count):
        for t in range(count):
            for d in (0, 1):
                for i, s in enumerate((0, cross[d])):
                    m = mask_row(far[d], s, t, b)
                    fe_m[d, i, b, t] = jnp.broadcast_to(m[:, 0:256], (ch, 256)).astype(BF16)
            from_r, from_l = mask_row(far[0], 0, t, b), mask_row(far[1], 0, t, b)
            mixed = (
                (from_l, mask_row(far[0], -1, t, b)),
                (from_r, from_l),
                (mask_row(far[1], 1, t, b), from_r),
            )
            for i, (lower, upper) in enumerate(mixed):
                m = jnp.where(low, lower[:, 256:384], upper[:, 256:384])
                ce_m[i, b, t] = jnp.broadcast_to(m, (cc, 128)).astype(BF16)
    far_live = [[far[d][first_live + b : first_live + b + 1, :] for b in range(count)] for d in (0, 1)]
    far_valid = [[far[d][first_valid + b : first_valid + b + 1, :] for b in range(count)] for d in (0, 1)]

    receive(face_copies)
    for d in (0, 1):
        for k in range(DEPTH):
            for t in range(count):
                r0 = ((d * DEPTH + k) * count + t) * ch
                lhse[r0 : r0 + ch, 0:face] = rx[d, t, :, k * face : (k + 1) * face]
    sele[...] = dot(lhse[:, 0:face], t1[...]).astype(BF16)

    def far_parts(d, k):
        return split(sele, (d * DEPTH + k) * count * ch, ch)

    convolve(into(y1, 0, 0, 1), w1, far_parts(1, DEPTH - 1), lambda b: fm.at[b, 0], 0, 1)
    convolve(into(y1, side + 1, 2, 3), w1, far_parts(0, 0), lambda b: fm.at[b, 2], 2, 3)
    for b in range(count):
        first_plane(b, 0)
        first_plane(b, side - 1)
    near = ((split(sel, (side - 1) * count * ch, ch), 1), (split(sel, 0, ch), 1))
    stacks = (
        (near[0], (far_parts(0, 0), 0), (far_parts(0, 1), 0)),
        ((far_parts(1, 0), 0), (far_parts(1, 1), 0), near[1]),
    )
    for d in (0, 1):
        deep = jnp.concatenate(
            [
                jnp.concatenate([taps(blend(parts, fe_m.at[d, i, b]), 16) for b in range(count)], axis=1)
                for parts, i in stacks[d]
            ],
            axis=0,
        )
        u = dot(w1_ref[...], deep) + b1
        for b in range(count):
            v = silu(u[:, b * 256 : (b + 1) * 256])
            fe[d, b] = (far_live[d][b][:, 0:256] * v).astype(BF16)

    sources = [[fe[1, t] for t in range(count)], [fst[t, 0] for t in range(count)]]
    sources += [[fst[t, side - 1] for t in range(count)], [fe[0, t] for t in range(count)]]
    selo = dot(jnp.concatenate([v for s in sources for v in s], axis=0), t2[...]).astype(BF16)
    convolve(into(yf, 0, 0, 1), w2f, split(selo, 0, ch), lambda b: fm.at[b, 0], 0, 1)
    convolve(biased(1), w2f, split(selo, count * ch, ch), lambda b: fm.at[b, 1], 0, 3)
    convolve(biased(side), w2f, split(selo, 2 * count * ch, ch), lambda b: fm.at[b, 1], 0, 3)
    convolve(into(yf, side + 1, 2, 3), w2f, split(selo, 3 * count * ch, ch), lambda b: fm.at[b, 2], 2, 3)

    for b in range(count):
        for x in range(side):
            uf[b, x] = yf[b, x, 0:ch] + yf[b, x + 1, ch : 2 * ch] + yf[b, x + 2, 2 * ch :]

    ends_ = reduce_units(len(inner), [own_unit(t, 0, half - 1) for t in range(count)])

    def pick(a, b):
        return jnp.where(low, a.astype(F32), b.astype(F32)).astype(BF16)

    shared, middle = inner[0:count], inner[count:]
    middle = [middle[j * count : (j + 1) * count] for j in range(pairs - 2)]
    bottom = [pick(ends_[t], shared[t]) for t in range(count)]
    top = [pick(shared[t], ends_[t]) for t in range(count)]
    for b in range(count):
        padded = [blend(v, cm.at[b, 0]) for v in [bottom] + middle + [top]]
        yc[b] = dot(wc[...], jnp.concatenate([taps(v, 8) for v in padded], axis=1))

    receive(coarse_copies)
    receive(first_copies)

    def far_unit(t):
        r = (fe[0, t], rf[0, t])
        l = (rf[1, t], fe[1, t])
        keep = jnp.where(low, far_live[0][t][:, 256:384], far_live[1][t][:, 256:384])
        return (lambda p: r[p]), (lambda p: l[p]), keep

    rim = reduce_units(len(inner) + count, [far_unit(t) for t in range(count)])
    from_right, from_left = [[rc[d, t] for t in range(count)] for d in (0, 1)]

    y_rim = dot(wc[...], jnp.concatenate([taps(blend(rim, cm.at[b, 1]), 8) for b in range(count)], axis=1))
    coarse = []
    ups = []
    for b in range(count):
        y = jnp.concatenate([yc[b], y_rim[:, b * 128 : (b + 1) * 128]], axis=1)
        width = y.shape[1]
        u = pltpu.roll(y[0:cc], 64, 1) + y[cc : 2 * cc] + pltpu.roll(y[2 * cc :], width - 64, 1) + bc
        coarse.append((valid[b] * silu(u[:, 0 : 64 * half])).astype(BF16))

    def outgoing(r, k):
        total = jnp.zeros(coarse[0].shape, F32)
        for b in range(count):
            total = total + coarse[b].astype(F32) * jnp.where(dest[b] == r * SEND_CAP + k, valid[b], 0.0)
        return total.astype(BF16)

    sent = []
    for d in range(1, n_group):
        other = lax.rem(grp + d, n_group)
        for k in range(SEND_CAP):
            sb[d - 1, k] = outgoing(other, k)
        c = pltpu.make_async_remote_copy(
            src_ref=sb.at[d - 1],
            dst_ref=rb.at[d - 1],
            send_sem=bal_send.at[d - 1],
            recv_sem=bal_recv.at[d - 1],
            device_id={"group": other},
            device_id_type=MESH,
        )
        c.start()
        sent.append(c)
    for k in range(SEND_CAP):
        bal_ref[grp * SEND_CAP + k] = outgoing(grp, k)

    for b in range(count):
        v = (live[b] * (dot(wu_ref[...], coarse[b]) + bu)).astype(BF16)
        ups.append([v[:, j * 128 : (j + 1) * 128] for j in range(pairs)])

    below = [pick(from_left[t], ends_[t]) for t in range(count)]
    above = [pick(ends_[t], from_right[t]) for t in range(count)]
    zs = [[blend(v, ce_m.at[i, b]) for b in range(count)] for i, v in enumerate((below, rim, above))]
    zs[1] = [shifted(v, 64) for v in zs[1]]
    deep = jnp.concatenate([taps(jnp.concatenate(z, axis=1), 8) for z in zs], axis=0)
    u = dot(wc_ref[...], deep) + bc
    keep = jnp.concatenate(
        [jnp.where(low, far_valid[1][b][:, 256:384], far_valid[0][b][:, 256:384]) for b in range(count)], axis=1
    )
    co = (keep * silu(u)).astype(BF16)
    keep = jnp.concatenate(
        [jnp.where(low, far_live[1][b][:, 256:384], far_live[0][b][:, 256:384]) for b in range(count)], axis=1
    )
    v = (keep * (dot(wu_ref[...], co) + bu)).astype(BF16)
    for b in range(count):
        ups[b].append(v[:, b * 128 : (b + 1) * 128])

    wide = jnp.concatenate([ups[t][j] for j in range(pairs + 1) for t in range(count)], axis=0)
    selu = dot(wide, tup[...]).astype(BF16)
    for j in range(pairs + 1):
        for h in (0, 1):
            parts = [v[:, h * 256 : (h + 1) * 256] for v in split(selu, j * count * ch, ch)]
            if j < pairs:
                convolve(into(y2, 1 + 2 * j + h), w2u, parts, lambda b: fm.at[b, 1], 0, 3)
            elif h == 0:
                convolve(into(y2, 0, 0, 1), w2u, parts, lambda b: fm.at[b, 0], 0, 1)
            else:
                convolve(into(y2, half + 1, 2, 3), w2u, parts, lambda b: fm.at[b, 2], 2, 3)

    for b in range(count):
        for x in range(side):
            u = uf[b, x]
            for p in range(3):
                u = u + y2[b, (x + p + 1) // 2, p * ch : (p + 1) * ch]
            rows_ref[b, x * ch : (x + 1) * ch] = (live[b] * silu(u)).astype(BF16)

    for copies in (mask_copies, face_copies, coarse_copies, first_copies):
        for d in (0, 1):
            pl.when(sends[d])(copies[d].wait_send)
    for d, c in enumerate(sent):
        c.wait()
        source = lax.rem(grp + n_group - (d + 1), n_group)
        for k in range(SEND_CAP):
            bal_ref[source * SEND_CAP + k] = rb[d, k]


def finish_kernel(rows_ref, tout, tbal, bal_ref, out_hbm, bal_hbm, out, bal, sems):
    count, ch = out.shape[:2]
    face = tout.shape[1]
    side = out.shape[2] // face
    copies = []
    for b in range(count):
        flat = dot(rows_ref[b], tout[...])
        for x in range(side):
            out[b, :, x * face : (x + 1) * face] = flat[x * ch : (x + 1) * ch].astype(BF16)
        copies.append(pltpu.make_async_copy(out.at[b], out_hbm.at[b], sems.at[b]))
        copies[-1].start()
    slots, cc = bal_ref.shape[0], bal_ref.shape[1]
    dense = dot(jnp.concatenate([bal_ref[k] for k in range(slots)], axis=0), tbal[...])
    for k in range(slots):
        bal[k] = dense[k * cc : (k + 1) * cc].astype(BF16)
    copies.append(pltpu.make_async_copy(bal, bal_hbm, sems.at[count]))
    copies[-1].start()
    for c in copies:
        c.wait()


def tables(side):
    half = side // 2
    face = side * side

    def hot(rows, target):
        return (np.arange(rows)[:, None] == target[None, :]).astype(BF16)

    def wrap(v, n):
        return np.where(v == 0, n - 1, np.where(v == n + 1, 0, v - 1))

    n = np.arange(256)
    ny, nz = n >> 4, n & 15
    inside = (ny < side + 2) & (nz < side + 2)
    t1 = hot(face, np.where(inside, wrap(ny, side) * side + wrap(nz, side), -1))
    t2 = hot(256, np.where(inside, wrap(ny, side) * 16 + wrap(nz, side), -1))
    n2 = np.arange(512)
    ry, rz = (n2 >> 3) & 7, n2 & 7
    target = ((n2 >> 6) & 1) * 256 + (2 * wrap(ry, half) + ((n2 >> 8) & 1)) * 16 + 2 * wrap(rz, half) + ((n2 >> 7) & 1)
    tred = hot(512, np.where((ry < half + 2) & (rz < half + 2), target, -1))
    uy, uz = (n2 >> 4) & 15, n2 & 15
    target = (n2 >> 8) * 64 + (wrap(uy, side) >> 1) * 8 + (wrap(uz, side) >> 1)
    tup = hot(128, np.where((uy < side + 2) & (uz < side + 2), target, -1))
    tout = hot(face, np.where((ny < side) & (nz < side), ny * side + nz, -1)).T
    k = np.arange(64 * half)
    kx, ky, kz = k >> 6, (k >> 3) & 7, k & 7
    tbal = hot(half**3, np.where((ky < half) & (kz < half), (kx * half + ky) * half + kz, -1)).T
    return [jnp.asarray(t) for t in (t1, t2, tred, tup, tout, tbal)]


def local(n_local, n_group, features, neighbours, coarse_dest, *weights):
    count, ch, cells = features.shape
    side = round(cells ** (1 / 3))
    cc = weights[2].shape[0]
    half, face = side // 2, side * side
    pairs = half // 2
    rows = (3 * count * count + 2 * count + 15) // 16 * 16
    span = (DEPTH * face + 127) // 128 * 128
    if side + 2 > 16 or half + 2 > 8 or half % 2 or side**3 != cells or pairs < 2:
        raise ValueError("side")
    vmem = lambda *shape: pltpu.VMEM(shape, BF16)
    weights = [w.reshape(1, -1) if w.ndim == 1 else w for w in weights]
    onehots = tables(side)
    anywhere = pl.BlockSpec(memory_space=pl.ANY)
    whole = pl.BlockSpec(memory_space=pltpu.VMEM)
    units = (pairs - 1) * count
    middle = pl.pallas_call(
        functools.partial(kernel, (side, count, ch, cc, n_local, n_group)),
        out_shape=(
            vmem(count, side * ch, 256),
            vmem(256, face),
            vmem(64 * half, half**3),
            vmem(n_group * SEND_CAP, cc, 64 * half),
        ),
        in_specs=[anywhere] * (3 + len(weights) + len(onehots)),
        out_specs=(whole,) * 4,
        scratch_shapes=[
            pltpu.SMEM(neighbours.shape, I32),
            pltpu.SMEM(coarse_dest.shape, I32),
            pltpu.VMEM(neighbours.shape, I32),
            vmem(*features.shape),
        ]
        + [pltpu.VMEM(w.shape, w.dtype) for w in weights]
        + [
            vmem(2, count, ch, span),
            vmem(2, count, ch, span),
            vmem(rows, 384),
            vmem(2, rows, 384),
            vmem(2, count, ch, 256),
            vmem(2, count, ch, 256),
            vmem(count, cc, 128),
            vmem(2, count, cc, 128),
            vmem(n_group - 1, SEND_CAP, cc, 64 * half),
            vmem(n_group - 1, SEND_CAP, cc, 64 * half),
            vmem(face, 256),
            vmem(256, 256),
            vmem(512, 512),
            vmem(128, 512),
            vmem(3 * ch, 9 * ch),
            vmem(3 * cc, 9 * cc),
            vmem(3 * ch, 9 * ch),
            vmem(3 * ch, 9 * ch),
            vmem(side * count * ch, 512),
            vmem(2 * DEPTH * count * ch, 256),
            vmem((units + 2 * count) * 2 * ch, 512),
            pltpu.VMEM((count, side + 2, 3 * ch, 256), F32),
            pltpu.VMEM((count, side + 2, 3 * ch, 256), F32),
            pltpu.VMEM((count, half + 2, 3 * ch, 256), F32),
            pltpu.VMEM((count, side, ch, 256), F32),
            pltpu.VMEM((count, 3 * cc, pairs * 128), F32),
            vmem(count, side, ch, 256),
            vmem(2, count, ch, 256),
            vmem(side * count * ch, 256),
            vmem(2 * DEPTH * count * ch, 256),
            vmem(count, 3, count, ch, 256),
            vmem(2, 2, count, count, ch, 256),
            vmem(count, 2, count, cc, 128),
            vmem(3, count, count, cc, 128),
            pltpu.SemaphoreType.DMA((3 + len(weights) + 1 + len(onehots),)),
            pltpu.SemaphoreType.DMA((4, 2)),
            pltpu.SemaphoreType.DMA((4, 2)),
            pltpu.SemaphoreType.DMA((n_group - 1,)),
            pltpu.SemaphoreType.DMA((n_group - 1,)),
        ],
        compiler_params=pltpu.CompilerParams(
            collective_id=0, has_side_effects=True, vmem_limit_bytes=48 << 20
        ),
    )(*[pltpu.with_memory_space_constraint(a, pltpu.HBM) for a in (neighbours, coarse_dest, features, *weights, *onehots)])
    return pl.pallas_call(
        finish_kernel,
        out_shape=(
            jax.ShapeDtypeStruct(features.shape, BF16),
            jax.ShapeDtypeStruct((n_group * SEND_CAP, cc, half**3), BF16),
        ),
        in_specs=[whole] * 4,
        out_specs=(anywhere,) * 2,
        scratch_shapes=[
            vmem(*features.shape),
            vmem(n_group * SEND_CAP, cc, half**3),
            pltpu.SemaphoreType.DMA((count + 1,)),
        ],
        compiler_params=pltpu.CompilerParams(vmem_limit_bytes=24 << 20),
    )(*[pltpu.with_memory_space_constraint(a, pltpu.VMEM) for a in middle])


def solution(mesh):
    slots = P(("group", "local"), None, None)
    return jax.shard_map(
        functools.partial(local, mesh.shape["local"], mesh.shape["group"]),
        mesh=mesh,
        in_specs=(slots, P(("group", "local"), None), P(("group", "local"))) + (P(),) * 10,
        out_specs=(slots, slots),
        check_vma=False,
    )
```

```python
import functools

import jax
import jax.numpy as jnp
import numpy as np
from jax import lax
from jax.experimental import pallas as pl
from jax.experimental.pallas import tpu as pltpu
from jax.sharding import PartitionSpec as P

SEND_CAP = 2
DEPTH = 2
HELD = 4
MESH = pl.DeviceIdType.MESH
F32 = jnp.float32
BF16 = jnp.bfloat16
I32 = jnp.int32


def iota(shape, dim):
    return lax.broadcasted_iota(I32, shape, dim)


def onehot(mask):
    return jnp.where(mask, 1.0, 0.0).astype(BF16)


def column(row):
    n = row.shape[1]
    wide = jnp.broadcast_to(row, (n, n))
    return jnp.sum(jnp.where(iota((n, n), 0) == iota((n, n), 1), wide, 0.0), axis=1, keepdims=True)


def silu(u):
    return u / (1.0 + jnp.exp(-u))


def shifted(v, s):
    if s == 0:
        return v
    return jnp.concatenate([v[:, s:], v[:, :s]], axis=1)


def dot(a, b):
    return jnp.dot(a, b, preferred_element_type=F32)


def taps(v, stride):
    return jnp.concatenate([shifted(v, q * stride + r) for q in range(3) for r in range(3)], axis=0)


def offset(v, top):
    return jnp.where(v == 0, -1, jnp.where(v == top, 1, 0))


def kernel(
    sizes,
    nb_hbm,
    dest_hbm,
    x_hbm,
    w1_hbm,
    b1_hbm,
    wr_hbm,
    br_hbm,
    wc_hbm,
    bc_hbm,
    wu_hbm,
    bu_hbm,
    w2_hbm,
    b2_hbm,
    t1_hbm,
    t2_hbm,
    tred_hbm,
    tup_hbm,
    tout_hbm,
    tbal_hbm,
    rows_ref,
    tout,
    tbal,
    bal_ref,
    nb,
    dest,
    nb_ref,
    x_ref,
    w1_ref,
    b1_ref,
    wr_ref,
    br_ref,
    wc_ref,
    bc_ref,
    wu_ref,
    bu_ref,
    w2_ref,
    b2_ref,
    sx,
    rx,
    sm,
    rm,
    sf,
    rf,
    sc,
    rc,
    sb,
    rb,
    t1,
    t2,
    tred,
    tup,
    w1,
    wc,
    w2f,
    w2u,
    lhs1,
    lhse,
    lhsr,
    y1,
    yf,
    y2,
    uf,
    yc,
    fst,
    fe,
    sel,
    sele,
    fm,
    fe_m,
    cm,
    ce_m,
    load_sem,
    send_sem,
    recv_sem,
    bal_send,
    bal_recv,
):
    side, count, ch, cc, n_local, n_group = sizes
    half = side // 2
    face = side * side
    planes = side + 2
    pairs = half // 2
    me = lax.axis_index("local")
    grp = lax.axis_index("group")
    right, left = lax.rem(me + 1, n_local), lax.rem(me + n_local - 1, n_local)
    ends = (left, right)
    has_left, has_right = me > 0, me < n_local - 1
    sends, receives = (has_left, has_right), (has_right, has_left)

    barrier = pltpu.get_barrier_semaphore()
    for d in (0, 1):

        @pl.when(sends[d])
        def _():
            pl.semaphore_signal(barrier, inc=1, device_id={"local": ends[d]}, device_id_type=MESH)

    for d in range(1, n_group):
        pl.semaphore_signal(
            barrier, inc=1, device_id={"group": lax.rem(grp + d, n_group)}, device_id_type=MESH
        )

    loads = {}
    pieces = (
        ("nbv", nb_hbm, nb_ref),
        ("x", x_hbm, x_ref),
        ("nb", nb_hbm, nb),
        ("dest", dest_hbm, dest),
        ("t1", t1_hbm, t1),
        ("w1", w1_hbm, w1_ref),
        ("b1", b1_hbm, b1_ref),
        ("tred", tred_hbm, tred),
        ("wr", wr_hbm, wr_ref),
        ("br", br_hbm, br_ref),
        ("t2", t2_hbm, t2),
        ("w2", w2_hbm, w2_ref),
        ("wc", wc_hbm, wc_ref),
        ("bc", bc_hbm, bc_ref),
        ("wu", wu_hbm, wu_ref),
        ("bu", bu_hbm, bu_ref),
        ("b2", b2_hbm, b2_ref),
        ("tup", tup_hbm, tup),
        ("tout", tout_hbm, tout),
        ("tbal", tbal_hbm, tbal),
    )
    for i, (name, src, dst) in enumerate(pieces):
        loads[name] = pltpu.make_async_copy(src, dst, load_sem.at[i])
        loads[name].start()

    for d in (0, 1):

        @pl.when(jnp.logical_not(receives[d]))
        def _():
            rx[d] = jnp.zeros(rx.shape[1:], BF16)
            rm[d] = jnp.zeros(rm.shape[1:], BF16)
            rf[d] = jnp.zeros(rf.shape[1:], BF16)
            rc[d] = jnp.zeros(rc.shape[1:], BF16)

    n = iota((1, 256), 1)
    ny, nz = n >> 4, n & 15
    n1 = iota((1, 128), 1)
    cy, cz = (n1 >> 3) & 7, n1 & 7
    low = n1 < 64
    fy, fz = offset(ny, side + 1), offset(nz, side + 1)
    gy, gz = offset(cy, half + 1), offset(cz, half + 1)

    direction = jnp.concatenate([(fy + 1) * 3 + fz + 1, (gy + 1) * 3 + gz + 1], axis=1)
    table = onehot(lax.rem(iota((27, 384), 0), 9) == direction)
    rows = sm.shape[0]
    first_live = 3 * count * count
    first_valid = first_live + count
    loads["nbv"].wait()
    row = iota((rows, 27), 0)
    entries = jnp.zeros((rows, 27), I32)
    for b in range(count):
        entries = jnp.where(lax.rem(row, count) == b, nb_ref[b : b + 1, :], entries)
    slot = lax.rem(lax.div(row, count), count)
    step_of = lax.div(row, count * count)
    chosen = onehot((entries == slot) & (lax.div(iota((rows, 27), 1), 9) == step_of) & (row < first_live))
    table_rows = dot(chosen, table)
    loads["nb"].wait()
    loads["dest"].wait()
    live = [jnp.where(nb[b, 13] >= 0, 1.0, 0.0) for b in range(count)]
    valid = [jnp.where(dest[b] >= 0, live[b], 0.0) for b in range(count)]
    wide_row = iota((rows, 384), 0)
    for b in range(count):
        table_rows = jnp.where(wide_row == first_live + b, live[b], table_rows)
        table_rows = jnp.where(wide_row == first_valid + b, valid[b], table_rows)
    sm[...] = table_rows.astype(BF16)

    loads["x"].wait()
    span = DEPTH * face
    for t in range(count):
        sx[0, t, :, 0:span] = x_ref[t, :, 0:span]
        sx[1, t, :, 0:span] = x_ref[t, :, side * face - span : side * face]
        tail = sx.shape[3] - span
        for d in (0, 1):
            sx[d, t, :, span:] = jnp.zeros((ch, tail), BF16)

    def remote(e, d, src, dst):
        return pltpu.make_async_remote_copy(
            src_ref=src,
            dst_ref=dst,
            send_sem=send_sem.at[e, d],
            recv_sem=recv_sem.at[e, d],
            device_id={"local": ends[d]},
            device_id_type=MESH,
        )

    def receive(copies):
        for d in (0, 1):
            pl.when(receives[d])(copies[d].wait_recv)

    def blend(parts, masks):
        total = parts[0] * masks[0]
        for t in range(1, count):
            total = total + parts[t] * masks[t]
        return total

    def mask_row(values, step, t, b):
        r = ((step + 1) * count + t) * count + b
        return values[r : r + 1, :]

    def convolve(store, weight, parts, masks, lo, hi):
        both = [taps(blend(parts, masks(b)), 16) for b in range(count)]
        y = dot(weight[lo * ch : hi * ch], jnp.concatenate(both, axis=1))
        for b in range(count):
            store(b, y[:, b * 256 : (b + 1) * 256])

    def into(dst, plane, lo=0, hi=3):
        def store(b, v):
            dst[b, plane, lo * ch : hi * ch] = v

        return store

    def split(a, base, size, n_parts=count):
        return [a[base + t * size : base + (t + 1) * size] for t in range(n_parts)]

    beside = jnp.where(has_left, 1, 0) + jnp.where(has_right, 1, 0)
    mask_copies = [remote(0, d, sm, rm.at[d]) for d in (0, 1)]
    face_copies = [remote(1, d, sx.at[d], rx.at[d]) for d in (0, 1)]

    own = sm[...].astype(F32)
    for b in range(count):
        for t in range(count):
            for s in range(3):
                m = mask_row(own, s - 1, t, b)[:, 0:256]
                fm[b, s, t] = jnp.broadcast_to(m, (ch, 256)).astype(BF16)
    def greet(mine):
        @pl.when(mine)
        def _():
            pl.semaphore_wait(barrier, beside + n_group - 1)

        for copies in (mask_copies, face_copies):
            for d in (0, 1):
                pl.when(mine & sends[d])(copies[d].start)

    greet(has_left)
    for t in range(count):
        for x in range(side):
            lhs1[(x * count + t) * ch : (x * count + t + 1) * ch, 0:face] = x_ref[
                t, :, x * face : (x + 1) * face
            ]
    loads["w1"].wait()
    for p in range(3):
        w1[p * ch : (p + 1) * ch] = w1_ref[:, p * 9 * ch : (p + 1) * 9 * ch]
    loads["t1"].wait()
    sel[...] = dot(lhs1[:, 0:face], t1[...]).astype(BF16)
    first_planes = [x for x in range(side) if x < 5 or x > side - 6]
    for x in first_planes:
        if x == 5 - 1:
            greet(jnp.logical_not(has_left))
        convolve(into(y1, x + 1), w1, split(sel, x * count * ch, ch), lambda b: fm.at[b, 1], 0, 3)
    loads["b1"].wait()
    b1 = column(b1_ref[...])

    def first_plane(b, x):
        u = y1[b, x, 0:ch] + y1[b, x + 1, ch : 2 * ch] + y1[b, x + 2, 2 * ch : 3 * ch] + b1
        fst[b, x] = (live[b] * silu(u)).astype(BF16)

    for b in range(count):
        for x in (1, 2, 3, side - 4, side - 3, side - 2):
            first_plane(b, x)

    loads["tred"].wait()
    loads["wr"].wait()
    loads["br"].wait()
    br = column(br_ref[...])

    def reduce_units(base, units):
        for i, (low_of, high_of, _) in enumerate(units):
            for p in (0, 1):
                r0 = ((base + i) * 2 + p) * ch
                lhsr[r0 : r0 + ch, 0:256] = low_of(p)
                lhsr[r0 : r0 + ch, 256:512] = high_of(p)
        start, size = base * 2 * ch, len(units) * 2 * ch
        a = dot(lhsr[start : start + size], tred[...]).astype(BF16)
        stacked = [
            jnp.concatenate(
                [
                    a[(i * 2 + p) * ch : (i * 2 + p + 1) * ch, k * 128 : (k + 1) * 128]
                    for p in (0, 1)
                    for k in range(4)
                ],
                axis=0,
            )
            for i in range(len(units))
        ]
        v = dot(wr_ref[...], jnp.concatenate(stacked, axis=1)) + br
        return [(keep * silu(v[:, i * 128 : (i + 1) * 128])).astype(BF16) for i, (_, _, keep) in enumerate(units)]

    def own_unit(t, lower, upper):
        return (lambda p: fst[t, 2 * lower + p]), (lambda p: fst[t, 2 * upper + p]), live[t]

    inner = reduce_units(0, [own_unit(t, half - 2, 1) for t in range(count)])
    for t in range(count):
        sc[t] = inner[t]
        sf[0, t] = fst[t, 1]
        sf[1, t] = fst[t, side - 2]
    first_copies = [remote(2, d, sf.at[d], rf.at[d]) for d in (0, 1)]
    coarse_copies = [remote(3, d, sc, rc.at[d]) for d in (0, 1)]
    for copies in (coarse_copies, first_copies):
        for d in (0, 1):
            pl.when(sends[d])(copies[d].start)

    for x in range(side):
        if x not in first_planes:
            convolve(into(y1, x + 1), w1, split(sel, x * count * ch, ch), lambda b: fm.at[b, 1], 0, 3)
    for b in range(count):
        for x in range(4, side - 4):
            first_plane(b, x)
    middles = [own_unit(t, 2 * j, 2 * j + 1) for j in range(1, pairs - 1) for t in range(count)]
    inner += reduce_units(count, middles)

    loads["b2"].wait()
    b2 = column(b2_ref[...])

    def biased(plane):
        def store(b, v):
            yf[b, plane, 0:ch] = v[0:ch]
            yf[b, plane, ch : 2 * ch] = v[ch : 2 * ch] + b2
            yf[b, plane, 2 * ch :] = v[2 * ch :]

        return store

    loads["t2"].wait()
    loads["w2"].wait()
    for p in range(3):
        for part, dst in ((0, w2f), (1, w2u)):
            dst[p * ch : (p + 1) * ch] = jnp.concatenate(
                [
                    w2_ref[:, ((9 * p + k) * 2 + part) * ch : ((9 * p + k) * 2 + part + 1) * ch]
                    for k in range(9)
                ],
                axis=1,
            )
    for x in range(1, side - 1):
        for t in range(count):
            lhs1[(x * count + t) * ch : (x * count + t + 1) * ch, 256:512] = fst[t, x]
    lo, hi = count * ch, (side - 1) * count * ch
    self_ = dot(lhs1[lo:hi, 256:512], t2[...]).astype(BF16)
    for x in range(1, side - 1):
        convolve(biased(x + 1), w2f, split(self_, (x - 1) * count * ch, ch), lambda b: fm.at[b, 1], 0, 3)

    for name in ("wc", "bc", "wu", "bu", "tup", "tout", "tbal"):
        loads[name].wait()
    for p in range(3):
        wc[p * cc : (p + 1) * cc] = wc_ref[:, p * 9 * cc : (p + 1) * 9 * cc]
    bc, bu = column(bc_ref[...]), column(bu_ref[...])
    for b in range(count):
        for t in range(count):
            m = mask_row(own, 0, t, b)[:, 256:384]
            cm[b, 0, t] = jnp.broadcast_to(m, (cc, 128)).astype(BF16)
            m = jnp.where(low, mask_row(own, 1, t, b)[:, 256:384], mask_row(own, -1, t, b)[:, 256:384])
            cm[b, 1, t] = jnp.broadcast_to(m, (cc, 128)).astype(BF16)

    receive(mask_copies)
    far = [rm[d].astype(F32) for d in (0, 1)]
    cross = (-1, 1)
    for b in range(count):
        for t in range(count):
            for d in (0, 1):
                for i, s in enumerate((0, cross[d])):
                    m = mask_row(far[d], s, t, b)
                    fe_m[d, i, b, t] = jnp.broadcast_to(m[:, 0:256], (ch, 256)).astype(BF16)
            from_r, from_l = mask_row(far[0], 0, t, b), mask_row(far[1], 0, t, b)
            mixed = (
                (from_l, mask_row(far[0], -1, t, b)),
                (from_r, from_l),
                (mask_row(far[1], 1, t, b), from_r),
            )
            for i, (lower, upper) in enumerate(mixed):
                m = jnp.where(low, lower[:, 256:384], upper[:, 256:384])
                ce_m[i, b, t] = jnp.broadcast_to(m, (cc, 128)).astype(BF16)
    far_live = [[far[d][first_live + b : first_live + b + 1, :] for b in range(count)] for d in (0, 1)]
    far_valid = [[far[d][first_valid + b : first_valid + b + 1, :] for b in range(count)] for d in (0, 1)]

    receive(face_copies)
    for d in (0, 1):
        for k in range(DEPTH):
            for t in range(count):
                r0 = ((d * DEPTH + k) * count + t) * ch
                lhse[r0 : r0 + ch, 0:face] = rx[d, t, :, k * face : (k + 1) * face]
    sele[...] = dot(lhse[:, 0:face], t1[...]).astype(BF16)

    def far_parts(d, k):
        return split(sele, (d * DEPTH + k) * count * ch, ch)

    convolve(into(y1, 0, 0, 1), w1, far_parts(1, DEPTH - 1), lambda b: fm.at[b, 0], 0, 1)
    convolve(into(y1, side + 1, 2, 3), w1, far_parts(0, 0), lambda b: fm.at[b, 2], 2, 3)
    for b in range(count):
        first_plane(b, 0)
        first_plane(b, side - 1)
    near = ((split(sel, (side - 1) * count * ch, ch), 1), (split(sel, 0, ch), 1))
    stacks = (
        (near[0], (far_parts(0, 0), 0), (far_parts(0, 1), 0)),
        ((far_parts(1, 0), 0), (far_parts(1, 1), 0), near[1]),
    )
    for d in (0, 1):
        deep = jnp.concatenate(
            [
                jnp.concatenate([taps(blend(parts, fe_m.at[d, i, b]), 16) for b in range(count)], axis=1)
                for parts, i in stacks[d]
            ],
            axis=0,
        )
        u = dot(w1_ref[...], deep) + b1
        for b in range(count):
            v = silu(u[:, b * 256 : (b + 1) * 256])
            fe[d, b] = (far_live[d][b][:, 0:256] * v).astype(BF16)

    sources = [[fe[1, t] for t in range(count)], [fst[t, 0] for t in range(count)]]
    sources += [[fst[t, side - 1] for t in range(count)], [fe[0, t] for t in range(count)]]
    selo = dot(jnp.concatenate([v for s in sources for v in s], axis=0), t2[...]).astype(BF16)
    convolve(into(yf, 0, 0, 1), w2f, split(selo, 0, ch), lambda b: fm.at[b, 0], 0, 1)
    convolve(biased(1), w2f, split(selo, count * ch, ch), lambda b: fm.at[b, 1], 0, 3)
    convolve(biased(side), w2f, split(selo, 2 * count * ch, ch), lambda b: fm.at[b, 1], 0, 3)
    convolve(into(yf, side + 1, 2, 3), w2f, split(selo, 3 * count * ch, ch), lambda b: fm.at[b, 2], 2, 3)

    for b in range(count):
        for x in range(side):
            uf[b, x] = yf[b, x, 0:ch] + yf[b, x + 1, ch : 2 * ch] + yf[b, x + 2, 2 * ch :]

    ends_ = reduce_units(len(inner), [own_unit(t, 0, half - 1) for t in range(count)])

    def pick(a, b):
        return jnp.where(low, a.astype(F32), b.astype(F32)).astype(BF16)

    shared, middle = inner[0:count], inner[count:]
    middle = [middle[j * count : (j + 1) * count] for j in range(pairs - 2)]
    bottom = [pick(ends_[t], shared[t]) for t in range(count)]
    top = [pick(shared[t], ends_[t]) for t in range(count)]
    for b in range(count):
        padded = [blend(v, cm.at[b, 0]) for v in [bottom] + middle + [top]]
        yc[b] = dot(wc[...], jnp.concatenate([taps(v, 8) for v in padded], axis=1))

    receive(coarse_copies)
    receive(first_copies)

    def far_unit(t):
        r = (fe[0, t], rf[0, t])
        l = (rf[1, t], fe[1, t])
        keep = jnp.where(low, far_live[0][t][:, 256:384], far_live[1][t][:, 256:384])
        return (lambda p: r[p]), (lambda p: l[p]), keep

    rim = reduce_units(len(inner) + count, [far_unit(t) for t in range(count)])
    from_right, from_left = [[rc[d, t] for t in range(count)] for d in (0, 1)]

    y_rim = dot(wc[...], jnp.concatenate([taps(blend(rim, cm.at[b, 1]), 8) for b in range(count)], axis=1))
    coarse = []
    ups = []
    for b in range(count):
        y = jnp.concatenate([yc[b], y_rim[:, b * 128 : (b + 1) * 128]], axis=1)
        width = y.shape[1]
        u = pltpu.roll(y[0:cc], 64, 1) + y[cc : 2 * cc] + pltpu.roll(y[2 * cc :], width - 64, 1) + bc
        coarse.append((valid[b] * silu(u[:, 0 : 64 * half])).astype(BF16))

    def outgoing(r, k):
        total = jnp.zeros(coarse[0].shape, F32)
        for b in range(count):
            total = total + coarse[b].astype(F32) * jnp.where(dest[b] == r * SEND_CAP + k, valid[b], 0.0)
        return total.astype(BF16)

    sent = []
    for d in range(1, n_group):
        other = lax.rem(grp + d, n_group)
        for k in range(SEND_CAP):
            sb[d - 1, k] = outgoing(other, k)
        c = pltpu.make_async_remote_copy(
            src_ref=sb.at[d - 1],
            dst_ref=rb.at[d - 1],
            send_sem=bal_send.at[d - 1],
            recv_sem=bal_recv.at[d - 1],
            device_id={"group": other},
            device_id_type=MESH,
        )
        c.start()
        sent.append(c)
    for k in range(SEND_CAP):
        bal_ref[grp * SEND_CAP + k] = outgoing(grp, k)

    for b in range(count):
        v = (live[b] * (dot(wu_ref[...], coarse[b]) + bu)).astype(BF16)
        ups.append([v[:, j * 128 : (j + 1) * 128] for j in range(pairs)])

    below = [pick(from_left[t], ends_[t]) for t in range(count)]
    above = [pick(ends_[t], from_right[t]) for t in range(count)]
    zs = [[blend(v, ce_m.at[i, b]) for b in range(count)] for i, v in enumerate((below, rim, above))]
    zs[1] = [shifted(v, 64) for v in zs[1]]
    deep = jnp.concatenate([taps(jnp.concatenate(z, axis=1), 8) for z in zs], axis=0)
    u = dot(wc_ref[...], deep) + bc
    keep = jnp.concatenate(
        [jnp.where(low, far_valid[1][b][:, 256:384], far_valid[0][b][:, 256:384]) for b in range(count)], axis=1
    )
    co = (keep * silu(u)).astype(BF16)
    keep = jnp.concatenate(
        [jnp.where(low, far_live[1][b][:, 256:384], far_live[0][b][:, 256:384]) for b in range(count)], axis=1
    )
    v = (keep * (dot(wu_ref[...], co) + bu)).astype(BF16)
    for b in range(count):
        ups[b].append(v[:, b * 128 : (b + 1) * 128])

    wide = jnp.concatenate([ups[t][j] for j in range(pairs + 1) for t in range(count)], axis=0)
    selu = dot(wide, tup[...]).astype(BF16)
    for j in range(pairs + 1):
        for h in (0, 1):
            parts = [v[:, h * 256 : (h + 1) * 256] for v in split(selu, j * count * ch, ch)]
            if j < pairs:
                convolve(into(y2, 1 + 2 * j + h), w2u, parts, lambda b: fm.at[b, 1], 0, 3)
            elif h == 0:
                convolve(into(y2, 0, 0, 1), w2u, parts, lambda b: fm.at[b, 0], 0, 1)
            else:
                convolve(into(y2, half + 1, 2, 3), w2u, parts, lambda b: fm.at[b, 2], 2, 3)

    for b in range(count):
        for x in range(side):
            u = uf[b, x]
            for p in range(3):
                u = u + y2[b, (x + p + 1) // 2, p * ch : (p + 1) * ch]
            rows_ref[b, x * ch : (x + 1) * ch] = (live[b] * silu(u)).astype(BF16)

    for copies in (mask_copies, face_copies, coarse_copies, first_copies):
        for d in (0, 1):
            pl.when(sends[d])(copies[d].wait_send)
    for d, c in enumerate(sent):
        c.wait()
        source = lax.rem(grp + n_group - (d + 1), n_group)
        for k in range(SEND_CAP):
            bal_ref[source * SEND_CAP + k] = rb[d, k]


def finish_kernel(rows_ref, tout, tbal, bal_ref, out_hbm, bal_hbm, out, bal, sems):
    count, ch = out.shape[:2]
    face = tout.shape[1]
    side = out.shape[2] // face
    copies = []
    for b in range(count):
        flat = dot(rows_ref[b], tout[...])
        for x in range(side):
            out[b, :, x * face : (x + 1) * face] = flat[x * ch : (x + 1) * ch].astype(BF16)
        copies.append(pltpu.make_async_copy(out.at[b], out_hbm.at[b], sems.at[b]))
        copies[-1].start()
    slots, cc = bal_ref.shape[0], bal_ref.shape[1]
    dense = dot(jnp.concatenate([bal_ref[k] for k in range(slots)], axis=0), tbal[...])
    for k in range(slots):
        bal[k] = dense[k * cc : (k + 1) * cc].astype(BF16)
    copies.append(pltpu.make_async_copy(bal, bal_hbm, sems.at[count]))
    copies[-1].start()
    for c in copies:
        c.wait()


def tables(side):
    half = side // 2
    face = side * side

    def hot(rows, target):
        return (np.arange(rows)[:, None] == target[None, :]).astype(BF16)

    def wrap(v, n):
        return np.where(v == 0, n - 1, np.where(v == n + 1, 0, v - 1))

    n = np.arange(256)
    ny, nz = n >> 4, n & 15
    inside = (ny < side + 2) & (nz < side + 2)
    t1 = hot(face, np.where(inside, wrap(ny, side) * side + wrap(nz, side), -1))
    t2 = hot(256, np.where(inside, wrap(ny, side) * 16 + wrap(nz, side), -1))
    n2 = np.arange(512)
    ry, rz = (n2 >> 3) & 7, n2 & 7
    target = ((n2 >> 6) & 1) * 256 + (2 * wrap(ry, half) + ((n2 >> 8) & 1)) * 16 + 2 * wrap(rz, half) + ((n2 >> 7) & 1)
    tred = hot(512, np.where((ry < half + 2) & (rz < half + 2), target, -1))
    uy, uz = (n2 >> 4) & 15, n2 & 15
    target = (n2 >> 8) * 64 + (wrap(uy, side) >> 1) * 8 + (wrap(uz, side) >> 1)
    tup = hot(128, np.where((uy < side + 2) & (uz < side + 2), target, -1))
    tout = hot(face, np.where((ny < side) & (nz < side), ny * side + nz, -1)).T
    k = np.arange(64 * half)
    kx, ky, kz = k >> 6, (k >> 3) & 7, k & 7
    tbal = hot(half**3, np.where((ky < half) & (kz < half), (kx * half + ky) * half + kz, -1)).T
    return [jnp.asarray(t) for t in (t1, t2, tred, tup, tout, tbal)]


def local(n_local, n_group, features, neighbours, coarse_dest, *weights):
    count, ch, cells = features.shape
    side = round(cells ** (1 / 3))
    cc = weights[2].shape[0]
    half, face = side // 2, side * side
    pairs = half // 2
    rows = (3 * count * count + 2 * count + 15) // 16 * 16
    span = (DEPTH * face + 127) // 128 * 128
    if side + 2 > 16 or half + 2 > 8 or half % 2 or side**3 != cells or pairs < 2:
        raise ValueError("side")
    vmem = lambda *shape: pltpu.VMEM(shape, BF16)
    weights = [w.reshape(1, -1) if w.ndim == 1 else w for w in weights]
    onehots = tables(side)
    anywhere = pl.BlockSpec(memory_space=pl.ANY)
    whole = pl.BlockSpec(memory_space=pltpu.VMEM)
    units = (pairs - 1) * count
    middle = pl.pallas_call(
        functools.partial(kernel, (side, count, ch, cc, n_local, n_group)),
        out_shape=(
            vmem(count, side * ch, 256),
            vmem(256, face),
            vmem(64 * half, half**3),
            vmem(n_group * SEND_CAP, cc, 64 * half),
        ),
        in_specs=[anywhere] * (3 + len(weights) + len(onehots)),
        out_specs=(whole,) * 4,
        scratch_shapes=[
            pltpu.SMEM(neighbours.shape, I32),
            pltpu.SMEM(coarse_dest.shape, I32),
            pltpu.VMEM(neighbours.shape, I32),
            vmem(*features.shape),
        ]
        + [pltpu.VMEM(w.shape, w.dtype) for w in weights]
        + [
            vmem(2, count, ch, span),
            vmem(2, count, ch, span),
            vmem(rows, 384),
            vmem(2, rows, 384),
            vmem(2, count, ch, 256),
            vmem(2, count, ch, 256),
            vmem(count, cc, 128),
            vmem(2, count, cc, 128),
            vmem(n_group - 1, SEND_CAP, cc, 64 * half),
            vmem(n_group - 1, SEND_CAP, cc, 64 * half),
            vmem(face, 256),
            vmem(256, 256),
            vmem(512, 512),
            vmem(128, 512),
            vmem(3 * ch, 9 * ch),
            vmem(3 * cc, 9 * cc),
            vmem(3 * ch, 9 * ch),
            vmem(3 * ch, 9 * ch),
            vmem(side * count * ch, 512),
            vmem(2 * DEPTH * count * ch, 256),
            vmem((units + 2 * count) * 2 * ch, 512),
            pltpu.VMEM((count, side + 2, 3 * ch, 256), F32),
            pltpu.VMEM((count, side + 2, 3 * ch, 256), F32),
            pltpu.VMEM((count, half + 2, 3 * ch, 256), F32),
            pltpu.VMEM((count, side, ch, 256), F32),
            pltpu.VMEM((count, 3 * cc, pairs * 128), F32),
            vmem(count, side, ch, 256),
            vmem(2, count, ch, 256),
            vmem(side * count * ch, 256),
            vmem(2 * DEPTH * count * ch, 256),
            vmem(count, 3, count, ch, 256),
            vmem(2, 2, count, count, ch, 256),
            vmem(count, 2, count, cc, 128),
            vmem(3, count, count, cc, 128),
            pltpu.SemaphoreType.DMA((3 + len(weights) + 1 + len(onehots),)),
            pltpu.SemaphoreType.DMA((4, 2)),
            pltpu.SemaphoreType.DMA((4, 2)),
            pltpu.SemaphoreType.DMA((n_group - 1,)),
            pltpu.SemaphoreType.DMA((n_group - 1,)),
        ],
        compiler_params=pltpu.CompilerParams(
            collective_id=0, has_side_effects=True, vmem_limit_bytes=48 << 20
        ),
    )(*[pltpu.with_memory_space_constraint(a, pltpu.HBM) for a in (neighbours, coarse_dest, features, *weights, *onehots)])
    return pl.pallas_call(
        finish_kernel,
        out_shape=(
            jax.ShapeDtypeStruct(features.shape, BF16),
            jax.ShapeDtypeStruct((n_group * SEND_CAP, cc, half**3), BF16),
        ),
        in_specs=[whole] * 4,
        out_specs=(anywhere,) * 2,
        scratch_shapes=[
            vmem(*features.shape),
            vmem(n_group * SEND_CAP, cc, half**3),
            pltpu.SemaphoreType.DMA((count + 1,)),
        ],
        compiler_params=pltpu.CompilerParams(vmem_limit_bytes=24 << 20),
    )(*[pltpu.with_memory_space_constraint(a, pltpu.VMEM) for a in middle])


def solution(mesh):
    slots = P(("group", "local"), None, None)
    return jax.shard_map(
        functools.partial(local, mesh.shape["local"], mesh.shape["group"]),
        mesh=mesh,
        in_specs=(slots, P(("group", "local"), None), P(("group", "local"))) + (P(),) * 10,
        out_specs=(slots, slots),
        check_vma=False,
    )
```

```python
import functools

import jax
import jax.numpy as jnp
import numpy as np
from jax import lax
from jax.experimental import pallas as pl
from jax.experimental.pallas import tpu as pltpu
from jax.sharding import PartitionSpec as P

SEND_CAP = 2
DEPTH = 2
HELD = 4
MESH = pl.DeviceIdType.MESH
F32 = jnp.float32
BF16 = jnp.bfloat16
I32 = jnp.int32


def iota(shape, dim):
    return lax.broadcasted_iota(I32, shape, dim)


def onehot(mask):
    return jnp.where(mask, 1.0, 0.0).astype(BF16)


def column(row):
    n = row.shape[1]
    wide = jnp.broadcast_to(row, (n, n))
    return jnp.sum(jnp.where(iota((n, n), 0) == iota((n, n), 1), wide, 0.0), axis=1, keepdims=True)


def silu(u):
    return u / (1.0 + jnp.exp(-u))


def shifted(v, s):
    if s == 0:
        return v
    return jnp.concatenate([v[:, s:], v[:, :s]], axis=1)


def dot(a, b):
    return jnp.dot(a, b, preferred_element_type=F32)


def taps(v, stride):
    return jnp.concatenate([shifted(v, q * stride + r) for q in range(3) for r in range(3)], axis=0)


def offset(v, top):
    return jnp.where(v == 0, -1, jnp.where(v == top, 1, 0))


def kernel(
    sizes,
    nb_hbm,
    dest_hbm,
    x_hbm,
    w1_hbm,
    b1_hbm,
    wr_hbm,
    br_hbm,
    wc_hbm,
    bc_hbm,
    wu_hbm,
    bu_hbm,
    w2_hbm,
    b2_hbm,
    t1_hbm,
    t2_hbm,
    tred_hbm,
    tup_hbm,
    tout_hbm,
    tbal_hbm,
    rows_ref,
    tout,
    tbal,
    bal_ref,
    nb,
    dest,
    nb_ref,
    x_ref,
    w1_ref,
    b1_ref,
    wr_ref,
    br_ref,
    wc_ref,
    bc_ref,
    wu_ref,
    bu_ref,
    w2_ref,
    b2_ref,
    sx,
    rx,
    sm,
    rm,
    sf,
    rf,
    sc,
    rc,
    sb,
    rb,
    t1,
    t2,
    tred,
    tup,
    w1,
    wc,
    w2f,
    w2u,
    lhs1,
    lhse,
    lhsr,
    y1,
    yf,
    y2,
    uf,
    yc,
    fst,
    fe,
    sel,
    sele,
    fm,
    fe_m,
    cm,
    ce_m,
    load_sem,
    send_sem,
    recv_sem,
    bal_send,
    bal_recv,
):
    side, count, ch, cc, n_local, n_group = sizes
    half = side // 2
    face = side * side
    planes = side + 2
    pairs = half // 2
    me = lax.axis_index("local")
    grp = lax.axis_index("group")
    right, left = lax.rem(me + 1, n_local), lax.rem(me + n_local - 1, n_local)
    ends = (left, right)
    has_left, has_right = me > 0, me < n_local - 1
    sends, receives = (has_left, has_right), (has_right, has_left)

    barrier = pltpu.get_barrier_semaphore()
    for d in (0, 1):

        @pl.when(sends[d])
        def _():
            pl.semaphore_signal(barrier, inc=1, device_id={"local": ends[d]}, device_id_type=MESH)

    for d in range(1, n_group):
        pl.semaphore_signal(
            barrier, inc=1, device_id={"group": lax.rem(grp + d, n_group)}, device_id_type=MESH
        )

    loads = {}
    pieces = (
        ("nbv", nb_hbm, nb_ref),
        ("x", x_hbm, x_ref),
        ("nb", nb_hbm, nb),
        ("dest", dest_hbm, dest),
        ("t1", t1_hbm, t1),
        ("w1", w1_hbm, w1_ref),
        ("b1", b1_hbm, b1_ref),
        ("tred", tred_hbm, tred),
        ("wr", wr_hbm, wr_ref),
        ("br", br_hbm, br_ref),
        ("t2", t2_hbm, t2),
        ("w2", w2_hbm, w2_ref),
        ("wc", wc_hbm, wc_ref),
        ("bc", bc_hbm, bc_ref),
        ("wu", wu_hbm, wu_ref),
        ("bu", bu_hbm, bu_ref),
        ("b2", b2_hbm, b2_ref),
        ("tup", tup_hbm, tup),
        ("tout", tout_hbm, tout),
        ("tbal", tbal_hbm, tbal),
    )
    for i, (name, src, dst) in enumerate(pieces):
        loads[name] = pltpu.make_async_copy(src, dst, load_sem.at[i])
    urgent = ("nbv", "x", "nb", "dest", "t1", "w1", "b1")
    for name in urgent:
        loads[name].start()

    for d in (0, 1):

        @pl.when(jnp.logical_not(receives[d]))
        def _():
            rx[d] = jnp.zeros(rx.shape[1:], BF16)
            rm[d] = jnp.zeros(rm.shape[1:], BF16)
            rf[d] = jnp.zeros(rf.shape[1:], BF16)
            rc[d] = jnp.zeros(rc.shape[1:], BF16)

    n = iota((1, 256), 1)
    ny, nz = n >> 4, n & 15
    n1 = iota((1, 128), 1)
    cy, cz = (n1 >> 3) & 7, n1 & 7
    low = n1 < 64
    fy, fz = offset(ny, side + 1), offset(nz, side + 1)
    gy, gz = offset(cy, half + 1), offset(cz, half + 1)

    direction = jnp.concatenate([(fy + 1) * 3 + fz + 1, (gy + 1) * 3 + gz + 1], axis=1)
    table = onehot(lax.rem(iota((27, 384), 0), 9) == direction)
    rows = sm.shape[0]
    first_live = 3 * count * count
    first_valid = first_live + count
    loads["nbv"].wait()
    row = iota((rows, 27), 0)
    entries = jnp.zeros((rows, 27), I32)
    for b in range(count):
        entries = jnp.where(lax.rem(row, count) == b, nb_ref[b : b + 1, :], entries)
    slot = lax.rem(lax.div(row, count), count)
    step_of = lax.div(row, count * count)
    chosen = onehot((entries == slot) & (lax.div(iota((rows, 27), 1), 9) == step_of) & (row < first_live))
    table_rows = dot(chosen, table)
    loads["nb"].wait()
    loads["dest"].wait()
    live = [jnp.where(nb[b, 13] >= 0, 1.0, 0.0) for b in range(count)]
    valid = [jnp.where(dest[b] >= 0, live[b], 0.0) for b in range(count)]
    wide_row = iota((rows, 384), 0)
    for b in range(count):
        table_rows = jnp.where(wide_row == first_live + b, live[b], table_rows)
        table_rows = jnp.where(wide_row == first_valid + b, valid[b], table_rows)
    sm[...] = table_rows.astype(BF16)

    loads["x"].wait()
    span = DEPTH * face
    for t in range(count):
        sx[0, t, :, 0:span] = x_ref[t, :, 0:span]
        sx[1, t, :, 0:span] = x_ref[t, :, side * face - span : side * face]
        tail = sx.shape[3] - span
        for d in (0, 1):
            sx[d, t, :, span:] = jnp.zeros((ch, tail), BF16)

    def remote(e, d, src, dst):
        return pltpu.make_async_remote_copy(
            src_ref=src,
            dst_ref=dst,
            send_sem=send_sem.at[e, d],
            recv_sem=recv_sem.at[e, d],
            device_id={"local": ends[d]},
            device_id_type=MESH,
        )

    def receive(copies):
        for d in (0, 1):
            pl.when(receives[d])(copies[d].wait_recv)

    def blend(parts, masks):
        total = parts[0] * masks[0]
        for t in range(1, count):
            total = total + parts[t] * masks[t]
        return total

    def mask_row(values, step, t, b):
        r = ((step + 1) * count + t) * count + b
        return values[r : r + 1, :]

    def convolve(store, weight, parts, masks, lo, hi):
        both = [taps(blend(parts, masks(b)), 16) for b in range(count)]
        y = dot(weight[lo * ch : hi * ch], jnp.concatenate(both, axis=1))
        for b in range(count):
            store(b, y[:, b * 256 : (b + 1) * 256])

    def into(dst, plane, lo=0, hi=3):
        def store(b, v):
            dst[b, plane, lo * ch : hi * ch] = v

        return store

    def split(a, base, size, n_parts=count):
        return [a[base + t * size : base + (t + 1) * size] for t in range(n_parts)]

    beside = jnp.where(has_left, 1, 0) + jnp.where(has_right, 1, 0)
    mask_copies = [remote(0, d, sm, rm.at[d]) for d in (0, 1)]
    face_copies = [remote(1, d, sx.at[d], rx.at[d]) for d in (0, 1)]

    own = sm[...].astype(F32)
    for b in range(count):
        for t in range(count):
            for s in range(3):
                m = mask_row(own, s - 1, t, b)[:, 0:256]
                fm[b, s, t] = jnp.broadcast_to(m, (ch, 256)).astype(BF16)
    def greet(mine):
        @pl.when(mine)
        def _():
            pl.semaphore_wait(barrier, beside + n_group - 1)

        for copies in (mask_copies, face_copies):
            for d in (0, 1):
                pl.when(mine & sends[d])(copies[d].start)

    greet(has_left)
    for name in loads:
        if name not in urgent:
            loads[name].start()
    for t in range(count):
        for x in range(side):
            lhs1[(x * count + t) * ch : (x * count + t + 1) * ch, 0:face] = x_ref[
                t, :, x * face : (x + 1) * face
            ]
    loads["w1"].wait()
    for p in range(3):
        w1[p * ch : (p + 1) * ch] = w1_ref[:, p * 9 * ch : (p + 1) * 9 * ch]
    loads["t1"].wait()
    sel[...] = dot(lhs1[:, 0:face], t1[...]).astype(BF16)
    first_planes = [x for x in range(side) if x < 5 or x > side - 6]
    for x in first_planes:
        if x == 3:
            greet(jnp.logical_not(has_left))
        convolve(into(y1, x + 1), w1, split(sel, x * count * ch, ch), lambda b: fm.at[b, 1], 0, 3)
    loads["b1"].wait()
    b1 = column(b1_ref[...])

    def first_plane(b, x):
        u = y1[b, x, 0:ch] + y1[b, x + 1, ch : 2 * ch] + y1[b, x + 2, 2 * ch : 3 * ch] + b1
        fst[b, x] = (live[b] * silu(u)).astype(BF16)

    for b in range(count):
        for x in (1, 2, 3, side - 4, side - 3, side - 2):
            first_plane(b, x)

    loads["tred"].wait()
    loads["wr"].wait()
    loads["br"].wait()
    br = column(br_ref[...])

    def reduce_units(base, units):
        for i, (low_of, high_of, _) in enumerate(units):
            for p in (0, 1):
                r0 = ((base + i) * 2 + p) * ch
                lhsr[r0 : r0 + ch, 0:256] = low_of(p)
                lhsr[r0 : r0 + ch, 256:512] = high_of(p)
        start, size = base * 2 * ch, len(units) * 2 * ch
        a = dot(lhsr[start : start + size], tred[...]).astype(BF16)
        stacked = [
            jnp.concatenate(
                [
                    a[(i * 2 + p) * ch : (i * 2 + p + 1) * ch, k * 128 : (k + 1) * 128]
                    for p in (0, 1)
                    for k in range(4)
                ],
                axis=0,
            )
            for i in range(len(units))
        ]
        v = dot(wr_ref[...], jnp.concatenate(stacked, axis=1)) + br
        return [(keep * silu(v[:, i * 128 : (i + 1) * 128])).astype(BF16) for i, (_, _, keep) in enumerate(units)]

    def own_unit(t, lower, upper):
        return (lambda p: fst[t, 2 * lower + p]), (lambda p: fst[t, 2 * upper + p]), live[t]

    inner = reduce_units(0, [own_unit(t, half - 2, 1) for t in range(count)])
    for t in range(count):
        sc[t] = inner[t]
        sf[0, t] = fst[t, 1]
        sf[1, t] = fst[t, side - 2]
    first_copies = [remote(2, d, sf.at[d], rf.at[d]) for d in (0, 1)]
    coarse_copies = [remote(3, d, sc, rc.at[d]) for d in (0, 1)]
    for copies in (coarse_copies, first_copies):
        for d in (0, 1):
            pl.when(sends[d])(copies[d].start)

    for x in range(side):
        if x not in first_planes:
            convolve(into(y1, x + 1), w1, split(sel, x * count * ch, ch), lambda b: fm.at[b, 1], 0, 3)
    for b in range(count):
        for x in range(4, side - 4):
            first_plane(b, x)
    middles = [own_unit(t, 2 * j, 2 * j + 1) for j in range(1, pairs - 1) for t in range(count)]
    inner += reduce_units(count, middles)

    loads["b2"].wait()
    b2 = column(b2_ref[...])

    def biased(plane):
        def store(b, v):
            yf[b, plane, 0:ch] = v[0:ch]
            yf[b, plane, ch : 2 * ch] = v[ch : 2 * ch] + b2
            yf[b, plane, 2 * ch :] = v[2 * ch :]

        return store

    loads["t2"].wait()
    loads["w2"].wait()
    for p in range(3):
        for part, dst in ((0, w2f), (1, w2u)):
            dst[p * ch : (p + 1) * ch] = jnp.concatenate(
                [
                    w2_ref[:, ((9 * p + k) * 2 + part) * ch : ((9 * p + k) * 2 + part + 1) * ch]
                    for k in range(9)
                ],
                axis=1,
            )
    for x in range(1, side - 1):
        for t in range(count):
            lhs1[(x * count + t) * ch : (x * count + t + 1) * ch, 256:512] = fst[t, x]
    lo, hi = count * ch, (side - 1) * count * ch
    self_ = dot(lhs1[lo:hi, 256:512], t2[...]).astype(BF16)
    for x in range(1, side - 1):
        convolve(biased(x + 1), w2f, split(self_, (x - 1) * count * ch, ch), lambda b: fm.at[b, 1], 0, 3)

    for name in ("wc", "bc", "wu", "bu", "tup", "tout", "tbal"):
        loads[name].wait()
    for p in range(3):
        wc[p * cc : (p + 1) * cc] = wc_ref[:, p * 9 * cc : (p + 1) * 9 * cc]
    bc, bu = column(bc_ref[...]), column(bu_ref[...])
    for b in range(count):
        for t in range(count):
            m = mask_row(own, 0, t, b)[:, 256:384]
            cm[b, 0, t] = jnp.broadcast_to(m, (cc, 128)).astype(BF16)
            m = jnp.where(low, mask_row(own, 1, t, b)[:, 256:384], mask_row(own, -1, t, b)[:, 256:384])
            cm[b, 1, t] = jnp.broadcast_to(m, (cc, 128)).astype(BF16)

    receive(mask_copies)
    far = [rm[d].astype(F32) for d in (0, 1)]
    cross = (-1, 1)
    for b in range(count):
        for t in range(count):
            for d in (0, 1):
                for i, s in enumerate((0, cross[d])):
                    m = mask_row(far[d], s, t, b)
                    fe_m[d, i, b, t] = jnp.broadcast_to(m[:, 0:256], (ch, 256)).astype(BF16)
            from_r, from_l = mask_row(far[0], 0, t, b), mask_row(far[1], 0, t, b)
            mixed = (
                (from_l, mask_row(far[0], -1, t, b)),
                (from_r, from_l),
                (mask_row(far[1], 1, t, b), from_r),
            )
            for i, (lower, upper) in enumerate(mixed):
                m = jnp.where(low, lower[:, 256:384], upper[:, 256:384])
                ce_m[i, b, t] = jnp.broadcast_to(m, (cc, 128)).astype(BF16)
    far_live = [[far[d][first_live + b : first_live + b + 1, :] for b in range(count)] for d in (0, 1)]
    far_valid = [[far[d][first_valid + b : first_valid + b + 1, :] for b in range(count)] for d in (0, 1)]

    receive(face_copies)
    for d in (0, 1):
        for k in range(DEPTH):
            for t in range(count):
                r0 = ((d * DEPTH + k) * count + t) * ch
                lhse[r0 : r0 + ch, 0:face] = rx[d, t, :, k * face : (k + 1) * face]
    sele[...] = dot(lhse[:, 0:face], t1[...]).astype(BF16)

    def far_parts(d, k):
        return split(sele, (d * DEPTH + k) * count * ch, ch)

    convolve(into(y1, 0, 0, 1), w1, far_parts(1, DEPTH - 1), lambda b: fm.at[b, 0], 0, 1)
    convolve(into(y1, side + 1, 2, 3), w1, far_parts(0, 0), lambda b: fm.at[b, 2], 2, 3)
    for b in range(count):
        first_plane(b, 0)
        first_plane(b, side - 1)
    near = ((split(sel, (side - 1) * count * ch, ch), 1), (split(sel, 0, ch), 1))
    stacks = (
        (near[0], (far_parts(0, 0), 0), (far_parts(0, 1), 0)),
        ((far_parts(1, 0), 0), (far_parts(1, 1), 0), near[1]),
    )
    for d in (0, 1):
        deep = jnp.concatenate(
            [
                jnp.concatenate([taps(blend(parts, fe_m.at[d, i, b]), 16) for b in range(count)], axis=1)
                for parts, i in stacks[d]
            ],
            axis=0,
        )
        u = dot(w1_ref[...], deep) + b1
        for b in range(count):
            v = silu(u[:, b * 256 : (b + 1) * 256])
            fe[d, b] = (far_live[d][b][:, 0:256] * v).astype(BF16)

    sources = [[fe[1, t] for t in range(count)], [fst[t, 0] for t in range(count)]]
    sources += [[fst[t, side - 1] for t in range(count)], [fe[0, t] for t in range(count)]]
    selo = dot(jnp.concatenate([v for s in sources for v in s], axis=0), t2[...]).astype(BF16)
    convolve(into(yf, 0, 0, 1), w2f, split(selo, 0, ch), lambda b: fm.at[b, 0], 0, 1)
    convolve(biased(1), w2f, split(selo, count * ch, ch), lambda b: fm.at[b, 1], 0, 3)
    convolve(biased(side), w2f, split(selo, 2 * count * ch, ch), lambda b: fm.at[b, 1], 0, 3)
    convolve(into(yf, side + 1, 2, 3), w2f, split(selo, 3 * count * ch, ch), lambda b: fm.at[b, 2], 2, 3)

    for b in range(count):
        for x in range(side):
            uf[b, x] = yf[b, x, 0:ch] + yf[b, x + 1, ch : 2 * ch] + yf[b, x + 2, 2 * ch :]

    ends_ = reduce_units(len(inner), [own_unit(t, 0, half - 1) for t in range(count)])

    def pick(a, b):
        return jnp.where(low, a.astype(F32), b.astype(F32)).astype(BF16)

    shared, middle = inner[0:count], inner[count:]
    middle = [middle[j * count : (j + 1) * count] for j in range(pairs - 2)]
    bottom = [pick(ends_[t], shared[t]) for t in range(count)]
    top = [pick(shared[t], ends_[t]) for t in range(count)]
    for b in range(count):
        padded = [blend(v, cm.at[b, 0]) for v in [bottom] + middle + [top]]
        yc[b] = dot(wc[...], jnp.concatenate([taps(v, 8) for v in padded], axis=1))

    receive(coarse_copies)
    receive(first_copies)

    def far_unit(t):
        r = (fe[0, t], rf[0, t])
        l = (rf[1, t], fe[1, t])
        keep = jnp.where(low, far_live[0][t][:, 256:384], far_live[1][t][:, 256:384])
        return (lambda p: r[p]), (lambda p: l[p]), keep

    rim = reduce_units(len(inner) + count, [far_unit(t) for t in range(count)])
    from_right, from_left = [[rc[d, t] for t in range(count)] for d in (0, 1)]

    y_rim = dot(wc[...], jnp.concatenate([taps(blend(rim, cm.at[b, 1]), 8) for b in range(count)], axis=1))
    coarse = []
    ups = []
    for b in range(count):
        y = jnp.concatenate([yc[b], y_rim[:, b * 128 : (b + 1) * 128]], axis=1)
        width = y.shape[1]
        u = pltpu.roll(y[0:cc], 64, 1) + y[cc : 2 * cc] + pltpu.roll(y[2 * cc :], width - 64, 1) + bc
        coarse.append((valid[b] * silu(u[:, 0 : 64 * half])).astype(BF16))

    def outgoing(r, k):
        total = jnp.zeros(coarse[0].shape, F32)
        for b in range(count):
            total = total + coarse[b].astype(F32) * jnp.where(dest[b] == r * SEND_CAP + k, valid[b], 0.0)
        return total.astype(BF16)

    sent = []
    for d in range(1, n_group):
        other = lax.rem(grp + d, n_group)
        for k in range(SEND_CAP):
            sb[d - 1, k] = outgoing(other, k)
        c = pltpu.make_async_remote_copy(
            src_ref=sb.at[d - 1],
            dst_ref=rb.at[d - 1],
            send_sem=bal_send.at[d - 1],
            recv_sem=bal_recv.at[d - 1],
            device_id={"group": other},
            device_id_type=MESH,
        )
        c.start()
        sent.append(c)
    for k in range(SEND_CAP):
        bal_ref[grp * SEND_CAP + k] = outgoing(grp, k)

    for b in range(count):
        v = (live[b] * (dot(wu_ref[...], coarse[b]) + bu)).astype(BF16)
        ups.append([v[:, j * 128 : (j + 1) * 128] for j in range(pairs)])

    below = [pick(from_left[t], ends_[t]) for t in range(count)]
    above = [pick(ends_[t], from_right[t]) for t in range(count)]
    zs = [[blend(v, ce_m.at[i, b]) for b in range(count)] for i, v in enumerate((below, rim, above))]
    zs[1] = [shifted(v, 64) for v in zs[1]]
    deep = jnp.concatenate([taps(jnp.concatenate(z, axis=1), 8) for z in zs], axis=0)
    u = dot(wc_ref[...], deep) + bc
    keep = jnp.concatenate(
        [jnp.where(low, far_valid[1][b][:, 256:384], far_valid[0][b][:, 256:384]) for b in range(count)], axis=1
    )
    co = (keep * silu(u)).astype(BF16)
    keep = jnp.concatenate(
        [jnp.where(low, far_live[1][b][:, 256:384], far_live[0][b][:, 256:384]) for b in range(count)], axis=1
    )
    v = (keep * (dot(wu_ref[...], co) + bu)).astype(BF16)
    for b in range(count):
        ups[b].append(v[:, b * 128 : (b + 1) * 128])

    wide = jnp.concatenate([ups[t][j] for j in range(pairs + 1) for t in range(count)], axis=0)
    selu = dot(wide, tup[...]).astype(BF16)
    for j in range(pairs + 1):
        for h in (0, 1):
            parts = [v[:, h * 256 : (h + 1) * 256] for v in split(selu, j * count * ch, ch)]
            if j < pairs:
                convolve(into(y2, 1 + 2 * j + h), w2u, parts, lambda b: fm.at[b, 1], 0, 3)
            elif h == 0:
                convolve(into(y2, 0, 0, 1), w2u, parts, lambda b: fm.at[b, 0], 0, 1)
            else:
                convolve(into(y2, half + 1, 2, 3), w2u, parts, lambda b: fm.at[b, 2], 2, 3)

    for b in range(count):
        for x in range(side):
            u = uf[b, x]
            for p in range(3):
                u = u + y2[b, (x + p + 1) // 2, p * ch : (p + 1) * ch]
            rows_ref[b, x * ch : (x + 1) * ch] = (live[b] * silu(u)).astype(BF16)

    for copies in (mask_copies, face_copies, coarse_copies, first_copies):
        for d in (0, 1):
            pl.when(sends[d])(copies[d].wait_send)
    for d, c in enumerate(sent):
        c.wait()
        source = lax.rem(grp + n_group - (d + 1), n_group)
        for k in range(SEND_CAP):
            bal_ref[source * SEND_CAP + k] = rb[d, k]


def finish_kernel(rows_ref, tout, tbal, bal_ref, out_hbm, bal_hbm, out, bal, sems):
    count, ch = out.shape[:2]
    face = tout.shape[1]
    side = out.shape[2] // face
    copies = []
    for b in range(count):
        flat = dot(rows_ref[b], tout[...])
        for x in range(side):
            out[b, :, x * face : (x + 1) * face] = flat[x * ch : (x + 1) * ch].astype(BF16)
        copies.append(pltpu.make_async_copy(out.at[b], out_hbm.at[b], sems.at[b]))
        copies[-1].start()
    slots, cc = bal_ref.shape[0], bal_ref.shape[1]
    dense = dot(jnp.concatenate([bal_ref[k] for k in range(slots)], axis=0), tbal[...])
    for k in range(slots):
        bal[k] = dense[k * cc : (k + 1) * cc].astype(BF16)
    copies.append(pltpu.make_async_copy(bal, bal_hbm, sems.at[count]))
    copies[-1].start()
    for c in copies:
        c.wait()


def tables(side):
    half = side // 2
    face = side * side

    def hot(rows, target):
        return (np.arange(rows)[:, None] == target[None, :]).astype(BF16)

    def wrap(v, n):
        return np.where(v == 0, n - 1, np.where(v == n + 1, 0, v - 1))

    n = np.arange(256)
    ny, nz = n >> 4, n & 15
    inside = (ny < side + 2) & (nz < side + 2)
    t1 = hot(face, np.where(inside, wrap(ny, side) * side + wrap(nz, side), -1))
    t2 = hot(256, np.where(inside, wrap(ny, side) * 16 + wrap(nz, side), -1))
    n2 = np.arange(512)
    ry, rz = (n2 >> 3) & 7, n2 & 7
    target = ((n2 >> 6) & 1) * 256 + (2 * wrap(ry, half) + ((n2 >> 8) & 1)) * 16 + 2 * wrap(rz, half) + ((n2 >> 7) & 1)
    tred = hot(512, np.where((ry < half + 2) & (rz < half + 2), target, -1))
    uy, uz = (n2 >> 4) & 15, n2 & 15
    target = (n2 >> 8) * 64 + (wrap(uy, side) >> 1) * 8 + (wrap(uz, side) >> 1)
    tup = hot(128, np.where((uy < side + 2) & (uz < side + 2), target, -1))
    tout = hot(face, np.where((ny < side) & (nz < side), ny * side + nz, -1)).T
    k = np.arange(64 * half)
    kx, ky, kz = k >> 6, (k >> 3) & 7, k & 7
    tbal = hot(half**3, np.where((ky < half) & (kz < half), (kx * half + ky) * half + kz, -1)).T
    return [jnp.asarray(t) for t in (t1, t2, tred, tup, tout, tbal)]


def local(n_local, n_group, features, neighbours, coarse_dest, *weights):
    count, ch, cells = features.shape
    side = round(cells ** (1 / 3))
    cc = weights[2].shape[0]
    half, face = side // 2, side * side
    pairs = half // 2
    rows = (3 * count * count + 2 * count + 15) // 16 * 16
    span = (DEPTH * face + 127) // 128 * 128
    if side + 2 > 16 or half + 2 > 8 or half % 2 or side**3 != cells or pairs < 2:
        raise ValueError("side")
    vmem = lambda *shape: pltpu.VMEM(shape, BF16)
    weights = [w.reshape(1, -1) if w.ndim == 1 else w for w in weights]
    onehots = tables(side)
    anywhere = pl.BlockSpec(memory_space=pl.ANY)
    whole = pl.BlockSpec(memory_space=pltpu.VMEM)
    units = (pairs - 1) * count
    middle = pl.pallas_call(
        functools.partial(kernel, (side, count, ch, cc, n_local, n_group)),
        out_shape=(
            vmem(count, side * ch, 256),
            vmem(256, face),
            vmem(64 * half, half**3),
            vmem(n_group * SEND_CAP, cc, 64 * half),
        ),
        in_specs=[anywhere] * (3 + len(weights) + len(onehots)),
        out_specs=(whole,) * 4,
        scratch_shapes=[
            pltpu.SMEM(neighbours.shape, I32),
            pltpu.SMEM(coarse_dest.shape, I32),
            pltpu.VMEM(neighbours.shape, I32),
            vmem(*features.shape),
        ]
        + [pltpu.VMEM(w.shape, w.dtype) for w in weights]
        + [
            vmem(2, count, ch, span),
            vmem(2, count, ch, span),
            vmem(rows, 384),
            vmem(2, rows, 384),
            vmem(2, count, ch, 256),
            vmem(2, count, ch, 256),
            vmem(count, cc, 128),
            vmem(2, count, cc, 128),
            vmem(n_group - 1, SEND_CAP, cc, 64 * half),
            vmem(n_group - 1, SEND_CAP, cc, 64 * half),
            vmem(face, 256),
            vmem(256, 256),
            vmem(512, 512),
            vmem(128, 512),
            vmem(3 * ch, 9 * ch),
            vmem(3 * cc, 9 * cc),
            vmem(3 * ch, 9 * ch),
            vmem(3 * ch, 9 * ch),
            vmem(side * count * ch, 512),
            vmem(2 * DEPTH * count * ch, 256),
            vmem((units + 2 * count) * 2 * ch, 512),
            pltpu.VMEM((count, side + 2, 3 * ch, 256), F32),
            pltpu.VMEM((count, side + 2, 3 * ch, 256), F32),
            pltpu.VMEM((count, half + 2, 3 * ch, 256), F32),
            pltpu.VMEM((count, side, ch, 256), F32),
            pltpu.VMEM((count, 3 * cc, pairs * 128), F32),
            vmem(count, side, ch, 256),
            vmem(2, count, ch, 256),
            vmem(side * count * ch, 256),
            vmem(2 * DEPTH * count * ch, 256),
            vmem(count, 3, count, ch, 256),
            vmem(2, 2, count, count, ch, 256),
            vmem(count, 2, count, cc, 128),
            vmem(3, count, count, cc, 128),
            pltpu.SemaphoreType.DMA((3 + len(weights) + 1 + len(onehots),)),
            pltpu.SemaphoreType.DMA((4, 2)),
            pltpu.SemaphoreType.DMA((4, 2)),
            pltpu.SemaphoreType.DMA((n_group - 1,)),
            pltpu.SemaphoreType.DMA((n_group - 1,)),
        ],
        compiler_params=pltpu.CompilerParams(
            collective_id=0, has_side_effects=True, vmem_limit_bytes=48 << 20
        ),
    )(*[pltpu.with_memory_space_constraint(a, pltpu.HBM) for a in (neighbours, coarse_dest, features, *weights, *onehots)])
    return pl.pallas_call(
        finish_kernel,
        out_shape=(
            jax.ShapeDtypeStruct(features.shape, BF16),
            jax.ShapeDtypeStruct((n_group * SEND_CAP, cc, half**3), BF16),
        ),
        in_specs=[whole] * 4,
        out_specs=(anywhere,) * 2,
        scratch_shapes=[
            vmem(*features.shape),
            vmem(n_group * SEND_CAP, cc, half**3),
            pltpu.SemaphoreType.DMA((count + 1,)),
        ],
        compiler_params=pltpu.CompilerParams(vmem_limit_bytes=24 << 20),
    )(*[pltpu.with_memory_space_constraint(a, pltpu.VMEM) for a in middle])


def solution(mesh):
    slots = P(("group", "local"), None, None)
    return jax.shard_map(
        functools.partial(local, mesh.shape["local"], mesh.shape["group"]),
        mesh=mesh,
        in_specs=(slots, P(("group", "local"), None), P(("group", "local"))) + (P(),) * 10,
        out_specs=(slots, slots),
        check_vma=False,
    )
```

```python
import functools

import jax
import jax.numpy as jnp
import numpy as np
from jax import lax
from jax.experimental import pallas as pl
from jax.experimental.pallas import tpu as pltpu
from jax.sharding import PartitionSpec as P

SEND_CAP = 2
DEPTH = 2
HELD = 4
MESH = pl.DeviceIdType.MESH
F32 = jnp.float32
BF16 = jnp.bfloat16
I32 = jnp.int32


def iota(shape, dim):
    return lax.broadcasted_iota(I32, shape, dim)


def onehot(mask):
    return jnp.where(mask, 1.0, 0.0).astype(BF16)


def column(row):
    n = row.shape[1]
    wide = jnp.broadcast_to(row, (n, n))
    return jnp.sum(jnp.where(iota((n, n), 0) == iota((n, n), 1), wide, 0.0), axis=1, keepdims=True)


def silu(u):
    return u / (1.0 + jnp.exp(-u))


def shifted(v, s):
    if s == 0:
        return v
    return jnp.concatenate([v[:, s:], v[:, :s]], axis=1)


def dot(a, b):
    return jnp.dot(a, b, preferred_element_type=F32)


def taps(v, stride):
    return jnp.concatenate([shifted(v, q * stride + r) for q in range(3) for r in range(3)], axis=0)


def offset(v, top):
    return jnp.where(v == 0, -1, jnp.where(v == top, 1, 0))


def kernel(
    sizes,
    nb_hbm,
    dest_hbm,
    x_hbm,
    w1_hbm,
    b1_hbm,
    wr_hbm,
    br_hbm,
    wc_hbm,
    bc_hbm,
    wu_hbm,
    bu_hbm,
    w2_hbm,
    b2_hbm,
    t1_hbm,
    t2_hbm,
    tred_hbm,
    tup_hbm,
    tout_hbm,
    tbal_hbm,
    out_ref,
    tbal,
    bal_ref,
    nb,
    dest,
    nb_ref,
    x_ref,
    w1_ref,
    b1_ref,
    wr_ref,
    br_ref,
    wc_ref,
    bc_ref,
    wu_ref,
    bu_ref,
    w2_ref,
    b2_ref,
    sx,
    rx,
    sm,
    rm,
    sf,
    rf,
    sc,
    rc,
    sb,
    rb,
    t1,
    t2,
    tred,
    tup,
    tout,
    rows_ref,
    w1,
    wc,
    w2f,
    w2u,
    lhs1,
    lhse,
    lhsr,
    y1,
    yf,
    y2,
    uf,
    yc,
    fst,
    fe,
    sel,
    sele,
    fm,
    fe_m,
    cm,
    ce_m,
    load_sem,
    send_sem,
    recv_sem,
    bal_send,
    bal_recv,
):
    side, count, ch, cc, n_local, n_group = sizes
    half = side // 2
    face = side * side
    planes = side + 2
    pairs = half // 2
    me = lax.axis_index("local")
    grp = lax.axis_index("group")
    right, left = lax.rem(me + 1, n_local), lax.rem(me + n_local - 1, n_local)
    ends = (left, right)
    has_left, has_right = me > 0, me < n_local - 1
    sends, receives = (has_left, has_right), (has_right, has_left)

    barrier = pltpu.get_barrier_semaphore()
    for d in (0, 1):

        @pl.when(sends[d])
        def _():
            pl.semaphore_signal(barrier, inc=1, device_id={"local": ends[d]}, device_id_type=MESH)

    for d in range(1, n_group):
        pl.semaphore_signal(
            barrier, inc=1, device_id={"group": lax.rem(grp + d, n_group)}, device_id_type=MESH
        )

    loads = {}
    pieces = (
        ("nbv", nb_hbm, nb_ref),
        ("x", x_hbm, x_ref),
        ("nb", nb_hbm, nb),
        ("dest", dest_hbm, dest),
        ("t1", t1_hbm, t1),
        ("w1", w1_hbm, w1_ref),
        ("b1", b1_hbm, b1_ref),
        ("tred", tred_hbm, tred),
        ("wr", wr_hbm, wr_ref),
        ("br", br_hbm, br_ref),
        ("t2", t2_hbm, t2),
        ("w2", w2_hbm, w2_ref),
        ("wc", wc_hbm, wc_ref),
        ("bc", bc_hbm, bc_ref),
        ("wu", wu_hbm, wu_ref),
        ("bu", bu_hbm, bu_ref),
        ("b2", b2_hbm, b2_ref),
        ("tup", tup_hbm, tup),
        ("tout", tout_hbm, tout),
        ("tbal", tbal_hbm, tbal),
    )
    for i, (name, src, dst) in enumerate(pieces):
        loads[name] = pltpu.make_async_copy(src, dst, load_sem.at[i])
    urgent = ("nbv", "x", "nb", "dest", "t1", "w1", "b1")
    for name in urgent:
        loads[name].start()

    for d in (0, 1):

        @pl.when(jnp.logical_not(receives[d]))
        def _():
            rx[d] = jnp.zeros(rx.shape[1:], BF16)
            rm[d] = jnp.zeros(rm.shape[1:], BF16)
            rf[d] = jnp.zeros(rf.shape[1:], BF16)
            rc[d] = jnp.zeros(rc.shape[1:], BF16)

    n = iota((1, 256), 1)
    ny, nz = n >> 4, n & 15
    n1 = iota((1, 128), 1)
    cy, cz = (n1 >> 3) & 7, n1 & 7
    low = n1 < 64
    fy, fz = offset(ny, side + 1), offset(nz, side + 1)
    gy, gz = offset(cy, half + 1), offset(cz, half + 1)

    direction = jnp.concatenate([(fy + 1) * 3 + fz + 1, (gy + 1) * 3 + gz + 1], axis=1)
    table = onehot(lax.rem(iota((27, 384), 0), 9) == direction)
    rows = sm.shape[0]
    first_live = 3 * count * count
    first_valid = first_live + count
    loads["nbv"].wait()
    row = iota((rows, 27), 0)
    entries = jnp.zeros((rows, 27), I32)
    for b in range(count):
        entries = jnp.where(lax.rem(row, count) == b, nb_ref[b : b + 1, :], entries)
    slot = lax.rem(lax.div(row, count), count)
    step_of = lax.div(row, count * count)
    chosen = onehot((entries == slot) & (lax.div(iota((rows, 27), 1), 9) == step_of) & (row < first_live))
    table_rows = dot(chosen, table)
    loads["nb"].wait()
    loads["dest"].wait()
    live = [jnp.where(nb[b, 13] >= 0, 1.0, 0.0) for b in range(count)]
    valid = [jnp.where(dest[b] >= 0, live[b], 0.0) for b in range(count)]
    wide_row = iota((rows, 384), 0)
    for b in range(count):
        table_rows = jnp.where(wide_row == first_live + b, live[b], table_rows)
        table_rows = jnp.where(wide_row == first_valid + b, valid[b], table_rows)
    sm[...] = table_rows.astype(BF16)

    loads["x"].wait()
    span = DEPTH * face
    for t in range(count):
        sx[0, t, :, 0:span] = x_ref[t, :, 0:span]
        sx[1, t, :, 0:span] = x_ref[t, :, side * face - span : side * face]
        tail = sx.shape[3] - span
        for d in (0, 1):
            sx[d, t, :, span:] = jnp.zeros((ch, tail), BF16)

    def remote(e, d, src, dst):
        return pltpu.make_async_remote_copy(
            src_ref=src,
            dst_ref=dst,
            send_sem=send_sem.at[e, d],
            recv_sem=recv_sem.at[e, d],
            device_id={"local": ends[d]},
            device_id_type=MESH,
        )

    def receive(copies):
        for d in (0, 1):
            pl.when(receives[d])(copies[d].wait_recv)

    def blend(parts, masks):
        total = parts[0] * masks[0]
        for t in range(1, count):
            total = total + parts[t] * masks[t]
        return total

    def mask_row(values, step, t, b):
        r = ((step + 1) * count + t) * count + b
        return values[r : r + 1, :]

    def convolve(store, weight, parts, masks, lo, hi):
        both = [taps(blend(parts, masks(b)), 16) for b in range(count)]
        y = dot(weight[lo * ch : hi * ch], jnp.concatenate(both, axis=1))
        for b in range(count):
            store(b, y[:, b * 256 : (b + 1) * 256])

    def into(dst, plane, lo=0, hi=3):
        def store(b, v):
            dst[b, plane, lo * ch : hi * ch] = v

        return store

    def split(a, base, size, n_parts=count):
        return [a[base + t * size : base + (t + 1) * size] for t in range(n_parts)]

    beside = jnp.where(has_left, 1, 0) + jnp.where(has_right, 1, 0)
    mask_copies = [remote(0, d, sm, rm.at[d]) for d in (0, 1)]
    face_copies = [remote(1, d, sx.at[d], rx.at[d]) for d in (0, 1)]

    own = sm[...].astype(F32)
    for b in range(count):
        for t in range(count):
            for s in range(3):
                m = mask_row(own, s - 1, t, b)[:, 0:256]
                fm[b, s, t] = jnp.broadcast_to(m, (ch, 256)).astype(BF16)
    def greet(mine):
        @pl.when(mine)
        def _():
            pl.semaphore_wait(barrier, beside + n_group - 1)

        for copies in (mask_copies, face_copies):
            for d in (0, 1):
                pl.when(mine & sends[d])(copies[d].start)

    greet(has_left)
    for name in loads:
        if name not in urgent:
            loads[name].start()
    for t in range(count):
        for x in range(side):
            lhs1[(x * count + t) * ch : (x * count + t + 1) * ch, 0:face] = x_ref[
                t, :, x * face : (x + 1) * face
            ]
    loads["w1"].wait()
    for p in range(3):
        w1[p * ch : (p + 1) * ch] = w1_ref[:, p * 9 * ch : (p + 1) * 9 * ch]
    loads["t1"].wait()
    sel[...] = dot(lhs1[:, 0:face], t1[...]).astype(BF16)
    first_planes = [x for x in range(side) if x < 5 or x > side - 6]
    for x in first_planes:
        if x == 3:
            greet(jnp.logical_not(has_left))
        convolve(into(y1, x + 1), w1, split(sel, x * count * ch, ch), lambda b: fm.at[b, 1], 0, 3)
    loads["b1"].wait()
    b1 = column(b1_ref[...])

    def first_plane(b, x):
        u = y1[b, x, 0:ch] + y1[b, x + 1, ch : 2 * ch] + y1[b, x + 2, 2 * ch : 3 * ch] + b1
        fst[b, x] = (live[b] * silu(u)).astype(BF16)

    for b in range(count):
        for x in (1, 2, 3, side - 4, side - 3, side - 2):
            first_plane(b, x)

    loads["tred"].wait()
    loads["wr"].wait()
    loads["br"].wait()
    br = column(br_ref[...])

    def reduce_units(base, units):
        for i, (low_of, high_of, _) in enumerate(units):
            for p in (0, 1):
                r0 = ((base + i) * 2 + p) * ch
                lhsr[r0 : r0 + ch, 0:256] = low_of(p)
                lhsr[r0 : r0 + ch, 256:512] = high_of(p)
        start, size = base * 2 * ch, len(units) * 2 * ch
        a = dot(lhsr[start : start + size], tred[...]).astype(BF16)
        stacked = [
            jnp.concatenate(
                [
                    a[(i * 2 + p) * ch : (i * 2 + p + 1) * ch, k * 128 : (k + 1) * 128]
                    for p in (0, 1)
                    for k in range(4)
                ],
                axis=0,
            )
            for i in range(len(units))
        ]
        v = dot(wr_ref[...], jnp.concatenate(stacked, axis=1)) + br
        return [(keep * silu(v[:, i * 128 : (i + 1) * 128])).astype(BF16) for i, (_, _, keep) in enumerate(units)]

    def own_unit(t, lower, upper):
        return (lambda p: fst[t, 2 * lower + p]), (lambda p: fst[t, 2 * upper + p]), live[t]

    inner = reduce_units(0, [own_unit(t, half - 2, 1) for t in range(count)])
    for t in range(count):
        sc[t] = inner[t]
        sf[0, t] = fst[t, 1]
        sf[1, t] = fst[t, side - 2]
    first_copies = [remote(2, d, sf.at[d], rf.at[d]) for d in (0, 1)]
    coarse_copies = [remote(3, d, sc, rc.at[d]) for d in (0, 1)]
    for copies in (coarse_copies, first_copies):
        for d in (0, 1):
            pl.when(sends[d])(copies[d].start)

    for x in range(side):
        if x not in first_planes:
            convolve(into(y1, x + 1), w1, split(sel, x * count * ch, ch), lambda b: fm.at[b, 1], 0, 3)
    for b in range(count):
        for x in range(4, side - 4):
            first_plane(b, x)
    middles = [own_unit(t, 2 * j, 2 * j + 1) for j in range(1, pairs - 1) for t in range(count)]
    inner += reduce_units(count, middles)

    loads["b2"].wait()
    b2 = column(b2_ref[...])

    def biased(plane):
        def store(b, v):
            yf[b, plane, 0:ch] = v[0:ch]
            yf[b, plane, ch : 2 * ch] = v[ch : 2 * ch] + b2
            yf[b, plane, 2 * ch :] = v[2 * ch :]

        return store

    loads["t2"].wait()
    loads["w2"].wait()
    for p in range(3):
        for part, dst in ((0, w2f), (1, w2u)):
            dst[p * ch : (p + 1) * ch] = jnp.concatenate(
                [
                    w2_ref[:, ((9 * p + k) * 2 + part) * ch : ((9 * p + k) * 2 + part + 1) * ch]
                    for k in range(9)
                ],
                axis=1,
            )
    for x in range(1, side - 1):
        for t in range(count):
            lhs1[(x * count + t) * ch : (x * count + t + 1) * ch, 256:512] = fst[t, x]
    lo, hi = count * ch, (side - 1) * count * ch
    self_ = dot(lhs1[lo:hi, 256:512], t2[...]).astype(BF16)
    for x in range(1, side - 1):
        convolve(biased(x + 1), w2f, split(self_, (x - 1) * count * ch, ch), lambda b: fm.at[b, 1], 0, 3)

    for name in ("wc", "bc", "wu", "bu", "tup", "tout", "tbal"):
        loads[name].wait()
    for p in range(3):
        wc[p * cc : (p + 1) * cc] = wc_ref[:, p * 9 * cc : (p + 1) * 9 * cc]
    bc, bu = column(bc_ref[...]), column(bu_ref[...])
    for b in range(count):
        for t in range(count):
            m = mask_row(own, 0, t, b)[:, 256:384]
            cm[b, 0, t] = jnp.broadcast_to(m, (cc, 128)).astype(BF16)
            m = jnp.where(low, mask_row(own, 1, t, b)[:, 256:384], mask_row(own, -1, t, b)[:, 256:384])
            cm[b, 1, t] = jnp.broadcast_to(m, (cc, 128)).astype(BF16)

    receive(mask_copies)
    far = [rm[d].astype(F32) for d in (0, 1)]
    cross = (-1, 1)
    for b in range(count):
        for t in range(count):
            for d in (0, 1):
                for i, s in enumerate((0, cross[d])):
                    m = mask_row(far[d], s, t, b)
                    fe_m[d, i, b, t] = jnp.broadcast_to(m[:, 0:256], (ch, 256)).astype(BF16)
            from_r, from_l = mask_row(far[0], 0, t, b), mask_row(far[1], 0, t, b)
            mixed = (
                (from_l, mask_row(far[0], -1, t, b)),
                (from_r, from_l),
                (mask_row(far[1], 1, t, b), from_r),
            )
            for i, (lower, upper) in enumerate(mixed):
                m = jnp.where(low, lower[:, 256:384], upper[:, 256:384])
                ce_m[i, b, t] = jnp.broadcast_to(m, (cc, 128)).astype(BF16)
    far_live = [[far[d][first_live + b : first_live + b + 1, :] for b in range(count)] for d in (0, 1)]
    far_valid = [[far[d][first_valid + b : first_valid + b + 1, :] for b in range(count)] for d in (0, 1)]

    receive(face_copies)
    for d in (0, 1):
        for k in range(DEPTH):
            for t in range(count):
                r0 = ((d * DEPTH + k) * count + t) * ch
                lhse[r0 : r0 + ch, 0:face] = rx[d, t, :, k * face : (k + 1) * face]
    sele[...] = dot(lhse[:, 0:face], t1[...]).astype(BF16)

    def far_parts(d, k):
        return split(sele, (d * DEPTH + k) * count * ch, ch)

    convolve(into(y1, 0, 0, 1), w1, far_parts(1, DEPTH - 1), lambda b: fm.at[b, 0], 0, 1)
    convolve(into(y1, side + 1, 2, 3), w1, far_parts(0, 0), lambda b: fm.at[b, 2], 2, 3)
    for b in range(count):
        first_plane(b, 0)
        first_plane(b, side - 1)
    near = ((split(sel, (side - 1) * count * ch, ch), 1), (split(sel, 0, ch), 1))
    stacks = (
        (near[0], (far_parts(0, 0), 0), (far_parts(0, 1), 0)),
        ((far_parts(1, 0), 0), (far_parts(1, 1), 0), near[1]),
    )
    for d in (0, 1):
        deep = jnp.concatenate(
            [
                jnp.concatenate([taps(blend(parts, fe_m.at[d, i, b]), 16) for b in range(count)], axis=1)
                for parts, i in stacks[d]
            ],
            axis=0,
        )
        u = dot(w1_ref[...], deep) + b1
        for b in range(count):
            v = silu(u[:, b * 256 : (b + 1) * 256])
            fe[d, b] = (far_live[d][b][:, 0:256] * v).astype(BF16)

    sources = [[fe[1, t] for t in range(count)], [fst[t, 0] for t in range(count)]]
    sources += [[fst[t, side - 1] for t in range(count)], [fe[0, t] for t in range(count)]]
    selo = dot(jnp.concatenate([v for s in sources for v in s], axis=0), t2[...]).astype(BF16)
    convolve(into(yf, 0, 0, 1), w2f, split(selo, 0, ch), lambda b: fm.at[b, 0], 0, 1)
    convolve(biased(1), w2f, split(selo, count * ch, ch), lambda b: fm.at[b, 1], 0, 3)
    convolve(biased(side), w2f, split(selo, 2 * count * ch, ch), lambda b: fm.at[b, 1], 0, 3)
    convolve(into(yf, side + 1, 2, 3), w2f, split(selo, 3 * count * ch, ch), lambda b: fm.at[b, 2], 2, 3)

    for b in range(count):
        for x in range(side):
            uf[b, x] = yf[b, x, 0:ch] + yf[b, x + 1, ch : 2 * ch] + yf[b, x + 2, 2 * ch :]

    ends_ = reduce_units(len(inner), [own_unit(t, 0, half - 1) for t in range(count)])

    def pick(a, b):
        return jnp.where(low, a.astype(F32), b.astype(F32)).astype(BF16)

    shared, middle = inner[0:count], inner[count:]
    middle = [middle[j * count : (j + 1) * count] for j in range(pairs - 2)]
    bottom = [pick(ends_[t], shared[t]) for t in range(count)]
    top = [pick(shared[t], ends_[t]) for t in range(count)]
    for b in range(count):
        padded = [blend(v, cm.at[b, 0]) for v in [bottom] + middle + [top]]
        yc[b] = dot(wc[...], jnp.concatenate([taps(v, 8) for v in padded], axis=1))

    receive(coarse_copies)
    receive(first_copies)

    def far_unit(t):
        r = (fe[0, t], rf[0, t])
        l = (rf[1, t], fe[1, t])
        keep = jnp.where(low, far_live[0][t][:, 256:384], far_live[1][t][:, 256:384])
        return (lambda p: r[p]), (lambda p: l[p]), keep

    rim = reduce_units(len(inner) + count, [far_unit(t) for t in range(count)])
    from_right, from_left = [[rc[d, t] for t in range(count)] for d in (0, 1)]

    y_rim = dot(wc[...], jnp.concatenate([taps(blend(rim, cm.at[b, 1]), 8) for b in range(count)], axis=1))
    coarse = []
    ups = []
    for b in range(count):
        y = jnp.concatenate([yc[b], y_rim[:, b * 128 : (b + 1) * 128]], axis=1)
        width = y.shape[1]
        u = pltpu.roll(y[0:cc], 64, 1) + y[cc : 2 * cc] + pltpu.roll(y[2 * cc :], width - 64, 1) + bc
        coarse.append((valid[b] * silu(u[:, 0 : 64 * half])).astype(BF16))

    def outgoing(r, k):
        total = jnp.zeros(coarse[0].shape, F32)
        for b in range(count):
            total = total + coarse[b].astype(F32) * jnp.where(dest[b] == r * SEND_CAP + k, valid[b], 0.0)
        return total.astype(BF16)

    sent = []
    for d in range(1, n_group):
        other = lax.rem(grp + d, n_group)
        for k in range(SEND_CAP):
            sb[d - 1, k] = outgoing(other, k)
        c = pltpu.make_async_remote_copy(
            src_ref=sb.at[d - 1],
            dst_ref=rb.at[d - 1],
            send_sem=bal_send.at[d - 1],
            recv_sem=bal_recv.at[d - 1],
            device_id={"group": other},
            device_id_type=MESH,
        )
        c.start()
        sent.append(c)
    for k in range(SEND_CAP):
        bal_ref[grp * SEND_CAP + k] = outgoing(grp, k)

    for b in range(count):
        v = (live[b] * (dot(wu_ref[...], coarse[b]) + bu)).astype(BF16)
        ups.append([v[:, j * 128 : (j + 1) * 128] for j in range(pairs)])

    below = [pick(from_left[t], ends_[t]) for t in range(count)]
    above = [pick(ends_[t], from_right[t]) for t in range(count)]
    zs = [[blend(v, ce_m.at[i, b]) for b in range(count)] for i, v in enumerate((below, rim, above))]
    zs[1] = [shifted(v, 64) for v in zs[1]]
    deep = jnp.concatenate([taps(jnp.concatenate(z, axis=1), 8) for z in zs], axis=0)
    u = dot(wc_ref[...], deep) + bc
    keep = jnp.concatenate(
        [jnp.where(low, far_valid[1][b][:, 256:384], far_valid[0][b][:, 256:384]) for b in range(count)], axis=1
    )
    co = (keep * silu(u)).astype(BF16)
    keep = jnp.concatenate(
        [jnp.where(low, far_live[1][b][:, 256:384], far_live[0][b][:, 256:384]) for b in range(count)], axis=1
    )
    v = (keep * (dot(wu_ref[...], co) + bu)).astype(BF16)
    for b in range(count):
        ups[b].append(v[:, b * 128 : (b + 1) * 128])

    wide = jnp.concatenate([ups[t][j] for j in range(pairs + 1) for t in range(count)], axis=0)
    selu = dot(wide, tup[...]).astype(BF16)
    for j in range(pairs + 1):
        for h in (0, 1):
            parts = [v[:, h * 256 : (h + 1) * 256] for v in split(selu, j * count * ch, ch)]
            if j < pairs:
                convolve(into(y2, 1 + 2 * j + h), w2u, parts, lambda b: fm.at[b, 1], 0, 3)
            elif h == 0:
                convolve(into(y2, 0, 0, 1), w2u, parts, lambda b: fm.at[b, 0], 0, 1)
            else:
                convolve(into(y2, half + 1, 2, 3), w2u, parts, lambda b: fm.at[b, 2], 2, 3)

    for b in range(count):
        for x in range(side):
            u = uf[b, x]
            for p in range(3):
                u = u + y2[b, (x + p + 1) // 2, p * ch : (p + 1) * ch]
            rows_ref[b, x * ch : (x + 1) * ch] = (live[b] * silu(u)).astype(BF16)
        flat = dot(rows_ref[b], tout[...])
        for x in range(side):
            out_ref[b, :, x * face : (x + 1) * face] = flat[x * ch : (x + 1) * ch].astype(BF16)

    for copies in (mask_copies, face_copies, coarse_copies, first_copies):
        for d in (0, 1):
            pl.when(sends[d])(copies[d].wait_send)
    for d, c in enumerate(sent):
        c.wait()
        source = lax.rem(grp + n_group - (d + 1), n_group)
        for k in range(SEND_CAP):
            bal_ref[source * SEND_CAP + k] = rb[d, k]


def finish_kernel(out_ref, tbal, bal_ref, out_hbm, bal_hbm, bal, sems):
    copies = [pltpu.make_async_copy(out_ref, out_hbm, sems.at[0]), pltpu.make_async_copy(bal, bal_hbm, sems.at[1])]
    copies[0].start()
    slots, cc = bal_ref.shape[0], bal_ref.shape[1]
    dense = dot(jnp.concatenate([bal_ref[k] for k in range(slots)], axis=0), tbal[...])
    for k in range(slots):
        bal[k] = dense[k * cc : (k + 1) * cc].astype(BF16)
    copies[1].start()
    for c in copies:
        c.wait()


def tables(side):
    half = side // 2
    face = side * side

    def hot(rows, target):
        return (np.arange(rows)[:, None] == target[None, :]).astype(BF16)

    def wrap(v, n):
        return np.where(v == 0, n - 1, np.where(v == n + 1, 0, v - 1))

    n = np.arange(256)
    ny, nz = n >> 4, n & 15
    inside = (ny < side + 2) & (nz < side + 2)
    t1 = hot(face, np.where(inside, wrap(ny, side) * side + wrap(nz, side), -1))
    t2 = hot(256, np.where(inside, wrap(ny, side) * 16 + wrap(nz, side), -1))
    n2 = np.arange(512)
    ry, rz = (n2 >> 3) & 7, n2 & 7
    target = ((n2 >> 6) & 1) * 256 + (2 * wrap(ry, half) + ((n2 >> 8) & 1)) * 16 + 2 * wrap(rz, half) + ((n2 >> 7) & 1)
    tred = hot(512, np.where((ry < half + 2) & (rz < half + 2), target, -1))
    uy, uz = (n2 >> 4) & 15, n2 & 15
    target = (n2 >> 8) * 64 + (wrap(uy, side) >> 1) * 8 + (wrap(uz, side) >> 1)
    tup = hot(128, np.where((uy < side + 2) & (uz < side + 2), target, -1))
    tout = hot(face, np.where((ny < side) & (nz < side), ny * side + nz, -1)).T
    k = np.arange(64 * half)
    kx, ky, kz = k >> 6, (k >> 3) & 7, k & 7
    tbal = hot(half**3, np.where((ky < half) & (kz < half), (kx * half + ky) * half + kz, -1)).T
    return [jnp.asarray(t) for t in (t1, t2, tred, tup, tout, tbal)]


def local(n_local, n_group, features, neighbours, coarse_dest, *weights):
    count, ch, cells = features.shape
    side = round(cells ** (1 / 3))
    cc = weights[2].shape[0]
    half, face = side // 2, side * side
    pairs = half // 2
    rows = (3 * count * count + 2 * count + 15) // 16 * 16
    span = (DEPTH * face + 127) // 128 * 128
    if side + 2 > 16 or half + 2 > 8 or half % 2 or side**3 != cells or pairs < 2:
        raise ValueError("side")
    vmem = lambda *shape: pltpu.VMEM(shape, BF16)
    weights = [w.reshape(1, -1) if w.ndim == 1 else w for w in weights]
    onehots = tables(side)
    anywhere = pl.BlockSpec(memory_space=pl.ANY)
    whole = pl.BlockSpec(memory_space=pltpu.VMEM)
    units = (pairs - 1) * count
    middle = pl.pallas_call(
        functools.partial(kernel, (side, count, ch, cc, n_local, n_group)),
        out_shape=(
            vmem(*features.shape),
            vmem(64 * half, half**3),
            vmem(n_group * SEND_CAP, cc, 64 * half),
        ),
        in_specs=[anywhere] * (3 + len(weights) + len(onehots)),
        out_specs=(whole,) * 3,
        scratch_shapes=[
            pltpu.SMEM(neighbours.shape, I32),
            pltpu.SMEM(coarse_dest.shape, I32),
            pltpu.VMEM(neighbours.shape, I32),
            vmem(*features.shape),
        ]
        + [pltpu.VMEM(w.shape, w.dtype) for w in weights]
        + [
            vmem(2, count, ch, span),
            vmem(2, count, ch, span),
            vmem(rows, 384),
            vmem(2, rows, 384),
            vmem(2, count, ch, 256),
            vmem(2, count, ch, 256),
            vmem(count, cc, 128),
            vmem(2, count, cc, 128),
            vmem(n_group - 1, SEND_CAP, cc, 64 * half),
            vmem(n_group - 1, SEND_CAP, cc, 64 * half),
            vmem(face, 256),
            vmem(256, 256),
            vmem(512, 512),
            vmem(128, 512),
            vmem(256, face),
            vmem(count, side * ch, 256),
            vmem(3 * ch, 9 * ch),
            vmem(3 * cc, 9 * cc),
            vmem(3 * ch, 9 * ch),
            vmem(3 * ch, 9 * ch),
            vmem(side * count * ch, 512),
            vmem(2 * DEPTH * count * ch, 256),
            vmem((units + 2 * count) * 2 * ch, 512),
            pltpu.VMEM((count, side + 2, 3 * ch, 256), F32),
            pltpu.VMEM((count, side + 2, 3 * ch, 256), F32),
            pltpu.VMEM((count, half + 2, 3 * ch, 256), F32),
            pltpu.VMEM((count, side, ch, 256), F32),
            pltpu.VMEM((count, 3 * cc, pairs * 128), F32),
            vmem(count, side, ch, 256),
            vmem(2, count, ch, 256),
            vmem(side * count * ch, 256),
            vmem(2 * DEPTH * count * ch, 256),
            vmem(count, 3, count, ch, 256),
            vmem(2, 2, count, count, ch, 256),
            vmem(count, 2, count, cc, 128),
            vmem(3, count, count, cc, 128),
            pltpu.SemaphoreType.DMA((3 + len(weights) + 1 + len(onehots),)),
            pltpu.SemaphoreType.DMA((4, 2)),
            pltpu.SemaphoreType.DMA((4, 2)),
            pltpu.SemaphoreType.DMA((n_group - 1,)),
            pltpu.SemaphoreType.DMA((n_group - 1,)),
        ],
        compiler_params=pltpu.CompilerParams(
            collective_id=0, has_side_effects=True, vmem_limit_bytes=48 << 20
        ),
    )(*[pltpu.with_memory_space_constraint(a, pltpu.HBM) for a in (neighbours, coarse_dest, features, *weights, *onehots)])
    return pl.pallas_call(
        finish_kernel,
        out_shape=(
            jax.ShapeDtypeStruct(features.shape, BF16),
            jax.ShapeDtypeStruct((n_group * SEND_CAP, cc, half**3), BF16),
        ),
        in_specs=[whole] * 3,
        out_specs=(anywhere,) * 2,
        scratch_shapes=[
            vmem(n_group * SEND_CAP, cc, half**3),
            pltpu.SemaphoreType.DMA((2,)),
        ],
        compiler_params=pltpu.CompilerParams(vmem_limit_bytes=24 << 20),
    )(*[pltpu.with_memory_space_constraint(a, pltpu.VMEM) for a in middle])


def solution(mesh):
    slots = P(("group", "local"), None, None)
    return jax.shard_map(
        functools.partial(local, mesh.shape["local"], mesh.shape["group"]),
        mesh=mesh,
        in_specs=(slots, P(("group", "local"), None), P(("group", "local"))) + (P(),) * 10,
        out_specs=(slots, slots),
        check_vma=False,
    )
```

```python
import functools

import jax
import jax.numpy as jnp
import numpy as np
from jax import lax
from jax.experimental import pallas as pl
from jax.experimental.pallas import tpu as pltpu
from jax.sharding import PartitionSpec as P

SEND_CAP = 2
DEPTH = 2
HELD = 4
MESH = pl.DeviceIdType.MESH
F32 = jnp.float32
BF16 = jnp.bfloat16
I32 = jnp.int32


def iota(shape, dim):
    return lax.broadcasted_iota(I32, shape, dim)


def onehot(mask):
    return jnp.where(mask, 1.0, 0.0).astype(BF16)


def column(row):
    n = row.shape[1]
    wide = jnp.broadcast_to(row, (n, n))
    return jnp.sum(jnp.where(iota((n, n), 0) == iota((n, n), 1), wide, 0.0), axis=1, keepdims=True)


def silu(u):
    return u / (1.0 + jnp.exp(-u))


def shifted(v, s):
    if s == 0:
        return v
    return jnp.concatenate([v[:, s:], v[:, :s]], axis=1)


def dot(a, b):
    return jnp.dot(a, b, preferred_element_type=F32)


def taps(v, stride):
    return jnp.concatenate([shifted(v, q * stride + r) for q in range(3) for r in range(3)], axis=0)


def offset(v, top):
    return jnp.where(v == 0, -1, jnp.where(v == top, 1, 0))


def kernel(
    sizes,
    nb_hbm,
    dest_hbm,
    x_hbm,
    w1_hbm,
    b1_hbm,
    wr_hbm,
    br_hbm,
    wc_hbm,
    bc_hbm,
    wu_hbm,
    bu_hbm,
    w2_hbm,
    b2_hbm,
    t1_hbm,
    t2_hbm,
    tred_hbm,
    tup_hbm,
    tout_hbm,
    tbal_hbm,
    rows_ref,
    tout,
    tbal,
    bal_ref,
    nb,
    dest,
    nb_ref,
    x_ref,
    w1_ref,
    b1_ref,
    wr_ref,
    br_ref,
    wc_ref,
    bc_ref,
    wu_ref,
    bu_ref,
    w2_ref,
    b2_ref,
    sx,
    rx,
    sm,
    rm,
    sf,
    rf,
    sc,
    rc,
    sb,
    rb,
    t1,
    t2,
    tred,
    tup,
    w1,
    wc,
    w2f,
    w2u,
    lhs1,
    lhse,
    lhsr,
    y1,
    yf,
    y2,
    uf,
    yc,
    fst,
    fe,
    sel,
    sele,
    fm,
    fe_m,
    cm,
    ce_m,
    load_sem,
    send_sem,
    recv_sem,
    bal_send,
    bal_recv,
):
    side, count, ch, cc, n_local, n_group = sizes
    half = side // 2
    face = side * side
    planes = side + 2
    pairs = half // 2
    me = lax.axis_index("local")
    grp = lax.axis_index("group")
    right, left = lax.rem(me + 1, n_local), lax.rem(me + n_local - 1, n_local)
    ends = (left, right)
    has_left, has_right = me > 0, me < n_local - 1
    sends, receives = (has_left, has_right), (has_right, has_left)

    barrier = pltpu.get_barrier_semaphore()
    for d in (0, 1):

        @pl.when(sends[d])
        def _():
            pl.semaphore_signal(barrier, inc=1, device_id={"local": ends[d]}, device_id_type=MESH)

    for d in range(1, n_group):
        pl.semaphore_signal(
            barrier, inc=1, device_id={"group": lax.rem(grp + d, n_group)}, device_id_type=MESH
        )

    loads = {}
    pieces = (
        ("nbv", nb_hbm, nb_ref),
        ("x", x_hbm, x_ref),
        ("nb", nb_hbm, nb),
        ("dest", dest_hbm, dest),
        ("t1", t1_hbm, t1),
        ("w1", w1_hbm, w1_ref),
        ("b1", b1_hbm, b1_ref),
        ("tred", tred_hbm, tred),
        ("wr", wr_hbm, wr_ref),
        ("br", br_hbm, br_ref),
        ("t2", t2_hbm, t2),
        ("w2", w2_hbm, w2_ref),
        ("wc", wc_hbm, wc_ref),
        ("bc", bc_hbm, bc_ref),
        ("wu", wu_hbm, wu_ref),
        ("bu", bu_hbm, bu_ref),
        ("b2", b2_hbm, b2_ref),
        ("tup", tup_hbm, tup),
        ("tout", tout_hbm, tout),
        ("tbal", tbal_hbm, tbal),
    )
    for i, (name, src, dst) in enumerate(pieces):
        loads[name] = pltpu.make_async_copy(src, dst, load_sem.at[i])
        loads[name].start()

    for d in (0, 1):

        @pl.when(jnp.logical_not(receives[d]))
        def _():
            rx[d] = jnp.zeros(rx.shape[1:], BF16)
            rm[d] = jnp.zeros(rm.shape[1:], BF16)
            rf[d] = jnp.zeros(rf.shape[1:], BF16)
            rc[d] = jnp.zeros(rc.shape[1:], BF16)

    n = iota((1, 256), 1)
    ny, nz = n >> 4, n & 15
    n1 = iota((1, 128), 1)
    cy, cz = (n1 >> 3) & 7, n1 & 7
    low = n1 < 64
    fy, fz = offset(ny, side + 1), offset(nz, side + 1)
    gy, gz = offset(cy, half + 1), offset(cz, half + 1)

    direction = jnp.concatenate([(fy + 1) * 3 + fz + 1, (gy + 1) * 3 + gz + 1], axis=1)
    table = onehot(lax.rem(iota((27, 384), 0), 9) == direction)
    rows = sm.shape[0]
    first_live = 3 * count * count
    first_valid = first_live + count
    loads["nbv"].wait()
    row = iota((rows, 27), 0)
    entries = jnp.zeros((rows, 27), I32)
    for b in range(count):
        entries = jnp.where(lax.rem(row, count) == b, nb_ref[b : b + 1, :], entries)
    slot = lax.rem(lax.div(row, count), count)
    step_of = lax.div(row, count * count)
    chosen = onehot((entries == slot) & (lax.div(iota((rows, 27), 1), 9) == step_of) & (row < first_live))
    table_rows = dot(chosen, table)
    loads["nb"].wait()
    loads["dest"].wait()
    live = [jnp.where(nb[b, 13] >= 0, 1.0, 0.0) for b in range(count)]
    valid = [jnp.where(dest[b] >= 0, live[b], 0.0) for b in range(count)]
    wide_row = iota((rows, 384), 0)
    for b in range(count):
        table_rows = jnp.where(wide_row == first_live + b, live[b], table_rows)
        table_rows = jnp.where(wide_row == first_valid + b, valid[b], table_rows)
    sm[...] = table_rows.astype(BF16)

    loads["x"].wait()
    span = DEPTH * face
    for t in range(count):
        sx[0, t, :, 0:span] = x_ref[t, :, 0:span]
        sx[1, t, :, 0:span] = x_ref[t, :, side * face - span : side * face]
        tail = sx.shape[3] - span
        for d in (0, 1):
            sx[d, t, :, span:] = jnp.zeros((ch, tail), BF16)

    def remote(e, d, src, dst):
        return pltpu.make_async_remote_copy(
            src_ref=src,
            dst_ref=dst,
            send_sem=send_sem.at[e, d],
            recv_sem=recv_sem.at[e, d],
            device_id={"local": ends[d]},
            device_id_type=MESH,
        )

    def receive(copies):
        for d in (0, 1):
            pl.when(receives[d])(copies[d].wait_recv)

    def blend(parts, masks):
        total = parts[0] * masks[0]
        for t in range(1, count):
            total = total + parts[t] * masks[t]
        return total

    def mask_row(values, step, t, b):
        r = ((step + 1) * count + t) * count + b
        return values[r : r + 1, :]

    def convolve(store, weight, parts, masks, lo, hi):
        both = [taps(blend(parts, masks(b)), 16) for b in range(count)]
        y = dot(weight[lo * ch : hi * ch], jnp.concatenate(both, axis=1))
        for b in range(count):
            store(b, y[:, b * 256 : (b + 1) * 256])

    def into(dst, plane, lo=0, hi=3):
        def store(b, v):
            dst[b, plane, lo * ch : hi * ch] = v

        return store

    def split(a, base, size, n_parts=count):
        return [a[base + t * size : base + (t + 1) * size] for t in range(n_parts)]

    beside = jnp.where(has_left, 1, 0) + jnp.where(has_right, 1, 0)
    mask_copies = [remote(0, d, sm, rm.at[d]) for d in (0, 1)]
    face_copies = [remote(1, d, sx.at[d], rx.at[d]) for d in (0, 1)]

    own = sm[...].astype(F32)
    for b in range(count):
        for t in range(count):
            for s in range(3):
                m = mask_row(own, s - 1, t, b)[:, 0:256]
                fm[b, s, t] = jnp.broadcast_to(m, (ch, 256)).astype(BF16)
    def greet(mine):
        @pl.when(mine)
        def _():
            pl.semaphore_wait(barrier, beside + n_group - 1)

        for copies in (mask_copies, face_copies):
            for d in (0, 1):
                pl.when(mine & sends[d])(copies[d].start)

    greet(has_left)
    for t in range(count):
        for x in range(side):
            lhs1[(x * count + t) * ch : (x * count + t + 1) * ch, 0:face] = x_ref[
                t, :, x * face : (x + 1) * face
            ]
    loads["w1"].wait()
    for p in range(3):
        w1[p * ch : (p + 1) * ch] = w1_ref[:, p * 9 * ch : (p + 1) * 9 * ch]
    loads["t1"].wait()
    sel[...] = dot(lhs1[:, 0:face], t1[...]).astype(BF16)
    first_planes = [x for x in range(side) if x < 5 or x > side - 6]
    for x in first_planes:
        if x == 2:
            greet(jnp.logical_not(has_left))
        convolve(into(y1, x + 1), w1, split(sel, x * count * ch, ch), lambda b: fm.at[b, 1], 0, 3)
    loads["b1"].wait()
    b1 = column(b1_ref[...])

    def first_plane(b, x):
        u = y1[b, x, 0:ch] + y1[b, x + 1, ch : 2 * ch] + y1[b, x + 2, 2 * ch : 3 * ch] + b1
        fst[b, x] = (live[b] * silu(u)).astype(BF16)

    for b in range(count):
        for x in (1, 2, 3, side - 4, side - 3, side - 2):
            first_plane(b, x)

    loads["tred"].wait()
    loads["wr"].wait()
    loads["br"].wait()
    br = column(br_ref[...])

    def reduce_units(base, units):
        for i, (low_of, high_of, _) in enumerate(units):
            for p in (0, 1):
                r0 = ((base + i) * 2 + p) * ch
                lhsr[r0 : r0 + ch, 0:256] = low_of(p)
                lhsr[r0 : r0 + ch, 256:512] = high_of(p)
        start, size = base * 2 * ch, len(units) * 2 * ch
        a = dot(lhsr[start : start + size], tred[...]).astype(BF16)
        stacked = [
            jnp.concatenate(
                [
                    a[(i * 2 + p) * ch : (i * 2 + p + 1) * ch, k * 128 : (k + 1) * 128]
                    for p in (0, 1)
                    for k in range(4)
                ],
                axis=0,
            )
            for i in range(len(units))
        ]
        v = dot(wr_ref[...], jnp.concatenate(stacked, axis=1)) + br
        return [(keep * silu(v[:, i * 128 : (i + 1) * 128])).astype(BF16) for i, (_, _, keep) in enumerate(units)]

    def own_unit(t, lower, upper):
        return (lambda p: fst[t, 2 * lower + p]), (lambda p: fst[t, 2 * upper + p]), live[t]

    inner = reduce_units(0, [own_unit(t, half - 2, 1) for t in range(count)])
    for t in range(count):
        sc[t] = inner[t]
        sf[0, t] = fst[t, 1]
        sf[1, t] = fst[t, side - 2]
    first_copies = [remote(2, d, sf.at[d], rf.at[d]) for d in (0, 1)]
    coarse_copies = [remote(3, d, sc, rc.at[d]) for d in (0, 1)]
    for copies in (coarse_copies, first_copies):
        for d in (0, 1):
            pl.when(sends[d])(copies[d].start)

    for x in range(side):
        if x not in first_planes:
            convolve(into(y1, x + 1), w1, split(sel, x * count * ch, ch), lambda b: fm.at[b, 1], 0, 3)
    for b in range(count):
        for x in range(4, side - 4):
            first_plane(b, x)
    middles = [own_unit(t, 2 * j, 2 * j + 1) for j in range(1, pairs - 1) for t in range(count)]
    inner += reduce_units(count, middles)

    loads["b2"].wait()
    b2 = column(b2_ref[...])

    def biased(plane):
        def store(b, v):
            yf[b, plane, 0:ch] = v[0:ch]
            yf[b, plane, ch : 2 * ch] = v[ch : 2 * ch] + b2
            yf[b, plane, 2 * ch :] = v[2 * ch :]

        return store

    loads["t2"].wait()
    loads["w2"].wait()
    for p in range(3):
        for part, dst in ((0, w2f), (1, w2u)):
            dst[p * ch : (p + 1) * ch] = jnp.concatenate(
                [
                    w2_ref[:, ((9 * p + k) * 2 + part) * ch : ((9 * p + k) * 2 + part + 1) * ch]
                    for k in range(9)
                ],
                axis=1,
            )
    for x in range(1, side - 1):
        for t in range(count):
            lhs1[(x * count + t) * ch : (x * count + t + 1) * ch, 256:512] = fst[t, x]
    lo, hi = count * ch, (side - 1) * count * ch
    self_ = dot(lhs1[lo:hi, 256:512], t2[...]).astype(BF16)
    for x in range(1, side - 1):
        convolve(biased(x + 1), w2f, split(self_, (x - 1) * count * ch, ch), lambda b: fm.at[b, 1], 0, 3)

    for name in ("wc", "bc", "wu", "bu", "tup", "tout", "tbal"):
        loads[name].wait()
    for p in range(3):
        wc[p * cc : (p + 1) * cc] = wc_ref[:, p * 9 * cc : (p + 1) * 9 * cc]
    bc, bu = column(bc_ref[...]), column(bu_ref[...])
    for b in range(count):
        for t in range(count):
            m = mask_row(own, 0, t, b)[:, 256:384]
            cm[b, 0, t] = jnp.broadcast_to(m, (cc, 128)).astype(BF16)
            m = jnp.where(low, mask_row(own, 1, t, b)[:, 256:384], mask_row(own, -1, t, b)[:, 256:384])
            cm[b, 1, t] = jnp.broadcast_to(m, (cc, 128)).astype(BF16)

    receive(mask_copies)
    far = [rm[d].astype(F32) for d in (0, 1)]
    cross = (-1, 1)
    for b in range(count):
        for t in range(count):
            for d in (0, 1):
                for i, s in enumerate((0, cross[d])):
                    m = mask_row(far[d], s, t, b)
                    fe_m[d, i, b, t] = jnp.broadcast_to(m[:, 0:256], (ch, 256)).astype(BF16)
            from_r, from_l = mask_row(far[0], 0, t, b), mask_row(far[1], 0, t, b)
            mixed = (
                (from_l, mask_row(far[0], -1, t, b)),
                (from_r, from_l),
                (mask_row(far[1], 1, t, b), from_r),
            )
            for i, (lower, upper) in enumerate(mixed):
                m = jnp.where(low, lower[:, 256:384], upper[:, 256:384])
                ce_m[i, b, t] = jnp.broadcast_to(m, (cc, 128)).astype(BF16)
    far_live = [[far[d][first_live + b : first_live + b + 1, :] for b in range(count)] for d in (0, 1)]
    far_valid = [[far[d][first_valid + b : first_valid + b + 1, :] for b in range(count)] for d in (0, 1)]

    receive(face_copies)
    for d in (0, 1):
        for k in range(DEPTH):
            for t in range(count):
                r0 = ((d * DEPTH + k) * count + t) * ch
                lhse[r0 : r0 + ch, 0:face] = rx[d, t, :, k * face : (k + 1) * face]
    sele[...] = dot(lhse[:, 0:face], t1[...]).astype(BF16)

    def far_parts(d, k):
        return split(sele, (d * DEPTH + k) * count * ch, ch)

    convolve(into(y1, 0, 0, 1), w1, far_parts(1, DEPTH - 1), lambda b: fm.at[b, 0], 0, 1)
    convolve(into(y1, side + 1, 2, 3), w1, far_parts(0, 0), lambda b: fm.at[b, 2], 2, 3)
    for b in range(count):
        first_plane(b, 0)
        first_plane(b, side - 1)
    near = ((split(sel, (side - 1) * count * ch, ch), 1), (split(sel, 0, ch), 1))
    stacks = (
        (near[0], (far_parts(0, 0), 0), (far_parts(0, 1), 0)),
        ((far_parts(1, 0), 0), (far_parts(1, 1), 0), near[1]),
    )
    for d in (0, 1):
        deep = jnp.concatenate(
            [
                jnp.concatenate([taps(blend(parts, fe_m.at[d, i, b]), 16) for b in range(count)], axis=1)
                for parts, i in stacks[d]
            ],
            axis=0,
        )
        u = dot(w1_ref[...], deep) + b1
        for b in range(count):
            v = silu(u[:, b * 256 : (b + 1) * 256])
            fe[d, b] = (far_live[d][b][:, 0:256] * v).astype(BF16)

    sources = [[fe[1, t] for t in range(count)], [fst[t, 0] for t in range(count)]]
    sources += [[fst[t, side - 1] for t in range(count)], [fe[0, t] for t in range(count)]]
    selo = dot(jnp.concatenate([v for s in sources for v in s], axis=0), t2[...]).astype(BF16)
    convolve(into(yf, 0, 0, 1), w2f, split(selo, 0, ch), lambda b: fm.at[b, 0], 0, 1)
    convolve(biased(1), w2f, split(selo, count * ch, ch), lambda b: fm.at[b, 1], 0, 3)
    convolve(biased(side), w2f, split(selo, 2 * count * ch, ch), lambda b: fm.at[b, 1], 0, 3)
    convolve(into(yf, side + 1, 2, 3), w2f, split(selo, 3 * count * ch, ch), lambda b: fm.at[b, 2], 2, 3)

    for b in range(count):
        for x in range(side):
            uf[b, x] = yf[b, x, 0:ch] + yf[b, x + 1, ch : 2 * ch] + yf[b, x + 2, 2 * ch :]

    ends_ = reduce_units(len(inner), [own_unit(t, 0, half - 1) for t in range(count)])

    def pick(a, b):
        return jnp.where(low, a.astype(F32), b.astype(F32)).astype(BF16)

    shared, middle = inner[0:count], inner[count:]
    middle = [middle[j * count : (j + 1) * count] for j in range(pairs - 2)]
    bottom = [pick(ends_[t], shared[t]) for t in range(count)]
    top = [pick(shared[t], ends_[t]) for t in range(count)]
    for b in range(count):
        padded = [blend(v, cm.at[b, 0]) for v in [bottom] + middle + [top]]
        yc[b] = dot(wc[...], jnp.concatenate([taps(v, 8) for v in padded], axis=1))

    receive(coarse_copies)
    receive(first_copies)

    def far_unit(t):
        r = (fe[0, t], rf[0, t])
        l = (rf[1, t], fe[1, t])
        keep = jnp.where(low, far_live[0][t][:, 256:384], far_live[1][t][:, 256:384])
        return (lambda p: r[p]), (lambda p: l[p]), keep

    rim = reduce_units(len(inner) + count, [far_unit(t) for t in range(count)])
    from_right, from_left = [[rc[d, t] for t in range(count)] for d in (0, 1)]

    y_rim = dot(wc[...], jnp.concatenate([taps(blend(rim, cm.at[b, 1]), 8) for b in range(count)], axis=1))
    coarse = []
    ups = []
    for b in range(count):
        y = jnp.concatenate([yc[b], y_rim[:, b * 128 : (b + 1) * 128]], axis=1)
        width = y.shape[1]
        u = pltpu.roll(y[0:cc], 64, 1) + y[cc : 2 * cc] + pltpu.roll(y[2 * cc :], width - 64, 1) + bc
        coarse.append((valid[b] * silu(u[:, 0 : 64 * half])).astype(BF16))

    def outgoing(r, k):
        total = jnp.zeros(coarse[0].shape, F32)
        for b in range(count):
            total = total + coarse[b].astype(F32) * jnp.where(dest[b] == r * SEND_CAP + k, valid[b], 0.0)
        return total.astype(BF16)

    sent = []
    for d in range(1, n_group):
        other = lax.rem(grp + d, n_group)
        for k in range(SEND_CAP):
            sb[d - 1, k] = outgoing(other, k)
        c = pltpu.make_async_remote_copy(
            src_ref=sb.at[d - 1],
            dst_ref=rb.at[d - 1],
            send_sem=bal_send.at[d - 1],
            recv_sem=bal_recv.at[d - 1],
            device_id={"group": other},
            device_id_type=MESH,
        )
        c.start()
        sent.append(c)
    for k in range(SEND_CAP):
        bal_ref[grp * SEND_CAP + k] = outgoing(grp, k)

    for b in range(count):
        v = (live[b] * (dot(wu_ref[...], coarse[b]) + bu)).astype(BF16)
        ups.append([v[:, j * 128 : (j + 1) * 128] for j in range(pairs)])

    below = [pick(from_left[t], ends_[t]) for t in range(count)]
    above = [pick(ends_[t], from_right[t]) for t in range(count)]
    zs = [[blend(v, ce_m.at[i, b]) for b in range(count)] for i, v in enumerate((below, rim, above))]
    zs[1] = [shifted(v, 64) for v in zs[1]]
    deep = jnp.concatenate([taps(jnp.concatenate(z, axis=1), 8) for z in zs], axis=0)
    u = dot(wc_ref[...], deep) + bc
    keep = jnp.concatenate(
        [jnp.where(low, far_valid[1][b][:, 256:384], far_valid[0][b][:, 256:384]) for b in range(count)], axis=1
    )
    co = (keep * silu(u)).astype(BF16)
    keep = jnp.concatenate(
        [jnp.where(low, far_live[1][b][:, 256:384], far_live[0][b][:, 256:384]) for b in range(count)], axis=1
    )
    v = (keep * (dot(wu_ref[...], co) + bu)).astype(BF16)
    for b in range(count):
        ups[b].append(v[:, b * 128 : (b + 1) * 128])

    wide = jnp.concatenate([ups[t][j] for j in range(pairs + 1) for t in range(count)], axis=0)
    selu = dot(wide, tup[...]).astype(BF16)
    for j in range(pairs + 1):
        for h in (0, 1):
            parts = [v[:, h * 256 : (h + 1) * 256] for v in split(selu, j * count * ch, ch)]
            if j < pairs:
                convolve(into(y2, 1 + 2 * j + h), w2u, parts, lambda b: fm.at[b, 1], 0, 3)
            elif h == 0:
                convolve(into(y2, 0, 0, 1), w2u, parts, lambda b: fm.at[b, 0], 0, 1)
            else:
                convolve(into(y2, half + 1, 2, 3), w2u, parts, lambda b: fm.at[b, 2], 2, 3)

    for b in range(count):
        for x in range(side):
            u = uf[b, x]
            for p in range(3):
                u = u + y2[b, (x + p + 1) // 2, p * ch : (p + 1) * ch]
            rows_ref[b, x * ch : (x + 1) * ch] = (live[b] * silu(u)).astype(BF16)

    for copies in (mask_copies, face_copies, coarse_copies, first_copies):
        for d in (0, 1):
            pl.when(sends[d])(copies[d].wait_send)
    for d, c in enumerate(sent):
        c.wait()
        source = lax.rem(grp + n_group - (d + 1), n_group)
        for k in range(SEND_CAP):
            bal_ref[source * SEND_CAP + k] = rb[d, k]


def finish_kernel(rows_ref, tout, tbal, bal_ref, out_hbm, bal_hbm, out, bal, sems):
    count, ch = out.shape[:2]
    face = tout.shape[1]
    side = out.shape[2] // face
    copies = []
    for b in range(count):
        flat = dot(rows_ref[b], tout[...])
        for x in range(side):
            out[b, :, x * face : (x + 1) * face] = flat[x * ch : (x + 1) * ch].astype(BF16)
        copies.append(pltpu.make_async_copy(out.at[b], out_hbm.at[b], sems.at[b]))
        copies[-1].start()
    slots, cc = bal_ref.shape[0], bal_ref.shape[1]
    dense = dot(jnp.concatenate([bal_ref[k] for k in range(slots)], axis=0), tbal[...])
    for k in range(slots):
        bal[k] = dense[k * cc : (k + 1) * cc].astype(BF16)
    copies.append(pltpu.make_async_copy(bal, bal_hbm, sems.at[count]))
    copies[-1].start()
    for c in copies:
        c.wait()


def tables(side):
    half = side // 2
    face = side * side

    def hot(rows, target):
        return (np.arange(rows)[:, None] == target[None, :]).astype(BF16)

    def wrap(v, n):
        return np.where(v == 0, n - 1, np.where(v == n + 1, 0, v - 1))

    n = np.arange(256)
    ny, nz = n >> 4, n & 15
    inside = (ny < side + 2) & (nz < side + 2)
    t1 = hot(face, np.where(inside, wrap(ny, side) * side + wrap(nz, side), -1))
    t2 = hot(256, np.where(inside, wrap(ny, side) * 16 + wrap(nz, side), -1))
    n2 = np.arange(512)
    ry, rz = (n2 >> 3) & 7, n2 & 7
    target = ((n2 >> 6) & 1) * 256 + (2 * wrap(ry, half) + ((n2 >> 8) & 1)) * 16 + 2 * wrap(rz, half) + ((n2 >> 7) & 1)
    tred = hot(512, np.where((ry < half + 2) & (rz < half + 2), target, -1))
    uy, uz = (n2 >> 4) & 15, n2 & 15
    target = (n2 >> 8) * 64 + (wrap(uy, side) >> 1) * 8 + (wrap(uz, side) >> 1)
    tup = hot(128, np.where((uy < side + 2) & (uz < side + 2), target, -1))
    tout = hot(face, np.where((ny < side) & (nz < side), ny * side + nz, -1)).T
    k = np.arange(64 * half)
    kx, ky, kz = k >> 6, (k >> 3) & 7, k & 7
    tbal = hot(half**3, np.where((ky < half) & (kz < half), (kx * half + ky) * half + kz, -1)).T
    return [jnp.asarray(t) for t in (t1, t2, tred, tup, tout, tbal)]


def local(n_local, n_group, features, neighbours, coarse_dest, *weights):
    count, ch, cells = features.shape
    side = round(cells ** (1 / 3))
    cc = weights[2].shape[0]
    half, face = side // 2, side * side
    pairs = half // 2
    rows = (3 * count * count + 2 * count + 15) // 16 * 16
    span = (DEPTH * face + 127) // 128 * 128
    if side + 2 > 16 or half + 2 > 8 or half % 2 or side**3 != cells or pairs < 2:
        raise ValueError("side")
    vmem = lambda *shape: pltpu.VMEM(shape, BF16)
    weights = [w.reshape(1, -1) if w.ndim == 1 else w for w in weights]
    onehots = tables(side)
    anywhere = pl.BlockSpec(memory_space=pl.ANY)
    whole = pl.BlockSpec(memory_space=pltpu.VMEM)
    units = (pairs - 1) * count
    middle = pl.pallas_call(
        functools.partial(kernel, (side, count, ch, cc, n_local, n_group)),
        out_shape=(
            vmem(count, side * ch, 256),
            vmem(256, face),
            vmem(64 * half, half**3),
            vmem(n_group * SEND_CAP, cc, 64 * half),
        ),
        in_specs=[anywhere] * (3 + len(weights) + len(onehots)),
        out_specs=(whole,) * 4,
        scratch_shapes=[
            pltpu.SMEM(neighbours.shape, I32),
            pltpu.SMEM(coarse_dest.shape, I32),
            pltpu.VMEM(neighbours.shape, I32),
            vmem(*features.shape),
        ]
        + [pltpu.VMEM(w.shape, w.dtype) for w in weights]
        + [
            vmem(2, count, ch, span),
            vmem(2, count, ch, span),
            vmem(rows, 384),
            vmem(2, rows, 384),
            vmem(2, count, ch, 256),
            vmem(2, count, ch, 256),
            vmem(count, cc, 128),
            vmem(2, count, cc, 128),
            vmem(n_group - 1, SEND_CAP, cc, 64 * half),
            vmem(n_group - 1, SEND_CAP, cc, 64 * half),
            vmem(face, 256),
            vmem(256, 256),
            vmem(512, 512),
            vmem(128, 512),
            vmem(3 * ch, 9 * ch),
            vmem(3 * cc, 9 * cc),
            vmem(3 * ch, 9 * ch),
            vmem(3 * ch, 9 * ch),
            vmem(side * count * ch, 512),
            vmem(2 * DEPTH * count * ch, 256),
            vmem((units + 2 * count) * 2 * ch, 512),
            pltpu.VMEM((count, side + 2, 3 * ch, 256), F32),
            pltpu.VMEM((count, side + 2, 3 * ch, 256), F32),
            pltpu.VMEM((count, half + 2, 3 * ch, 256), F32),
            pltpu.VMEM((count, side, ch, 256), F32),
            pltpu.VMEM((count, 3 * cc, pairs * 128), F32),
            vmem(count, side, ch, 256),
            vmem(2, count, ch, 256),
            vmem(side * count * ch, 256),
            vmem(2 * DEPTH * count * ch, 256),
            vmem(count, 3, count, ch, 256),
            vmem(2, 2, count, count, ch, 256),
            vmem(count, 2, count, cc, 128),
            vmem(3, count, count, cc, 128),
            pltpu.SemaphoreType.DMA((3 + len(weights) + 1 + len(onehots),)),
            pltpu.SemaphoreType.DMA((4, 2)),
            pltpu.SemaphoreType.DMA((4, 2)),
            pltpu.SemaphoreType.DMA((n_group - 1,)),
            pltpu.SemaphoreType.DMA((n_group - 1,)),
        ],
        compiler_params=pltpu.CompilerParams(
            collective_id=0, has_side_effects=True, vmem_limit_bytes=48 << 20
        ),
    )(*[pltpu.with_memory_space_constraint(a, pltpu.HBM) for a in (neighbours, coarse_dest, features, *weights, *onehots)])
    return pl.pallas_call(
        finish_kernel,
        out_shape=(
            jax.ShapeDtypeStruct(features.shape, BF16),
            jax.ShapeDtypeStruct((n_group * SEND_CAP, cc, half**3), BF16),
        ),
        in_specs=[whole] * 4,
        out_specs=(anywhere,) * 2,
        scratch_shapes=[
            vmem(*features.shape),
            vmem(n_group * SEND_CAP, cc, half**3),
            pltpu.SemaphoreType.DMA((count + 1,)),
        ],
        compiler_params=pltpu.CompilerParams(vmem_limit_bytes=24 << 20),
    )(*[pltpu.with_memory_space_constraint(a, pltpu.VMEM) for a in middle])


def solution(mesh):
    slots = P(("group", "local"), None, None)
    return jax.shard_map(
        functools.partial(local, mesh.shape["local"], mesh.shape["group"]),
        mesh=mesh,
        in_specs=(slots, P(("group", "local"), None), P(("group", "local"))) + (P(),) * 10,
        out_specs=(slots, slots),
        check_vma=False,
    )
```
